32 devices in a mesh: dp: 4 (over z), seq: 8 (over y, x, core).
Axes of the slice: x: 2, y: 2, z: 4, core: 2. Of those that a mesh axis runs over, the one named last changes fastest.
Arguments:
- inputs: bfloat16 [2, 4, 512, 2048], P(None, 'dp', 'seq'), may hold values from -6 to 6
- norm_attn: bfloat16 [2048], P(('dp', 'seq')), may hold values from 0.5 to 1.5
- w_query: bfloat16 [2048, 2048], P(('dp', 'seq')), may hold values from -0.125 to 0.125
- w_key: bfloat16 [2048, 2048], P(('dp', 'seq')), may hold values from -0.125 to 0.125
- w_value: bfloat16 [2048, 2048], P(('dp', 'seq')), may hold values from -0.125 to 0.125
- conv_weight: bfloat16 [4, 6144], P(None, ('dp', 'seq')), may hold values from -3 to 3
- w_alpha: bfloat16 [2048, 16], P(('dp', 'seq')), may hold values from -0.125 to 0.125
- w_beta: bfloat16 [2048, 16], P(('dp', 'seq')), may hold values from -0.125 to 0.125
- decay_rate: float32 [16], replicated, may hold values from 0.00048828125 to 0.05
- decay_bias: float32 [16], replicated, may hold values from -3 to 3
- w_outgate: bfloat16 [2048, 2048], P(('dp', 'seq')), may hold values from -0.125 to 0.125
- head_gain: float32 [128], replicated, may hold values from 0.5 to 1.5
- w_output: bfloat16 [2048, 2048], P(('dp', 'seq')), may hold values from -0.25 to 0.25
- norm_mlp: bfloat16 [2048], P(('dp', 'seq')), may hold values from 0.5 to 1.5
- w_gate: bfloat16 [2048, 5632], P(('dp', 'seq')), may hold values from -0.125 to 0.125
- w_up: bfloat16 [2048, 5632], P(('dp', 'seq')), may hold values from -0.125 to 0.125
- w_down: bfloat16 [5632, 2048], P(('dp', 'seq')), may hold values from -0.15625 to 0.15625
- cotangent: bfloat16 [2, 4, 512, 2048], P(None, 'dp', 'seq'), may hold values from -6 to 6
Outputs:
- output: bfloat16 [2, 4, 512, 2048], P(None, 'dp', 'seq')
- input_grad: float32 [2, 4, 512, 2048], P(None, 'dp', 'seq')
- grad_norm_attn: float32 [2048], P(('dp', 'seq'))
- grad_w_query: float32 [2048, 2048], P(('dp', 'seq'))
- grad_w_key: float32 [2048, 2048], P(('dp', 'seq'))
- grad_w_value: float32 [2048, 2048], P(('dp', 'seq'))
- grad_conv_weight: float32 [4, 6144], P(None, ('dp', 'seq'))
- grad_w_alpha: float32 [2048, 16], P(('dp', 'seq'))
- grad_w_beta: float32 [2048, 16], P(('dp', 'seq'))
- grad_decay_rate: float32 [16], replicated
- grad_decay_bias: float32 [16], replicated
- grad_w_outgate: float32 [2048, 2048], P(('dp', 'seq'))
- grad_head_gain: float32 [128], replicated
- grad_w_output: float32 [2048, 2048], P(('dp', 'seq'))
- grad_norm_mlp: float32 [2048], P(('dp', 'seq'))
- grad_w_gate: float32 [2048, 5632], P(('dp', 'seq'))
- grad_w_up: float32 [2048, 5632], P(('dp', 'seq'))
- grad_w_down: float32 [5632, 2048], P(('dp', 'seq'))
The draws below stay inside these ranges and needn't reach their ends.
All inputs are finite; a program needn't handle non-finite values.
Results may differ from the reference program's by a relative error of at most 0.03.
Values may be sent and summed in bfloat16 or wider, within the bound.
No kernel may reach another device: no remote copies, remote signals or barrier semaphores. Data moves between devices by JAX's collectives and lax.ppermute only.
A program may use at most 368 MiB of HBM per device.

```python
import math
import jax
import jax.numpy as jnp
from jax import lax

D = 2048
HEADS = 16
DK = 128
FF = 5632
BLOCK = 64
CONV = 4
MB = 2
LEN = 512
BATCH = 4


def shard_levels(own_key, shape, cuts, smallest, top_value):
    gain = 1.0
    for dim, blocks in cuts:
        steps = jax.random.uniform(jax.random.fold_in(jax.random.fold_in(own_key, 6), dim), (blocks,), jnp.float32, smallest / len(cuts), top_value / len(cuts))
        gain = gain * jnp.repeat(jnp.exp(steps), shape[dim] // blocks).reshape((-1,) + (1,) * (len(shape) - 1 - dim))
    return gain


def normal_values(own_key, shape, deviation, reach, cuts=(), kind=jnp.bfloat16):
    loudness = shard_levels(own_key, shape, cuts, -0.22, 0.18) if cuts else 1.0
    array = jax.random.normal(own_key, shape, jnp.float32) * deviation * loudness
    return jnp.minimum(jnp.maximum(array, -reach), reach).astype(kind)


def setup_inputs(seed: int = 0) -> dict:
    keys = jax.random.split(jax.random.key(seed), 19)
    return {
        "inputs": normal_values(keys[0], (MB, BATCH, LEN, D), 1.0, 6.0, ((1, 4), (2, 8))),
        "norm_attn": jnp.clip(1.0 + 0.1 * jax.random.normal(keys[1], (D,), jnp.float32), 0.5, 1.5).astype(jnp.bfloat16),
        "w_query": normal_values(keys[2], (D, D), D ** -0.5, 0.125, ((0, 32),)),
        "w_key": normal_values(keys[3], (D, D), D ** -0.5, 0.125, ((0, 32),)),
        "w_value": normal_values(keys[4], (D, D), D ** -0.5, 0.125, ((0, 32),)),
        "conv_weight": normal_values(keys[5], (CONV, 3 * D), CONV ** -0.5, 3.0, ((1, 32),)),
        "w_alpha": normal_values(keys[6], (D, HEADS), D ** -0.5, 0.125, ((0, 32),)),
        "w_beta": normal_values(keys[7], (D, HEADS), D ** -0.5, 0.125, ((0, 32),)),
        "decay_rate": jnp.clip(jnp.exp(jax.random.uniform(keys[8], (HEADS,), jnp.float32, math.log(0.00048828125), math.log(0.05))), 0.00048828125, 0.05),
        "decay_bias": normal_values(keys[9], (HEADS,), 0.5, 3.0, (), jnp.float32),
        "w_outgate": normal_values(keys[10], (D, D), D ** -0.5, 0.125, ((0, 32),)),
        "head_gain": jnp.clip(1.0 + 0.1 * jax.random.normal(keys[11], (DK,), jnp.float32), 0.5, 1.5),
        "w_output": normal_values(keys[12], (D, D), (D // 4) ** -0.5, 0.25, ((0, 32),)),
        "norm_mlp": jnp.clip(1.0 + 0.1 * jax.random.normal(keys[13], (D,), jnp.float32), 0.5, 1.5).astype(jnp.bfloat16),
        "w_gate": normal_values(keys[14], (D, FF), D ** -0.5, 0.125, ((0, 32),)),
        "w_up": normal_values(keys[15], (D, FF), D ** -0.5, 0.125, ((0, 32),)),
        "w_down": normal_values(keys[16], (FF, D), (FF // 4) ** -0.5, 0.15625, ((0, 32),)),
        "cotangent": normal_values(keys[17], (MB, BATCH, LEN, D), 1.0, 6.0, ((1, 4), (2, 8))),
    }


@jax.custom_vjp
def low(v):
    return lax.optimization_barrier(v.astype(jnp.bfloat16)).astype(jnp.float32)

@jax.custom_vjp
def low_back(v):
    return v

def low_keep(v):
    return (low(v), None)

def low_pass(kept, grad):
    return (grad,)

def back_keep(v):
    return (v, None)

def back_low(kept, grad):
    return (low(grad),)
low.defvjp(low_keep, low_pass)
low_back.defvjp(back_keep, back_low)
eps_norm = 1e-06
highest = lax.Precision.HIGHEST

def rms_scale(values, gain_vec):
    return values * lax.rsqrt(lax.optimization_barrier(jnp.mean(values * values, axis=-1, keepdims=True)) + eps_norm) * gain_vec

def unit_rows(values):
    return values * lax.rsqrt(lax.optimization_barrier(jnp.sum(values * values, axis=-1, keepdims=True)) + eps_norm)

def product(left_side, right_side):
    return jnp.dot(left_side, right_side, precision=highest)

def delta_rule(query_in, key_in, value_in, beta_in, decay_in):
    head_count, length, head_width = query_in.shape
    blocks = length // BLOCK
    query_blocks = query_in.reshape(head_count, blocks, BLOCK, head_width)
    key_blocks = key_in.reshape(head_count, blocks, BLOCK, head_width)
    value_blocks = value_in.reshape(head_count, blocks, BLOCK, head_width)
    beta_blocks = beta_in.reshape(head_count, blocks, BLOCK)
    cumulative = jnp.cumsum(decay_in.reshape(head_count, blocks, BLOCK), axis=-1)
    places = jnp.arange(BLOCK)
    strict = places[:, None] > places[None, :]
    within = places[:, None] >= places[None, :]
    spread = cumulative[..., :, None] - cumulative[..., None, :]
    fall_strict = jnp.where(strict, jnp.exp(jnp.where(strict, spread, 0.0)), 0.0)
    fall_within = jnp.where(within, jnp.exp(jnp.where(within, spread, 0.0)), 0.0)
    key_key = jnp.einsum('hnid,hnjd->hnij', key_blocks, key_blocks, precision=highest)
    query_key = jnp.einsum('hnid,hnjd->hnij', query_blocks, key_blocks, precision=highest)
    lower_part = -(beta_blocks[..., :, None] * fall_strict * key_key)
    inverse = jnp.eye(BLOCK, dtype=jnp.float32) + lower_part
    powered = lower_part
    for doubling in range(int(BLOCK).bit_length() - 2):
        powered = jnp.einsum('hnij,hnjk->hnik', powered, powered, precision=highest)
        inverse = inverse + jnp.einsum('hnij,hnjk->hnik', inverse, powered, precision=highest)
    growth = jnp.exp(cumulative)
    fresh_part = jnp.einsum('hnij,hnjd->hnid', inverse, beta_blocks[..., None] * value_blocks, precision=highest)
    carried = jnp.einsum('hnij,hnjd->hnid', inverse, (beta_blocks * growth)[..., None] * key_blocks, precision=highest)
    scores = query_key * fall_within
    query_grown = growth[..., None] * query_blocks
    key_fallen = jnp.exp(cumulative[..., -1:] - cumulative)[..., None] * key_blocks
    totals = jnp.exp(cumulative[..., -1])

    def advance(memory, block_data):
        fresh_now, carried_now, scores_now, query_now, key_now, total_now = block_data
        written = fresh_now - jnp.einsum('hid,hde->hie', carried_now, memory, precision=highest)
        results = jnp.einsum('hid,hde->hie', query_now, memory, precision=highest)
        results = results + jnp.einsum('hij,hje->hie', scores_now, written, precision=highest)
        memory = total_now[:, None, None] * memory + jnp.einsum('hid,hie->hde', key_now, written, precision=highest)
        return (memory, results)
    by_block = (jnp.moveaxis(fresh_part, 1, 0), jnp.moveaxis(carried, 1, 0), jnp.moveaxis(scores, 1, 0), jnp.moveaxis(query_grown, 1, 0), jnp.moveaxis(key_fallen, 1, 0), jnp.moveaxis(totals, 1, 0))
    initial = jnp.zeros((head_count, head_width, head_width), jnp.float32)
    final_memory, results = lax.scan(jax.checkpoint(advance), initial, by_block)
    return jnp.moveaxis(results, 0, 1).reshape(head_count, length, head_width)

def gated_inputs(padded, conv_full, alpha_pre, beta_pre, decay_rate, decay_bias):
    rows_out = padded.shape[0] - CONV + 1
    convolved = conv_full[0] * padded[0:rows_out]
    for conv_tap in range(1, CONV):
        convolved = convolved + conv_full[conv_tap] * padded[conv_tap:conv_tap + rows_out]
    active = jax.nn.silu(convolved)
    head_count = decay_rate.shape[0]
    model_width = active.shape[1] // 3
    head_width = model_width // head_count
    pieces = active.reshape(rows_out, 3, head_count, head_width)
    query_out = unit_rows(pieces[:, 0]) * head_width ** (-0.5)
    key_out = unit_rows(pieces[:, 1])
    value_out = pieces[:, 2]
    beta_out = jax.nn.sigmoid(beta_pre)
    decay_out = -decay_rate * jax.nn.softplus(alpha_pre + decay_bias)
    return (query_out.reshape(rows_out, model_width), key_out.reshape(rows_out, model_width), value_out.reshape(rows_out, model_width), beta_out, decay_out)

def head_rule(query_in, key_in, value_in, beta_in, decay_in):
    length, model_width = query_in.shape
    head_count = beta_in.shape[1]
    head_width = model_width // head_count
    query_heads = jnp.transpose(query_in.reshape(length, head_count, head_width), (1, 0, 2))
    key_heads = jnp.transpose(key_in.reshape(length, head_count, head_width), (1, 0, 2))
    value_heads = jnp.transpose(value_in.reshape(length, head_count, head_width), (1, 0, 2))
    outcome = delta_rule(query_heads, key_heads, value_heads, beta_in.T, decay_in.T)
    return jnp.transpose(outcome, (1, 0, 2)).reshape(length, model_width)

def gated_output(core_in, out_gate, head_gain):
    rows_out, model_width = core_in.shape
    head_width = head_gain.shape[0]
    pieces = core_in.reshape(rows_out, model_width // head_width, head_width)
    normed = pieces * lax.rsqrt(lax.optimization_barrier(jnp.mean(pieces * pieces, axis=-1, keepdims=True)) + eps_norm) * head_gain
    return normed.reshape(rows_out, model_width) * jax.nn.silu(out_gate)

def forward(tokens, norm_attn, w_query, w_key, w_value, conv_weight, w_alpha, w_beta, decay_rate, decay_bias, w_outgate, head_gain, w_output, norm_mlp, w_gate, w_up, w_down):
    hidden_in = low(rms_scale(tokens, norm_attn))
    projected = low_back(low(jnp.concatenate([product(hidden_in, w_query), product(hidden_in, w_key), product(hidden_in, w_value)], axis=1)))
    padded = jnp.concatenate([jnp.zeros((CONV - 1, projected.shape[1]), jnp.float32), projected], axis=0)
    alpha_pre = low_back(product(hidden_in, w_alpha))
    beta_pre = low_back(product(hidden_in, w_beta))
    query_out, key_out, value_out, beta_out, decay_out = gated_inputs(padded, conv_weight, alpha_pre, beta_pre, decay_rate, decay_bias)
    core_out = head_rule(low_back(low(query_out)), low_back(low(key_out)), low_back(low(value_out)), low_back(low(beta_out)), low_back(low(decay_out)))
    core_out = low_back(low(core_out))
    out_gate = low_back(product(hidden_in, w_outgate))
    mixed = low_back(low(gated_output(core_out, out_gate, head_gain)))
    residual = tokens + low_back(product(mixed, w_output))
    hidden_mid = low(rms_scale(residual, norm_mlp))
    gate_pre = low_back(product(hidden_mid, w_gate))
    up_proj = low_back(product(hidden_mid, w_up))
    activ = low(jax.nn.silu(gate_pre) * up_proj)
    return residual + product(activ, w_down)

def reference(inputs, norm_attn, w_query, w_key, w_value, conv_weight, w_alpha, w_beta, decay_rate, decay_bias, w_outgate, head_gain, w_output, norm_mlp, w_gate, w_up, w_down, cotangent):
    params = (norm_attn.astype(jnp.float32), w_query.astype(jnp.float32), w_key.astype(jnp.float32), w_value.astype(jnp.float32), conv_weight.astype(jnp.float32), w_alpha.astype(jnp.float32), w_beta.astype(jnp.float32), decay_rate.astype(jnp.float32), decay_bias.astype(jnp.float32), w_outgate.astype(jnp.float32), head_gain.astype(jnp.float32), w_output.astype(jnp.float32), norm_mlp.astype(jnp.float32), w_gate.astype(jnp.float32), w_up.astype(jnp.float32), w_down.astype(jnp.float32))
    sequences = inputs.astype(jnp.float32).reshape(MB * BATCH, LEN, D)
    seeds = cotangent.astype(jnp.float32).reshape(MB * BATCH, LEN, D)

    def one_sequence(running, seq_pair):
        tokens, seed_grad = seq_pair
        result, pull_back = jax.vjp(forward, tokens, *params)
        gradients = pull_back(seed_grad)
        summed = tuple((left_side + right_side for left_side, right_side in zip(running, gradients[1:])))
        return (summed, (result, gradients[0]))
    zeros_init = tuple((jnp.zeros_like(weight_arr) for weight_arr in params))
    totals, (results, input_grads) = lax.scan(one_sequence, zeros_init, (sequences, seeds))
    return (results.reshape(MB, BATCH, LEN, D).astype(jnp.bfloat16), input_grads.reshape(MB, BATCH, LEN, D), totals[0], totals[1], totals[2], totals[3], totals[4], totals[5], totals[6], totals[7], totals[8], totals[9], totals[10], totals[11], totals[12], totals[13], totals[14], totals[15])
```

```python
import functools

import jax
import jax.numpy as jnp
from jax import lax
from jax.experimental import pallas as pl
from jax.experimental.pallas import tpu as pltpu
from jax.sharding import PartitionSpec as P

BLOCK = 64
CONV = 4
MB = 2


eps_norm = 1e-06
highest = lax.Precision.HIGHEST


def rms_scale(values, gain_vec):
    return (
        values * lax.rsqrt(jnp.mean(values * values, axis=-1, keepdims=True) + eps_norm) * gain_vec
    )


def product(left_side, right_side):
    return jnp.dot(left_side, right_side, preferred_element_type=jnp.float32)


def contract_rows(left_side, right_side):
    return lax.dot_general(
        left_side, right_side, (((0,), (0,)), ((), ())), preferred_element_type=jnp.float32
    )


def times_transposed(left_side, right_side):
    return lax.dot_general(
        left_side, right_side, (((1,), (1,)), ((), ())), preferred_element_type=jnp.float32
    )


ALL = ("dp", "seq")


def swap(value, bit):
    count = lax.axis_size("seq")
    return lax.ppermute(value, "seq", [(place, place ^ bit) for place in range(count)])


def seq_offsets():
    count = lax.axis_size("seq")
    half = count // 2
    return [2 * place for place in range(half)] + [2 * place + 1 for place in range(half)]


def gather_seq(value):
    count = lax.axis_size("seq")
    held = {0: value}
    if count == 8:
        half = value.shape[0] // 2
        held[2] = swap(value, 2)
        held[4] = swap(value, 4)
        held[6] = jnp.concatenate(
            [swap(held[2][:half], 4), swap(held[4][half:], 2)], axis=0
        )
    else:
        bit = 2
        while bit < count:
            for offset in list(held):
                held[offset | bit] = swap(held[offset], bit)
            bit *= 2
    for offset in list(held):
        held[offset | 1] = swap(held[offset], 1)
    return jnp.stack([held[offset] for offset in seq_offsets()], axis=0)


def add_low(left_side, right_side):
    return (left_side.astype(jnp.float32) + right_side.astype(jnp.float32)).astype(jnp.bfloat16)


def scatter_seq(parts):
    f32 = jnp.float32
    count = lax.axis_size("seq")
    half = count // 2
    own = add_low(parts[:half], swap(parts[half:], 1))
    if count == 8:
        rows = own.shape[1] // 2
        first, second = own[:, :rows], own[:, rows:]
        first = add_low(first[:2], swap(first[2:], 4))
        second_y = second[0::2]
        second = add_low(second_y, swap(second[1::2], 2))
        first = first[0].astype(f32) + swap(first[1], 2).astype(f32)
        second = second[0].astype(f32) + swap(second[1], 4).astype(f32)
        return jnp.concatenate([first, second], axis=0)
    while half > 1:
        half //= 2
        own = add_low(own[:half], swap(own[half:], 2 * half))
    return own[0].astype(f32)


NN = ((1,), (0,))
NT = ((1,), (1,))
TN = ((0,), (0,))
PAIR = 2


def low_dot(left_side, right_side, dims):
    bf16 = jnp.bfloat16
    return lax.dot_general(
        left_side.astype(bf16),
        right_side.astype(bf16),
        (dims, ((), ())),
        preferred_element_type=jnp.float32,
    )


def rounded(value):
    return value.astype(jnp.bfloat16).astype(jnp.float32)


def softplus(value):
    return jnp.maximum(value, 0.0) + jnp.log1p(jnp.exp(-jnp.abs(value)))


def rows_sum(value):
    return jnp.sum(value, axis=1, keepdims=True)


def stack(pieces):
    return jnp.concatenate(pieces, axis=0)


def half(value, which):
    return value[which * BLOCK : (which + 1) * BLOCK]


def fill_masks(mask_ref, level_ref):
    size = PAIR * BLOCK
    down = lax.broadcasted_iota(jnp.int32, (size, size), 0)
    across = lax.broadcasted_iota(jnp.int32, (size, size), 1)
    apart = down ^ across
    mask_ref[0] = jnp.where((apart < BLOCK) & (down >= across), 1.0, 0.0)
    mask_ref[1] = jnp.where(apart == 0, 1.0, 0.0)
    for level in range(level_ref.shape[0]):
        inside = (apart >= 1 << level) & (apart < 2 << level) & (down > across)
        level_ref[level] = jnp.where(inside, 1.0, 0.0).astype(jnp.bfloat16)


def head_pieces(convolved, extras, gate_ref, mine, width):
    chains = []
    for conv_out, extra in zip(convolved, extras):
        active = conv_out * jax.nn.sigmoid(conv_out)
        beta = rounded(jax.nn.sigmoid(extra))
        decay = rounded(-gate_ref[0:1] * softplus(extra + gate_ref[1:2]))
        for head in range(mine):
            part = [
                active[:, (kind * mine + head) * width : (kind * mine + head + 1) * width]
                for kind in range(3)
            ]
            chains.append(
                part + [beta[:, mine + head : mine + head + 1], decay[:, head : head + 1]]
            )
    return chains


def block_values(chains, mask_ref, width):
    raw_query, raw_key, value, beta, decay = [stack(list(pieces)) for pieces in zip(*chains)]
    scale_query = lax.rsqrt(rows_sum(raw_query * raw_query) + eps_norm)
    scale_key = lax.rsqrt(rows_sum(raw_key * raw_key) + eps_norm)
    unit_query, unit_key = raw_query * scale_query, raw_key * scale_key
    query = rounded(unit_query * width ** (-0.5))
    key = rounded(unit_key)
    value = rounded(value)
    within = mask_ref[0]
    cumulative = low_dot(within, jnp.broadcast_to(decay, query.shape), NN)
    along = jnp.transpose(cumulative)[0:1, :]
    fall = within * jnp.exp(within * (cumulative[:, 0:1] - along))
    key_key = low_dot(key, key, NT)
    query_key = low_dot(query, key, NT)
    last = stack(
        [
            jnp.broadcast_to(half(cumulative, which)[BLOCK - 1 :], (BLOCK, width))
            for which in range(PAIR)
        ]
    )
    growth = jnp.exp(cumulative)
    key_fall = jnp.exp(last - cumulative)
    return dict(
        scale_query=scale_query,
        scale_key=scale_key,
        unit_query=unit_query,
        unit_key=unit_key,
        query=query,
        key=key,
        value=value,
        beta=beta,
        fall=fall,
        key_key=key_key,
        query_key=query_key,
        scores=query_key * fall,
        growth=growth,
        key_fall=key_fall,
        key_grown=growth * key,
        query_grown=growth * query,
        key_fallen=key_fall * key,
        totals=jnp.exp(last),
    )


def mixer_forward_body(
    me_ref,
    proj_ref,
    extra_ref,
    conv_ref,
    gate_ref,
    gain_ref,
    mixed_ref,
    conv_out_ref,
    core_ref,
    inverse_ref,
    made_ref,
    written_ref,
    memory_ref,
    rows_ref,
    state_ref,
    mask_ref,
    level_ref,
):
    bf16 = jnp.bfloat16
    sequences = proj_ref.shape[2]
    width = gain_ref.shape[1]
    cols = mixed_ref.shape[4]
    mine = cols // width
    pairs = sequences * mine // PAIR
    taps = conv_ref.shape[0]
    core_bit = jnp.bitwise_and(me_ref[0], 1)

    @pl.when(pl.program_id(0) == 0)
    def _():
        rows_ref[...] = jnp.zeros_like(rows_ref)
        state_ref[...] = jnp.zeros_like(state_ref)
        fill_masks(mask_ref, level_ref)

    blocks = []
    for block in range(2):
        spot = jnp.bitwise_xor(core_bit, block)
        convolved, extras = [], []
        for seq in range(sequences):
            rows_ref[seq, 8:] = rounded(proj_ref[spot, 0, seq, :, : 3 * cols])
            conv_out = conv_ref[0:1] * rows_ref[seq, 9 - taps : 9 - taps + BLOCK]
            for tap in range(1, taps):
                first = 9 - taps + tap
                conv_out = conv_out + conv_ref[tap : tap + 1] * rows_ref[seq, first : first + BLOCK]
            rows_ref[seq, 0:8] = rows_ref[seq, BLOCK : BLOCK + 8]
            conv_out_ref[0, block, seq] = conv_out
            convolved.append(conv_out)
            extras.append(extra_ref[spot, 0, seq])
        chains = head_pieces(convolved, extras, gate_ref, mine, width)
        for pair in range(pairs):
            made = block_values(chains[PAIR * pair : PAIR * (pair + 1)], mask_ref, width)
            lower = (made["beta"] * made["key_key"] * made["fall"]).astype(bf16)
            made["lower"] = lower
            made["inverse"] = mask_ref[1] - (level_ref[0] * lower).astype(jnp.float32)
            blocks.append((block, pair, made))
    for level in range(1, level_ref.shape[0]):
        inner = [
            low_dot(level_ref[level] * made["lower"], made["inverse"], NN) for _, _, made in blocks
        ]
        for (_, _, made), right_side in zip(blocks, inner):
            made["inverse"] = made["inverse"] - low_dot(made["inverse"], right_side, NN)
    for block, pair, made in blocks:
        inverse = made["inverse"].astype(bf16)
        inverse_ref[0, block, pair] = inverse
        weighted = jnp.concatenate(
            [made["beta"] * made["value"], made["beta"] * made["key_grown"]], axis=1
        )
        made["fresh_carried"] = low_dot(inverse, weighted, NN)
        made_ref[0, block, pair] = made["fresh_carried"].astype(bf16)
    for block, pair, made in blocks:
        fresh, carried = made["fresh_carried"][:, :width], made["fresh_carried"][:, width:]
        written, results = [], []
        for which in range(PAIR):
            chain = PAIR * pair + which
            state = state_ref[chain]
            low_state = state.astype(bf16)
            memory_ref[0, block, chain] = low_state
            seen = low_dot(
                stack([half(carried, which), half(made["query_grown"], which)]), low_state, NN
            )
            new = half(fresh, which) - seen[:BLOCK]
            written.append(new)
            results.append(seen[BLOCK:])
            state_ref[chain] = half(made["totals"], which)[0:1] * state + low_dot(
                half(made["key_fallen"], which), new, TN
            )
        written = stack(written).astype(bf16)
        written_ref[0, block, pair] = written
        core = (stack(results) + low_dot(made["scores"], written, NN)).astype(bf16)
        core_ref[0, block, pair] = core
        core = core.astype(jnp.float32)
        normed = core * lax.rsqrt(rows_sum(core * core) / width + eps_norm) * gain_ref[0:1]
        spot = jnp.bitwise_xor(core_bit, block)
        for which in range(PAIR):
            seq, head = divmod(PAIR * pair + which, mine)
            span = slice(head * width, (head + 1) * width)
            out_gate = proj_ref[
                spot, 0, seq, :, 3 * cols + head * width : 3 * cols + (head + 1) * width
            ]
            mixed = half(normed, which) * out_gate * jax.nn.sigmoid(out_gate)
            mixed_ref[spot, 0, seq, :, span] = mixed.astype(bf16)


def mixer_backward_body(
    me_ref,
    proj_ref,
    extra_ref,
    grad_mixed_ref,
    conv_out_ref,
    core_ref,
    inverse_ref,
    made_ref,
    written_ref,
    memory_ref,
    conv_ref,
    gate_ref,
    gain_ref,
    grad_proj_ref,
    grad_extra_ref,
    grad_conv_ref,
    grad_small_ref,
    rows_ref,
    state_ref,
    mask_ref,
    level_ref,
):
    f32 = jnp.float32
    bf16 = jnp.bfloat16
    sequences = proj_ref.shape[2]
    width = gain_ref.shape[1]
    cols = grad_mixed_ref.shape[4]
    mine = cols // width
    pairs = sequences * mine // PAIR
    taps = conv_ref.shape[0]
    core_bit = jnp.bitwise_and(me_ref[0], 1)

    @pl.when(pl.program_id(0) == 0)
    def _():
        rows_ref[...] = jnp.zeros_like(rows_ref)
        state_ref[...] = jnp.zeros_like(state_ref)
        grad_conv_ref[...] = jnp.zeros_like(grad_conv_ref)
        grad_small_ref[...] = jnp.zeros_like(grad_small_ref)
        fill_masks(mask_ref, level_ref)

    within = mask_ref[0]
    gain = gain_ref[0:1]
    grad_gain = jnp.zeros((1, width), f32)
    blocks = []
    for block in (1, 0):
        spot = jnp.bitwise_xor(core_bit, block)
        convolved = [conv_out_ref[0, block, seq] for seq in range(sequences)]
        extras = [extra_ref[spot, 0, seq] for seq in range(sequences)]
        chains = head_pieces(convolved, extras, gate_ref, mine, width)
        for pair in range(pairs):
            made = block_values(chains[PAIR * pair : PAIR * (pair + 1)], mask_ref, width)
            core = core_ref[0, block, pair].astype(f32)
            core_scale = lax.rsqrt(rows_sum(core * core) / width + eps_norm)
            normed = core * core_scale
            grad_unit = []
            for which in range(PAIR):
                seq, head = divmod(PAIR * pair + which, mine)
                span = slice(3 * cols + head * width, 3 * cols + (head + 1) * width)
                out_gate = proj_ref[spot, 0, seq, :, span]
                grad_mixed = grad_mixed_ref[
                    spot, 0, seq, :, head * width : (head + 1) * width
                ].astype(f32)
                sigmoid = jax.nn.sigmoid(out_gate)
                silu = out_gate * sigmoid
                scaled = grad_mixed * half(normed, which)
                grad_gate = scaled * gain * (sigmoid + silu * (1.0 - sigmoid))
                grad_proj_ref[spot, 0, seq, :, span] = grad_gate.astype(bf16)
                grad_gain = grad_gain + jnp.sum(scaled * silu, axis=0, keepdims=True)
                grad_unit.append(grad_mixed * gain * silu)
            grad_unit = stack(grad_unit)
            inner = rows_sum(grad_unit * normed) / width
            made["grad_core"] = (core_scale * (grad_unit - normed * inner)).astype(bf16)
            made["from_scores"] = low_dot(made["scores"], made["grad_core"], TN)
            made["grad_scores"] = (
                low_dot(made["grad_core"], written_ref[0, block, pair], NT) * made["fall"]
            )
            blocks.append((block, pair, made))
    grad_small_ref[0:1] += grad_gain

    for block, pair, made in blocks:
        carried = made_ref[0, block, pair, :, width:]
        parts = []
        for which in range(PAIR):
            chain = PAIR * pair + which
            state, grad_state = memory_ref[0, block, chain], state_ref[chain]
            low_grad_state = grad_state.astype(bf16)
            grad_out = half(made["grad_core"], which)
            grad_new = half(made["from_scores"], which) + low_dot(
                half(made["key_fallen"], which), low_grad_state, NN
            )
            low_new = grad_new.astype(bf16)
            totals = half(made["totals"], which)[0:1]
            state_ref[chain] = (
                totals * grad_state
                + low_dot(half(made["query_grown"], which), grad_out, TN)
                - low_dot(half(carried, which), low_new, TN)
            )
            back = low_dot(stack([grad_out, low_new]), state, NT)
            parts.append(
                (
                    low_new,
                    back[:BLOCK],
                    -back[BLOCK:],
                    low_dot(half(written_ref[0, block, pair], which), low_grad_state, NT),
                    rows_sum(
                        jnp.sum(state.astype(f32) * grad_state, axis=0, keepdims=True) * totals
                    ),
                )
            )
        made["grad_new"], made["grad_query_grown"], made["grad_carried"] = [
            stack([part[index] for part in parts]) for index in range(3)
        ]
        made["grad_key_fallen"] = stack([part[3] for part in parts])
        made["grad_totals"] = [part[4] for part in parts]

    lane = lax.broadcasted_iota(jnp.int32, (BLOCK, extra_ref.shape[4]), 1)
    at_end = lax.broadcasted_iota(jnp.int32, (BLOCK, 1), 0) == BLOCK - 1
    ones = jnp.ones((PAIR * BLOCK, width), bf16)
    results = {}
    for block, pair, made in blocks:
        beta, growth, fall = made["beta"], made["growth"], made["fall"]
        query, key, value = made["query"], made["key"], made["value"]
        fall_strict = fall - mask_ref[1]
        grad_weighted = low_dot(
            inverse_ref[0, block, pair],
            jnp.concatenate([made["grad_new"].astype(f32), made["grad_carried"]], axis=1),
            TN,
        )
        grad_lower = -low_dot(grad_weighted, made_ref[0, block, pair], NT) * fall_strict
        grad_key_key = grad_lower * beta
        from_lower = grad_lower * made["key_key"]
        grad_value_part, grad_key_part = grad_weighted[:, :width], grad_weighted[:, width:]
        grad_scores = made["grad_scores"]
        carried_part = grad_key_part * made["key_grown"]
        grad_beta = rows_sum(from_lower) + rows_sum(carried_part + grad_value_part * value)
        shifts = beta * from_lower + grad_scores * made["query_key"]
        fallen_part = made["grad_key_fallen"] * made["key_fallen"]
        fallen = rows_sum(fallen_part)
        grad_cumulative = rows_sum(shifts) + rows_sum(
            made["grad_query_grown"] * made["query_grown"] + beta * carried_part - fallen_part
        )
        ends = stack(
            [
                jnp.where(
                    at_end,
                    jnp.sum(half(fallen, which), axis=0, keepdims=True) + made["grad_totals"][which],
                    0.0,
                )
                for which in range(PAIR)
            ]
        )
        grad_cumulative = grad_cumulative + ends - low_dot(shifts, ones, TN)
        grad_decay = rounded(low_dot(within, grad_cumulative, TN))
        both = stack([grad_scores, grad_key_key]).astype(bf16)
        down = low_dot(both, key, NN)
        grad_query = growth * made["grad_query_grown"] + down[: PAIR * BLOCK]
        grad_key = (
            made["key_fall"] * made["grad_key_fallen"]
            + beta * growth * grad_key_part
            + down[PAIR * BLOCK :]
            + low_dot(both, stack([query, key]), TN)
        )
        grad_query = rounded(grad_query) * width ** (-0.5)
        grad_key = rounded(grad_key)
        grad_value = rounded(beta * grad_value_part)
        grad_beta = rounded(grad_beta)
        unit_query, unit_key = made["unit_query"], made["unit_key"]
        grad_query = made["scale_query"] * (
            grad_query - unit_query * rows_sum(grad_query * unit_query)
        )
        grad_key = made["scale_key"] * (grad_key - unit_key * rows_sum(grad_key * unit_key))
        for which in range(PAIR):
            results[block, PAIR * pair + which] = [
                half(part, which)
                for part in (grad_query, grad_key, grad_value, grad_decay, grad_beta)
            ]

    for block in (1, 0):
        spot = jnp.bitwise_xor(core_bit, block)
        for seq in range(sequences):
            conv_out = conv_out_ref[0, block, seq]
            sigmoid = jax.nn.sigmoid(conv_out)
            chains = [results[block, seq * mine + head] for head in range(mine)]
            grad_active = jnp.concatenate(
                [chain[kind] for kind in range(3) for chain in chains], axis=1
            )
            rows_ref[seq, :BLOCK] = grad_active * sigmoid * (1.0 + conv_out * (1.0 - sigmoid))
            pre = rounded(proj_ref[spot, 0, seq, :, : 3 * cols])
            grad_pre = jnp.zeros_like(conv_out)
            for tap in range(taps):
                shifted = rows_ref[seq, taps - 1 - tap : taps - 1 - tap + BLOCK]
                grad_pre = grad_pre + conv_ref[tap : tap + 1] * shifted
                grad_conv_ref[tap : tap + 1] += jnp.sum(pre * shifted, axis=0, keepdims=True)
            grad_proj_ref[spot, 0, seq, :, : 3 * cols] = grad_pre.astype(bf16)
            rows_ref[seq, BLOCK:] = rows_ref[seq, 0:8]
            extra = extra_ref[spot, 0, seq]
            moved = extra + gate_ref[1:2]
            spread_decay = jnp.zeros_like(extra)
            spread_beta = jnp.zeros_like(extra)
            for head, chain in enumerate(chains):
                spread_decay = jnp.where(lane == head, chain[3][:, 0:1], spread_decay)
                spread_beta = jnp.where(lane == mine + head, chain[4], spread_beta)
            grad_alpha = -gate_ref[0:1] * spread_decay * jax.nn.sigmoid(moved)
            squash = jax.nn.sigmoid(extra)
            grad_extra = grad_alpha + spread_beta * squash * (1.0 - squash)
            grad_extra_ref[spot, 0, seq] = grad_extra.astype(bf16)
            grad_small_ref[1:2] -= jnp.sum(spread_decay * softplus(moved), axis=0, keepdims=True)
            grad_small_ref[2:3] += jnp.sum(grad_alpha, axis=0, keepdims=True)


def ff_pack_body(width, gate_ref, up_ref, out_ref):
    count = out_ref.shape[0]
    blocks = gate_ref.shape[1] // (count * width)
    for spot in range(count):
        pieces = [
            ref[:, (block * count + spot) * width : (block * count + spot + 1) * width]
            for ref in (gate_ref, up_ref)
            for block in range(blocks)
        ]
        out_ref[spot] = jnp.concatenate(pieces, axis=1)


def ff_pack(gate, up, count, width):
    rows, hidden = gate.shape
    return pl.pallas_call(
        functools.partial(ff_pack_body, width),
        out_shape=jax.ShapeDtypeStruct((count, rows, 2 * hidden // count), gate.dtype),
    )(gate, up)


def ff_unpack_body(width, in_ref, gate_ref, up_ref):
    count = in_ref.shape[0]
    blocks = gate_ref.shape[1] // (count * width)
    for which, ref in enumerate((gate_ref, up_ref)):
        pieces = []
        for block in range(blocks):
            first = (which * blocks + block) * width
            pieces += [in_ref[spot, :, first : first + width] for spot in range(count)]
        ref[...] = jnp.concatenate([piece.astype(jnp.float32) for piece in pieces], axis=1)


def ff_unpack(packed, width):
    count, rows, columns = packed.shape
    shape = jax.ShapeDtypeStruct((rows, count * columns // 2), jnp.float32)
    return pl.pallas_call(functools.partial(ff_unpack_body, width), out_shape=[shape, shape])(packed)


def whole_spec(shape):
    return pl.BlockSpec(shape, lambda step, me: (0,) * len(shape))


def mixer_specs(projected, head_width, mine, forward):
    _, steps, sequences, span, _ = projected.shape
    chains = sequences * mine
    pairs = chains // PAIR
    cols = mine * head_width

    def step_of(step):
        return step if forward else steps - 1 - step

    def gathered(channels):
        return pl.BlockSpec(
            (2, 1, sequences, span, channels),
            lambda step, me: (
                0,
                jnp.bitwise_xor(jnp.right_shift(me[0], 1), step_of(step)),
                0,
                0,
                0,
            ),
        )

    def ordered(*shape):
        return pl.BlockSpec((1,) + shape, lambda step, me: (step_of(step),) + (0,) * len(shape))

    size = PAIR * span
    kept = [
        (jax.ShapeDtypeStruct((steps,) + shape, kind), ordered(*shape))
        for shape, kind in [
            ((2, sequences, span, 3 * cols), jnp.float32),
            ((2, pairs, size, head_width), jnp.bfloat16),
            ((2, pairs, size, size), jnp.bfloat16),
            ((2, pairs, size, 2 * head_width), jnp.bfloat16),
            ((2, pairs, size, head_width), jnp.bfloat16),
            ((2, chains, head_width, head_width), jnp.bfloat16),
        ]
    ]
    scratch = [
        pltpu.VMEM((sequences, span + 8, 3 * cols), jnp.float32),
        pltpu.VMEM((chains, head_width, head_width), jnp.float32),
        pltpu.VMEM((2, size, size), jnp.float32),
        pltpu.VMEM((int(BLOCK).bit_length() - 1, size, size), jnp.bfloat16),
    ]
    cost = pl.CostEstimate(
        flops=4 * steps * pairs * size**3 * 18,
        bytes_accessed=12 << 20,
        transcendentals=2 * steps << 18,
    )
    return gathered, kept, scratch, cost


def mixer_forward(me, projected, extra, conv_mine, gate_rows, gain_row, mine):
    channels = projected.shape[-1]
    head_width = gain_row.shape[1]
    gathered, kept, scratch, cost = mixer_specs(projected, head_width, mine, True)
    cols = mine * head_width
    return pl.pallas_call(
        mixer_forward_body,
        grid_spec=pltpu.PrefetchScalarGridSpec(
            num_scalar_prefetch=1,
            grid=(projected.shape[1],),
            in_specs=[
                gathered(channels),
                gathered(extra.shape[-1]),
                whole_spec(conv_mine.shape),
                whole_spec(gate_rows.shape),
                whole_spec(gain_row.shape),
            ],
            out_specs=[gathered(cols)] + [spec for _, spec in kept],
            scratch_shapes=scratch,
        ),
        out_shape=[jax.ShapeDtypeStruct(projected.shape[:-1] + (cols,), jnp.bfloat16)]
        + [shape for shape, _ in kept],
        compiler_params=pltpu.CompilerParams(vmem_limit_bytes=40 << 20),
        cost_estimate=cost,
    )(me, projected, extra, conv_mine, gate_rows, gain_row)


def mixer_backward(
    me, projected, extra, grad_mixed, kept_values, conv_mine, gate_rows, gain_row, mine
):
    channels = projected.shape[-1]
    head_width = gain_row.shape[1]
    gathered, kept, scratch, cost = mixer_specs(projected, head_width, mine, False)
    cols = mine * head_width
    return pl.pallas_call(
        mixer_backward_body,
        grid_spec=pltpu.PrefetchScalarGridSpec(
            num_scalar_prefetch=1,
            grid=(projected.shape[1],),
            in_specs=[gathered(channels), gathered(extra.shape[-1]), gathered(cols)]
            + [spec for _, spec in kept]
            + [
                whole_spec(conv_mine.shape),
                whole_spec(gate_rows.shape),
                whole_spec(gain_row.shape),
            ],
            out_specs=[
                gathered(channels),
                gathered(extra.shape[-1]),
                whole_spec(conv_mine.shape),
                whole_spec((8, head_width)),
            ],
            scratch_shapes=scratch,
        ),
        out_shape=[
            jax.ShapeDtypeStruct(projected.shape, jnp.bfloat16),
            jax.ShapeDtypeStruct(extra.shape, jnp.bfloat16),
            jax.ShapeDtypeStruct(conv_mine.shape, jnp.float32),
            jax.ShapeDtypeStruct((8, head_width), jnp.float32),
        ],
        compiler_params=pltpu.CompilerParams(vmem_limit_bytes=40 << 20),
        cost_estimate=cost,
    )(me, projected, extra, grad_mixed, *kept_values, conv_mine, gate_rows, gain_row)


def after(value, *others):
    return lax.optimization_barrier((value,) + others)[0]


def on_device(
    inputs,
    norm_attn,
    w_query,
    w_key,
    w_value,
    conv_weight,
    w_alpha,
    w_beta,
    decay_rate,
    decay_bias,
    w_outgate,
    head_gain,
    w_output,
    norm_mlp,
    w_gate,
    w_up,
    w_down,
    cotangent,
):
    f32 = jnp.float32
    bf16 = jnp.bfloat16
    n_dp = lax.axis_size("dp")
    n_seq = lax.axis_size("seq")
    devices = n_dp * n_seq
    me = lax.axis_index("seq")
    rows, width = w_query.shape
    heads = w_alpha.shape[1]
    head_width = head_gain.shape[0]
    mine = heads // n_seq
    cols = mine * head_width
    group = head_width // rows
    bands = n_seq // group
    band, place = me // group, me % group
    hidden = w_gate.shape[1]
    ff_rows = w_down.shape[0]
    ff = n_dp * ff_rows
    taps = conv_weight.shape[0]
    tokens_shape = inputs.shape
    span = inputs.shape[2]
    count = inputs.shape[0] * inputs.shape[1]
    total = n_seq * count * span

    def by_device(weight):
        split = weight.reshape(weight.shape[0], group, mine, bands, -1)
        return jnp.transpose(split, (3, 1, 0, 2, 4)).reshape(n_seq, weight.shape[0], -1)

    def by_columns(blocks):
        pieces = []
        for head in range(heads):
            spot, from_band = divmod(head, bands)
            from_place, which = divmod(spot, mine)
            block = blocks[from_band * group + from_place]
            pieces.append(block[:, which * head_width : (which + 1) * head_width])
        return jnp.concatenate(pieces, axis=1).astype(f32)

    def swap_all(blocks):
        return lax.all_to_all(blocks, ALL, split_axis=0, concat_axis=0, tiled=True)

    packed = jnp.concatenate([by_device(w) for w in (w_query, w_key, w_value, w_outgate)], axis=2)

    def exchange(blocks):
        return lax.all_to_all(blocks, "seq", split_axis=0, concat_axis=0, tiled=True)

    def gather_dp(block):
        return lax.all_gather(block, "dp", axis=0, tiled=True)

    sent = exchange(packed)
    mixer_full = gather_dp(sent.reshape(n_seq * rows, -1))
    shared = jnp.concatenate(
        [
            w_alpha.T.reshape(-1),
            w_beta.T.reshape(-1),
            norm_attn,
            norm_mlp,
            conv_weight.reshape(-1),
        ]
    )
    shared, w_gate, w_up, sent = lax.optimization_barrier((shared, w_gate, w_up, sent))
    shared = swap_all(jnp.broadcast_to(shared[None], (devices, shared.shape[0])))

    groups = [list(range(first, first + group)) for first in range(0, n_seq, group)]

    def exchange_group(blocks):
        if group == 2:
            away = swap(lax.dynamic_index_in_dim(blocks, 1 - place, 0, keepdims=False), 1)
            stay = lax.dynamic_index_in_dim(blocks, place, 0, keepdims=False)
            low = place == 0
            return jnp.stack([jnp.where(low, stay, away), jnp.where(low, away, stay)], axis=0)
        return lax.all_to_all(
            blocks, "seq", split_axis=0, concat_axis=0, tiled=True, axis_index_groups=groups
        )

    def to_heads(pieces):
        split = exchange_group(pieces.reshape(group, mine * rows, width))
        split = split.reshape(group, mine, rows, width)
        return jnp.transpose(split, (1, 0, 2, 3)).reshape(cols, width)

    def from_heads(full):
        split = jnp.transpose(full.reshape(mine, group, rows, width), (1, 0, 2, 3))
        return exchange_group(split.reshape(group, mine * rows, width))

    output_full = to_heads(gather_dp(w_output))

    gate_up_sent = exchange(ff_pack(w_gate, w_up, n_seq, ff_rows)).reshape(n_seq * rows, -1)
    gate_up_full = gather_dp(gate_up_sent)
    down_full = gather_dp(w_down).reshape(ff, width)
    mixer_full, shared, output_full = lax.optimization_barrier((mixer_full, shared, output_full))

    x_own = inputs.reshape(count * span, width)
    x_all = gather_seq(x_own).reshape(total, width)
    seed_own = cotangent.reshape(count * span, width)
    seed_all = gather_seq(seed_own).reshape(total, width)

    gates = shared[:, : 2 * heads * rows].reshape(devices, 2 * heads, rows)
    gates = jnp.transpose(gates, (1, 0, 2)).reshape(2, group, mine, bands, width)
    gates = lax.dynamic_index_in_dim(gates, band, 3, keepdims=False)
    gates = lax.dynamic_index_in_dim(gates, place, 1, keepdims=False).reshape(2 * mine, width)
    gates = jnp.pad(gates, ((0, 128 - 2 * mine), (0, 0)))
    first = 2 * heads * rows
    gain_attn = shared[:, first : first + rows].reshape(-1).astype(f32)
    gain_mlp = shared[:, first + rows : first + 2 * rows].reshape(-1).astype(f32)
    conv_all = shared[:, first + 2 * rows :].reshape(devices, taps, -1)
    conv_all = jnp.transpose(conv_all, (1, 0, 2)).reshape(taps, 3, group, mine, bands, head_width)
    conv_mine = lax.dynamic_index_in_dim(conv_all, band, 4, keepdims=False)
    conv_mine = lax.dynamic_index_in_dim(conv_mine, place, 2, keepdims=False)
    conv_mine = conv_mine.reshape(taps, 3 * cols).astype(f32)

    def my_heads(vector):
        split = lax.dynamic_index_in_dim(vector.reshape(group, mine, bands), band, 2, False)
        return lax.dynamic_index_in_dim(split, place, 0, keepdims=False)

    rate_mine = my_heads(decay_rate)
    bias_mine = my_heads(decay_bias)

    hidden_in = rms_scale(x_all.astype(f32), gain_attn).astype(bf16)
    projected = product(hidden_in, mixer_full)
    extra = times_transposed(hidden_in, gates).reshape(2, n_seq // 2, count, span, -1)

    projected = projected.reshape(2, n_seq // 2, count, span, -1)
    me_row = me.astype(jnp.int32).reshape(1)
    gate_rows = jnp.zeros((2, gates.shape[0]), f32)
    gate_rows = gate_rows.at[0, :mine].set(rate_mine).at[1, :mine].set(bias_mine)
    gain_row = head_gain.reshape(1, head_width)
    mixed, *kept_values = mixer_forward(
        me_row, projected, extra, conv_mine, gate_rows, gain_row, mine
    )
    mixed = mixed.reshape(total, cols)

    def shares(value):
        return value.astype(bf16).reshape(n_seq, count * span, -1)

    residual = x_own.astype(f32) + scatter_seq(shares(product(mixed, output_full)))
    normed_mid, pull_mid = jax.vjp(rms_scale, residual, gain_mlp)
    hidden_mid = gather_seq(normed_mid.astype(bf16)).reshape(total, width)
    gate_up = product(hidden_mid, gate_up_full)
    gate_pre, up_proj = gate_up[:, :ff], gate_up[:, ff:]
    sigmoid_gate = jax.nn.sigmoid(gate_pre)
    silu_gate = gate_pre * sigmoid_gate
    activ = (silu_gate * up_proj).astype(bf16)
    down_grads = contract_rows(activ, seed_all).astype(bf16)
    down_full, down_grads = lax.optimization_barrier((down_full, down_grads))
    from_down = times_transposed(seed_all, down_full)
    grad_gate = from_down * up_proj * sigmoid_gate * (1.0 + gate_pre * (1.0 - sigmoid_gate))
    grad_gate_up = jnp.concatenate([grad_gate, from_down * silu_gate], axis=1).astype(bf16)
    back_mid = scatter_seq(shares(times_transposed(grad_gate_up, gate_up_full)))
    grad_res_norm, grad_gain_mlp = pull_mid(back_mid)
    grad_res = seed_own.astype(f32) + grad_res_norm

    def scatter_dp(value):
        return lax.psum_scatter(value.astype(bf16), "dp", scatter_dimension=0, tiled=True)

    grad_down = scatter_dp(down_grads)
    grad_gate_up_own = scatter_dp(contract_rows(hidden_mid, grad_gate_up))

    grad_mixer_out = gather_seq(grad_res.astype(bf16)).reshape(total, width)
    grad_mixed = times_transposed(grad_mixer_out, output_full).astype(bf16)
    grad_projected, grad_extra, grad_conv, grad_small = mixer_backward(
        me_row,
        projected,
        extra,
        grad_mixed.reshape(2, n_seq // 2, count, span, cols),
        kept_values,
        conv_mine,
        gate_rows,
        gain_row,
        mine,
    )
    grad_projected = grad_projected.reshape(total, -1)
    grad_extra = grad_extra.reshape(total, -1)
    grad_head_gain = grad_small[0]
    grad_rate, grad_bias = grad_small[1, :mine], grad_small[2, :mine]
    grad_output = from_heads(contract_rows(mixed, grad_mixer_out).astype(bf16))
    weight_grads = contract_rows(hidden_in, grad_projected).astype(bf16)
    weight_grads = jnp.concatenate([weight_grads, grad_output.reshape(width, -1)], axis=1)
    weight_grads, grad_projected, grad_extra, activ = lax.optimization_barrier(
        (weight_grads, grad_projected, grad_extra, activ)
    )
    mixer_own = scatter_dp(weight_grads)
    back_in = times_transposed(grad_projected, mixer_full) + product(grad_extra, gates)
    back_in = scatter_seq(shares(back_in))
    grad_gate_up_own = exchange(grad_gate_up_own.reshape(n_seq, rows, -1))
    output_own = residual + scatter_seq(shares(product(activ, down_full)))
    grad_w_gate, grad_w_up = ff_unpack(grad_gate_up_own, ff_rows)
    back_in, grad_w_gate, grad_w_up = lax.optimization_barrier((back_in, grad_w_gate, grad_w_up))
    tokens = x_own.astype(f32)
    _, pull_in = jax.vjp(rms_scale, tokens, gain_attn)
    grad_tok_norm, grad_gain_attn = pull_in(back_in)
    input_grad = grad_res + grad_tok_norm

    conv_grad = jnp.zeros((taps, 3, group, mine, bands, head_width), f32)
    conv_grad = lax.dynamic_update_slice(
        conv_grad,
        grad_conv.reshape(taps, 3, 1, mine, 1, head_width),
        (0, 0, place, 0, band, 0),
    )
    conv_grad = jnp.transpose(conv_grad.reshape(taps, devices, -1), (1, 0, 2))
    gate_grad = contract_rows(grad_extra, hidden_in)[: 2 * mine]
    def place_heads(vector):
        slots = jnp.zeros((group, mine, bands), f32)
        return lax.dynamic_update_slice(
            slots, vector.reshape(1, mine, 1), (place, 0, band)
        ).reshape(heads)

    def by_owner(values):
        split = values.reshape(-1, devices, rows)
        return jnp.transpose(split, (1, 0, 2)).reshape(devices, -1)

    common = jnp.concatenate([grad_head_gain, place_heads(grad_rate), place_heads(grad_bias)])
    parts = [
        by_owner(gate_grad),
        by_owner(jnp.stack([grad_gain_attn, grad_gain_mlp])),
        conv_grad.reshape(devices, -1),
        jnp.broadcast_to(common[None], (devices, common.shape[0])),
    ]
    edges = [0]
    for part in parts:
        edges.append(edges[-1] + part.shape[1])
    parts.append(jnp.zeros((devices, -edges[-1] % 128), f32))
    swapped = swap_all(jnp.concatenate(parts, axis=1))
    done = lax.optimization_barrier(
        (swapped, grad_w_gate, grad_w_up, grad_down.astype(f32), output_own, input_grad)
    )
    mixer_own, *done = lax.optimization_barrier((mixer_own, *done))
    swapped, grad_w_gate, grad_w_up, grad_down, output_own, input_grad = done
    grad_output = mixer_own[:, 4 * cols :].reshape(rows, width).astype(f32)
    mixer_own = exchange(mixer_own[:, : 4 * cols].reshape(n_seq, rows, -1))
    sums = jnp.sum(swapped, axis=0)
    gate_sums = jnp.sum(swapped[:, : edges[1]].reshape(n_dp, n_seq, -1), axis=0)
    gate_sums = gate_sums.reshape(bands, group, 2, mine, rows)
    gate_sums = jnp.transpose(gate_sums, (2, 4, 1, 3, 0)).reshape(2, rows, heads)
    gain_sums = sums[edges[1] : edges[2]].reshape(2, rows)
    common = sums[edges[3] : edges[4]]
    return (
        output_own.astype(bf16).reshape(tokens_shape),
        input_grad.reshape(tokens_shape),
        gain_sums[0],
        by_columns(mixer_own[:, :, :cols]),
        by_columns(mixer_own[:, :, cols : 2 * cols]),
        by_columns(mixer_own[:, :, 2 * cols : 3 * cols]),
        sums[edges[2] : edges[3]].reshape(conv_weight.shape),
        gate_sums[0],
        gate_sums[1],
        common[head_width : head_width + heads],
        common[head_width + heads :],
        by_columns(mixer_own[:, :, 3 * cols :]),
        common[:head_width],
        grad_output,
        gain_sums[1],
        grad_w_gate,
        grad_w_up,
        grad_down,
    )


def solution(mesh):
    in_specs = (
        P(None, "dp", "seq", None),
        P(("dp", "seq")),
        P(("dp", "seq"), None),
        P(("dp", "seq"), None),
        P(("dp", "seq"), None),
        P(None, ("dp", "seq")),
        P(("dp", "seq"), None),
        P(("dp", "seq"), None),
        P(),
        P(),
        P(("dp", "seq"), None),
        P(),
        P(("dp", "seq"), None),
        P(("dp", "seq")),
        P(("dp", "seq"), None),
        P(("dp", "seq"), None),
        P(("dp", "seq"), None),
        P(None, "dp", "seq", None),
    )
    out_specs = (
        P(None, "dp", "seq", None),
        P(None, "dp", "seq", None),
        P(("dp", "seq")),
        P(("dp", "seq"), None),
        P(("dp", "seq"), None),
        P(("dp", "seq"), None),
        P(None, ("dp", "seq")),
        P(("dp", "seq"), None),
        P(("dp", "seq"), None),
        P(),
        P(),
        P(("dp", "seq"), None),
        P(),
        P(("dp", "seq"), None),
        P(("dp", "seq")),
        P(("dp", "seq"), None),
        P(("dp", "seq"), None),
        P(("dp", "seq"), None),
    )
    return jax.shard_map(
        on_device, mesh=mesh, in_specs=in_specs, out_specs=out_specs, check_vma=False
    )
```

```python
import functools

import jax
import jax.numpy as jnp
from jax import lax
from jax.experimental import pallas as pl
from jax.experimental.pallas import tpu as pltpu
from jax.sharding import PartitionSpec as P

BLOCK = 64
CONV = 4
MB = 2


eps_norm = 1e-06
highest = lax.Precision.HIGHEST


def rms_scale(values, gain_vec):
    return (
        values * lax.rsqrt(jnp.mean(values * values, axis=-1, keepdims=True) + eps_norm) * gain_vec
    )


def product(left_side, right_side):
    return jnp.dot(left_side, right_side, preferred_element_type=jnp.float32)


def contract_rows(left_side, right_side):
    return lax.dot_general(
        left_side, right_side, (((0,), (0,)), ((), ())), preferred_element_type=jnp.float32
    )


def times_transposed(left_side, right_side):
    return lax.dot_general(
        left_side, right_side, (((1,), (1,)), ((), ())), preferred_element_type=jnp.float32
    )


ALL = ("dp", "seq")


def swap(value, bit):
    count = lax.axis_size("seq")
    return lax.ppermute(value, "seq", [(place, place ^ bit) for place in range(count)])


def seq_offsets():
    count = lax.axis_size("seq")
    half = count // 2
    return [2 * place for place in range(half)] + [2 * place + 1 for place in range(half)]


def gather_seq(value):
    count = lax.axis_size("seq")
    held = {0: value}
    if count == 8:
        half = value.shape[0] // 2
        held[2] = swap(value, 2)
        held[4] = swap(value, 4)
        held[6] = jnp.concatenate(
            [swap(held[2][:half], 4), swap(held[4][half:], 2)], axis=0
        )
    else:
        bit = 2
        while bit < count:
            for offset in list(held):
                held[offset | bit] = swap(held[offset], bit)
            bit *= 2
    for offset in list(held):
        held[offset | 1] = swap(held[offset], 1)
    return jnp.stack([held[offset] for offset in seq_offsets()], axis=0)


def add_low(left_side, right_side):
    return (left_side.astype(jnp.float32) + right_side.astype(jnp.float32)).astype(jnp.bfloat16)


def scatter_seq(parts):
    f32 = jnp.float32
    count = lax.axis_size("seq")
    half = count // 2
    own = add_low(parts[:half], swap(parts[half:], 1))
    if count == 8:
        rows = own.shape[1] // 2
        first, second = own[:, :rows], own[:, rows:]
        first = add_low(first[:2], swap(first[2:], 4))
        second_y = second[0::2]
        second = add_low(second_y, swap(second[1::2], 2))
        first = first[0].astype(f32) + swap(first[1], 2).astype(f32)
        second = second[0].astype(f32) + swap(second[1], 4).astype(f32)
        return jnp.concatenate([first, second], axis=0)
    while half > 1:
        half //= 2
        own = add_low(own[:half], swap(own[half:], 2 * half))
    return own[0].astype(f32)


NN = ((1,), (0,))
NT = ((1,), (1,))
TN = ((0,), (0,))
PAIR = 2


def low_dot(left_side, right_side, dims):
    bf16 = jnp.bfloat16
    return lax.dot_general(
        left_side.astype(bf16),
        right_side.astype(bf16),
        (dims, ((), ())),
        preferred_element_type=jnp.float32,
    )


def split_dot(left_side, right_side, dims, exact_left):
    whole = right_side if exact_left else left_side
    high = rounded(whole)
    parts = [(left_side, part) if exact_left else (part, right_side) for part in (high, whole - high)]
    return low_dot(*parts[0], dims) + low_dot(*parts[1], dims)


def rounded(value):
    return value.astype(jnp.bfloat16).astype(jnp.float32)


def softplus(value):
    return jnp.maximum(value, 0.0) + jnp.log1p(jnp.exp(-jnp.abs(value)))


def rows_sum(value):
    return jnp.sum(value, axis=1, keepdims=True)


def stack(pieces):
    return jnp.concatenate(pieces, axis=0)


def half(value, which):
    return value[which * BLOCK : (which + 1) * BLOCK]


def fill_masks(mask_ref, level_ref):
    size = PAIR * BLOCK
    down = lax.broadcasted_iota(jnp.int32, (size, size), 0)
    across = lax.broadcasted_iota(jnp.int32, (size, size), 1)
    apart = down ^ across
    mask_ref[0] = jnp.where((apart < BLOCK) & (down >= across), 1.0, 0.0)
    mask_ref[1] = jnp.where(apart == 0, 1.0, 0.0)
    for level in range(level_ref.shape[0]):
        inside = (apart >= 1 << level) & (apart < 2 << level) & (down > across)
        level_ref[level] = jnp.where(inside, 1.0, 0.0).astype(jnp.bfloat16)


def head_pieces(convolved, extras, gate_ref, mine, width):
    chains = []
    for conv_out, extra in zip(convolved, extras):
        active = conv_out * jax.nn.sigmoid(conv_out)
        beta = rounded(jax.nn.sigmoid(extra))
        decay = rounded(-gate_ref[0:1] * softplus(extra + gate_ref[1:2]))
        for head in range(mine):
            part = [
                active[:, (kind * mine + head) * width : (kind * mine + head + 1) * width]
                for kind in range(3)
            ]
            chains.append(
                part + [beta[:, mine + head : mine + head + 1], decay[:, head : head + 1]]
            )
    return chains


def block_values(chains, mask_ref, width):
    raw_query, raw_key, value, beta, decay = [stack(list(pieces)) for pieces in zip(*chains)]
    scale_query = lax.rsqrt(rows_sum(raw_query * raw_query) + eps_norm)
    scale_key = lax.rsqrt(rows_sum(raw_key * raw_key) + eps_norm)
    unit_query, unit_key = raw_query * scale_query, raw_key * scale_key
    query = rounded(unit_query * width ** (-0.5))
    key = rounded(unit_key)
    value = rounded(value)
    within = mask_ref[0]
    cumulative = low_dot(within, jnp.broadcast_to(decay, query.shape), NN)
    along = jnp.transpose(cumulative)[0:1, :]
    fall = within * jnp.exp(within * (cumulative[:, 0:1] - along))
    key_key = low_dot(key, key, NT)
    query_key = low_dot(query, key, NT)
    last = stack(
        [
            jnp.broadcast_to(half(cumulative, which)[BLOCK - 1 :], (BLOCK, width))
            for which in range(PAIR)
        ]
    )
    growth = jnp.exp(cumulative)
    key_fall = jnp.exp(last - cumulative)
    return dict(
        scale_query=scale_query,
        scale_key=scale_key,
        unit_query=unit_query,
        unit_key=unit_key,
        query=query,
        key=key,
        value=value,
        beta=beta,
        fall=fall,
        key_key=key_key,
        query_key=query_key,
        scores=query_key * fall,
        growth=growth,
        key_fall=key_fall,
        key_grown=growth * key,
        query_grown=growth * query,
        key_fallen=key_fall * key,
        totals=jnp.exp(last),
    )


def mixer_forward_body(
    me_ref,
    proj_ref,
    extra_ref,
    conv_ref,
    gate_ref,
    gain_ref,
    mixed_ref,
    conv_out_ref,
    core_ref,
    inverse_ref,
    made_ref,
    written_ref,
    memory_ref,
    rows_ref,
    state_ref,
    mask_ref,
    level_ref,
):
    bf16 = jnp.bfloat16
    sequences = proj_ref.shape[2]
    width = gain_ref.shape[1]
    cols = mixed_ref.shape[4]
    mine = cols // width
    pairs = sequences * mine // PAIR
    taps = conv_ref.shape[0]
    core_bit = jnp.bitwise_and(me_ref[0], 1)

    @pl.when(pl.program_id(0) == 0)
    def _():
        rows_ref[...] = jnp.zeros_like(rows_ref)
        state_ref[...] = jnp.zeros_like(state_ref)
        fill_masks(mask_ref, level_ref)

    blocks = []
    for block in range(2):
        spot = jnp.bitwise_xor(core_bit, block)
        convolved, extras = [], []
        for seq in range(sequences):
            rows_ref[seq, 8:] = rounded(proj_ref[spot, 0, seq, :, : 3 * cols])
            conv_out = conv_ref[0:1] * rows_ref[seq, 9 - taps : 9 - taps + BLOCK]
            for tap in range(1, taps):
                first = 9 - taps + tap
                conv_out = conv_out + conv_ref[tap : tap + 1] * rows_ref[seq, first : first + BLOCK]
            rows_ref[seq, 0:8] = rows_ref[seq, BLOCK : BLOCK + 8]
            conv_out_ref[0, block, seq] = conv_out
            convolved.append(conv_out)
            extras.append(extra_ref[spot, 0, seq])
        chains = head_pieces(convolved, extras, gate_ref, mine, width)
        for pair in range(pairs):
            made = block_values(chains[PAIR * pair : PAIR * (pair + 1)], mask_ref, width)
            lower = (made["beta"] * made["key_key"] * made["fall"]).astype(bf16)
            made["lower"] = lower
            made["inverse"] = mask_ref[1] - (level_ref[0] * lower).astype(jnp.float32)
            blocks.append((block, pair, made))
    for level in range(1, level_ref.shape[0]):
        inner = [
            low_dot(level_ref[level] * made["lower"], made["inverse"], NN) for _, _, made in blocks
        ]
        for (_, _, made), right_side in zip(blocks, inner):
            made["inverse"] = made["inverse"] - low_dot(made["inverse"], right_side, NN)
    for block, pair, made in blocks:
        inverse = made["inverse"].astype(bf16)
        inverse_ref[0, block, pair] = inverse
        weighted = jnp.concatenate(
            [made["beta"] * made["value"], made["beta"] * made["key_grown"]], axis=1
        )
        made["fresh_carried"] = low_dot(inverse, weighted, NN)
        made_ref[0, block, pair] = made["fresh_carried"].astype(bf16)
    for block, pair, made in blocks:
        fresh, carried = made["fresh_carried"][:, :width], made["fresh_carried"][:, width:]
        written, results = [], []
        for which in range(PAIR):
            chain = PAIR * pair + which
            state = state_ref[chain]
            low_state = state.astype(bf16)
            memory_ref[0, block, chain] = low_state
            seen = low_dot(
                stack([half(carried, which), half(made["query_grown"], which)]), low_state, NN
            )
            new = half(fresh, which) - seen[:BLOCK]
            written.append(new)
            results.append(seen[BLOCK:])
            state_ref[chain] = half(made["totals"], which)[0:1] * state + low_dot(
                half(made["key_fallen"], which), new, TN
            )
        written = stack(written).astype(bf16)
        written_ref[0, block, pair] = written
        core = (stack(results) + low_dot(made["scores"], written, NN)).astype(bf16)
        core_ref[0, block, pair] = core
        core = core.astype(jnp.float32)
        normed = core * lax.rsqrt(rows_sum(core * core) / width + eps_norm) * gain_ref[0:1]
        spot = jnp.bitwise_xor(core_bit, block)
        for which in range(PAIR):
            seq, head = divmod(PAIR * pair + which, mine)
            span = slice(head * width, (head + 1) * width)
            out_gate = proj_ref[
                spot, 0, seq, :, 3 * cols + head * width : 3 * cols + (head + 1) * width
            ]
            mixed = half(normed, which) * out_gate * jax.nn.sigmoid(out_gate)
            mixed_ref[spot, 0, seq, :, span] = mixed.astype(bf16)


def mixer_backward_body(
    me_ref,
    proj_ref,
    extra_ref,
    grad_mixed_ref,
    conv_out_ref,
    core_ref,
    inverse_ref,
    made_ref,
    written_ref,
    memory_ref,
    conv_ref,
    gate_ref,
    gain_ref,
    grad_proj_ref,
    grad_extra_ref,
    grad_conv_ref,
    grad_small_ref,
    rows_ref,
    state_ref,
    mask_ref,
    level_ref,
):
    f32 = jnp.float32
    bf16 = jnp.bfloat16
    sequences = proj_ref.shape[2]
    width = gain_ref.shape[1]
    cols = grad_mixed_ref.shape[4]
    mine = cols // width
    pairs = sequences * mine // PAIR
    taps = conv_ref.shape[0]
    core_bit = jnp.bitwise_and(me_ref[0], 1)

    @pl.when(pl.program_id(0) == 0)
    def _():
        rows_ref[...] = jnp.zeros_like(rows_ref)
        state_ref[...] = jnp.zeros_like(state_ref)
        grad_conv_ref[...] = jnp.zeros_like(grad_conv_ref)
        grad_small_ref[...] = jnp.zeros_like(grad_small_ref)
        fill_masks(mask_ref, level_ref)

    within = mask_ref[0]
    gain = gain_ref[0:1]
    grad_gain = jnp.zeros((1, width), f32)
    blocks = []
    for block in (1, 0):
        spot = jnp.bitwise_xor(core_bit, block)
        convolved = [conv_out_ref[0, block, seq] for seq in range(sequences)]
        extras = [extra_ref[spot, 0, seq] for seq in range(sequences)]
        chains = head_pieces(convolved, extras, gate_ref, mine, width)
        for pair in range(pairs):
            made = block_values(chains[PAIR * pair : PAIR * (pair + 1)], mask_ref, width)
            core = core_ref[0, block, pair].astype(f32)
            core_scale = lax.rsqrt(rows_sum(core * core) / width + eps_norm)
            normed = core * core_scale
            grad_unit = []
            for which in range(PAIR):
                seq, head = divmod(PAIR * pair + which, mine)
                span = slice(3 * cols + head * width, 3 * cols + (head + 1) * width)
                out_gate = proj_ref[spot, 0, seq, :, span]
                grad_mixed = grad_mixed_ref[
                    spot, 0, seq, :, head * width : (head + 1) * width
                ].astype(f32)
                sigmoid = jax.nn.sigmoid(out_gate)
                silu = out_gate * sigmoid
                scaled = grad_mixed * half(normed, which)
                grad_gate = scaled * gain * (sigmoid + silu * (1.0 - sigmoid))
                grad_proj_ref[spot, 0, seq, :, span] = grad_gate.astype(bf16)
                grad_gain = grad_gain + jnp.sum(scaled * silu, axis=0, keepdims=True)
                grad_unit.append(grad_mixed * gain * silu)
            grad_unit = stack(grad_unit)
            inner = rows_sum(grad_unit * normed) / width
            made["grad_core"] = (core_scale * (grad_unit - normed * inner)).astype(bf16)
            made["from_scores"] = low_dot(made["scores"], made["grad_core"], TN)
            made["grad_scores"] = (
                low_dot(made["grad_core"], written_ref[0, block, pair], NT) * made["fall"]
            )
            blocks.append((block, pair, made))
    grad_small_ref[0:1] += grad_gain

    for block, pair, made in blocks:
        carried = made_ref[0, block, pair, :, width:]
        parts = []
        for which in range(PAIR):
            chain = PAIR * pair + which
            state, grad_state = memory_ref[0, block, chain], state_ref[chain]
            low_grad_state = grad_state.astype(bf16)
            grad_out = half(made["grad_core"], which)
            grad_new = half(made["from_scores"], which) + low_dot(
                half(made["key_fallen"], which), low_grad_state, NN
            )
            low_new = grad_new.astype(bf16)
            totals = half(made["totals"], which)[0:1]
            state_ref[chain] = (
                totals * grad_state
                + low_dot(half(made["query_grown"], which), grad_out, TN)
                - low_dot(half(carried, which), low_new, TN)
            )
            back = low_dot(stack([grad_out, low_new]), state, NT)
            parts.append(
                (
                    low_new,
                    back[:BLOCK],
                    -back[BLOCK:],
                    low_dot(half(written_ref[0, block, pair], which), low_grad_state, NT),
                    rows_sum(
                        jnp.sum(state.astype(f32) * grad_state, axis=0, keepdims=True) * totals
                    ),
                )
            )
        made["grad_new"], made["grad_query_grown"], made["grad_carried"] = [
            stack([part[index] for part in parts]) for index in range(3)
        ]
        made["grad_key_fallen"] = stack([part[3] for part in parts])
        made["grad_totals"] = [part[4] for part in parts]

    lane = lax.broadcasted_iota(jnp.int32, (BLOCK, extra_ref.shape[4]), 1)
    at_end = lax.broadcasted_iota(jnp.int32, (BLOCK, 1), 0) == BLOCK - 1
    ones = jnp.ones((PAIR * BLOCK, width), bf16)
    results = {}
    for block, pair, made in blocks:
        beta, growth, fall = made["beta"], made["growth"], made["fall"]
        query, key, value = made["query"], made["key"], made["value"]
        fall_strict = fall - mask_ref[1]
        grad_weighted = low_dot(
            inverse_ref[0, block, pair],
            jnp.concatenate([made["grad_new"].astype(f32), made["grad_carried"]], axis=1),
            TN,
        )
        grad_lower = -low_dot(grad_weighted, made_ref[0, block, pair], NT) * fall_strict
        grad_key_key = grad_lower * beta
        from_lower = grad_lower * made["key_key"]
        grad_value_part, grad_key_part = grad_weighted[:, :width], grad_weighted[:, width:]
        grad_scores = made["grad_scores"]
        carried_part = grad_key_part * made["key_grown"]
        grad_beta = rows_sum(from_lower) + rows_sum(carried_part + grad_value_part * value)
        shifts = beta * from_lower + grad_scores * made["query_key"]
        fallen_part = made["grad_key_fallen"] * made["key_fallen"]
        fallen = rows_sum(fallen_part)
        grad_cumulative = rows_sum(shifts) + rows_sum(
            made["grad_query_grown"] * made["query_grown"] + beta * carried_part - fallen_part
        )
        ends = stack(
            [
                jnp.where(
                    at_end,
                    jnp.sum(half(fallen, which), axis=0, keepdims=True) + made["grad_totals"][which],
                    0.0,
                )
                for which in range(PAIR)
            ]
        )
        grad_cumulative = grad_cumulative + ends - split_dot(shifts, ones, TN, False)
        grad_decay = rounded(split_dot(within, grad_cumulative, TN, True))
        both = stack([grad_scores, grad_key_key]).astype(bf16)
        down = low_dot(both, key, NN)
        grad_query = growth * made["grad_query_grown"] + down[: PAIR * BLOCK]
        grad_key = (
            made["key_fall"] * made["grad_key_fallen"]
            + beta * growth * grad_key_part
            + down[PAIR * BLOCK :]
            + low_dot(both, stack([query, key]), TN)
        )
        grad_query = rounded(grad_query) * width ** (-0.5)
        grad_key = rounded(grad_key)
        grad_value = rounded(beta * grad_value_part)
        grad_beta = rounded(grad_beta)
        unit_query, unit_key = made["unit_query"], made["unit_key"]
        grad_query = made["scale_query"] * (
            grad_query - unit_query * rows_sum(grad_query * unit_query)
        )
        grad_key = made["scale_key"] * (grad_key - unit_key * rows_sum(grad_key * unit_key))
        for which in range(PAIR):
            results[block, PAIR * pair + which] = [
                half(part, which)
                for part in (grad_query, grad_key, grad_value, grad_decay, grad_beta)
            ]

    for block in (1, 0):
        spot = jnp.bitwise_xor(core_bit, block)
        for seq in range(sequences):
            conv_out = conv_out_ref[0, block, seq]
            sigmoid = jax.nn.sigmoid(conv_out)
            chains = [results[block, seq * mine + head] for head in range(mine)]
            grad_active = jnp.concatenate(
                [chain[kind] for kind in range(3) for chain in chains], axis=1
            )
            rows_ref[seq, :BLOCK] = grad_active * sigmoid * (1.0 + conv_out * (1.0 - sigmoid))
            pre = rounded(proj_ref[spot, 0, seq, :, : 3 * cols])
            grad_pre = jnp.zeros_like(conv_out)
            for tap in range(taps):
                shifted = rows_ref[seq, taps - 1 - tap : taps - 1 - tap + BLOCK]
                grad_pre = grad_pre + conv_ref[tap : tap + 1] * shifted
                grad_conv_ref[tap : tap + 1] += jnp.sum(pre * shifted, axis=0, keepdims=True)
            grad_proj_ref[spot, 0, seq, :, : 3 * cols] = grad_pre.astype(bf16)
            rows_ref[seq, BLOCK:] = rows_ref[seq, 0:8]
            extra = extra_ref[spot, 0, seq]
            moved = extra + gate_ref[1:2]
            spread_decay = jnp.zeros_like(extra)
            spread_beta = jnp.zeros_like(extra)
            for head, chain in enumerate(chains):
                spread_decay = jnp.where(lane == head, chain[3][:, 0:1], spread_decay)
                spread_beta = jnp.where(lane == mine + head, chain[4], spread_beta)
            grad_alpha = -gate_ref[0:1] * spread_decay * jax.nn.sigmoid(moved)
            squash = jax.nn.sigmoid(extra)
            grad_extra = grad_alpha + spread_beta * squash * (1.0 - squash)
            grad_extra_ref[spot, 0, seq] = grad_extra.astype(bf16)
            grad_small_ref[1:2] -= jnp.sum(spread_decay * softplus(moved), axis=0, keepdims=True)
            grad_small_ref[2:3] += jnp.sum(grad_alpha, axis=0, keepdims=True)


def ff_pack_body(width, gate_ref, up_ref, out_ref):
    count = out_ref.shape[0]
    blocks = gate_ref.shape[1] // (count * width)
    for spot in range(count):
        pieces = [
            ref[:, (block * count + spot) * width : (block * count + spot + 1) * width]
            for ref in (gate_ref, up_ref)
            for block in range(blocks)
        ]
        out_ref[spot] = jnp.concatenate(pieces, axis=1)


def ff_pack(gate, up, count, width):
    rows, hidden = gate.shape
    return pl.pallas_call(
        functools.partial(ff_pack_body, width),
        out_shape=jax.ShapeDtypeStruct((count, rows, 2 * hidden // count), gate.dtype),
    )(gate, up)


def ff_unpack_body(width, in_ref, gate_ref, up_ref):
    count = in_ref.shape[0]
    blocks = gate_ref.shape[1] // (count * width)
    for which, ref in enumerate((gate_ref, up_ref)):
        pieces = []
        for block in range(blocks):
            first = (which * blocks + block) * width
            pieces += [in_ref[spot, :, first : first + width] for spot in range(count)]
        ref[...] = jnp.concatenate([piece.astype(jnp.float32) for piece in pieces], axis=1)


def ff_unpack(packed, width):
    count, rows, columns = packed.shape
    shape = jax.ShapeDtypeStruct((rows, count * columns // 2), jnp.float32)
    return pl.pallas_call(functools.partial(ff_unpack_body, width), out_shape=[shape, shape])(packed)


def whole_spec(shape):
    return pl.BlockSpec(shape, lambda step, me: (0,) * len(shape))


def mixer_specs(projected, head_width, mine, forward):
    _, steps, sequences, span, _ = projected.shape
    chains = sequences * mine
    pairs = chains // PAIR
    cols = mine * head_width

    def step_of(step):
        return step if forward else steps - 1 - step

    def gathered(channels):
        return pl.BlockSpec(
            (2, 1, sequences, span, channels),
            lambda step, me: (
                0,
                jnp.bitwise_xor(jnp.right_shift(me[0], 1), step_of(step)),
                0,
                0,
                0,
            ),
        )

    def ordered(*shape):
        return pl.BlockSpec((1,) + shape, lambda step, me: (step_of(step),) + (0,) * len(shape))

    size = PAIR * span
    kept = [
        (jax.ShapeDtypeStruct((steps,) + shape, kind), ordered(*shape))
        for shape, kind in [
            ((2, sequences, span, 3 * cols), jnp.float32),
            ((2, pairs, size, head_width), jnp.bfloat16),
            ((2, pairs, size, size), jnp.bfloat16),
            ((2, pairs, size, 2 * head_width), jnp.bfloat16),
            ((2, pairs, size, head_width), jnp.bfloat16),
            ((2, chains, head_width, head_width), jnp.bfloat16),
        ]
    ]
    scratch = [
        pltpu.VMEM((sequences, span + 8, 3 * cols), jnp.float32),
        pltpu.VMEM((chains, head_width, head_width), jnp.float32),
        pltpu.VMEM((2, size, size), jnp.float32),
        pltpu.VMEM((int(BLOCK).bit_length() - 1, size, size), jnp.bfloat16),
    ]
    cost = pl.CostEstimate(
        flops=4 * steps * pairs * size**3 * 18,
        bytes_accessed=12 << 20,
        transcendentals=2 * steps << 18,
    )
    return gathered, kept, scratch, cost


def mixer_forward(me, projected, extra, conv_mine, gate_rows, gain_row, mine):
    channels = projected.shape[-1]
    head_width = gain_row.shape[1]
    gathered, kept, scratch, cost = mixer_specs(projected, head_width, mine, True)
    cols = mine * head_width
    return pl.pallas_call(
        mixer_forward_body,
        grid_spec=pltpu.PrefetchScalarGridSpec(
            num_scalar_prefetch=1,
            grid=(projected.shape[1],),
            in_specs=[
                gathered(channels),
                gathered(extra.shape[-1]),
                whole_spec(conv_mine.shape),
                whole_spec(gate_rows.shape),
                whole_spec(gain_row.shape),
            ],
            out_specs=[gathered(cols)] + [spec for _, spec in kept],
            scratch_shapes=scratch,
        ),
        out_shape=[jax.ShapeDtypeStruct(projected.shape[:-1] + (cols,), jnp.bfloat16)]
        + [shape for shape, _ in kept],
        compiler_params=pltpu.CompilerParams(vmem_limit_bytes=40 << 20),
        cost_estimate=cost,
    )(me, projected, extra, conv_mine, gate_rows, gain_row)


def mixer_backward(
    me, projected, extra, grad_mixed, kept_values, conv_mine, gate_rows, gain_row, mine
):
    channels = projected.shape[-1]
    head_width = gain_row.shape[1]
    gathered, kept, scratch, cost = mixer_specs(projected, head_width, mine, False)
    cols = mine * head_width
    return pl.pallas_call(
        mixer_backward_body,
        grid_spec=pltpu.PrefetchScalarGridSpec(
            num_scalar_prefetch=1,
            grid=(projected.shape[1],),
            in_specs=[gathered(channels), gathered(extra.shape[-1]), gathered(cols)]
            + [spec for _, spec in kept]
            + [
                whole_spec(conv_mine.shape),
                whole_spec(gate_rows.shape),
                whole_spec(gain_row.shape),
            ],
            out_specs=[
                gathered(channels),
                gathered(extra.shape[-1]),
                whole_spec(conv_mine.shape),
                whole_spec((8, head_width)),
            ],
            scratch_shapes=scratch,
        ),
        out_shape=[
            jax.ShapeDtypeStruct(projected.shape, jnp.bfloat16),
            jax.ShapeDtypeStruct(extra.shape, jnp.bfloat16),
            jax.ShapeDtypeStruct(conv_mine.shape, jnp.float32),
            jax.ShapeDtypeStruct((8, head_width), jnp.float32),
        ],
        compiler_params=pltpu.CompilerParams(vmem_limit_bytes=40 << 20),
        cost_estimate=cost,
    )(me, projected, extra, grad_mixed, *kept_values, conv_mine, gate_rows, gain_row)


def after(value, *others):
    return lax.optimization_barrier((value,) + others)[0]


def on_device(
    inputs,
    norm_attn,
    w_query,
    w_key,
    w_value,
    conv_weight,
    w_alpha,
    w_beta,
    decay_rate,
    decay_bias,
    w_outgate,
    head_gain,
    w_output,
    norm_mlp,
    w_gate,
    w_up,
    w_down,
    cotangent,
):
    f32 = jnp.float32
    bf16 = jnp.bfloat16
    n_dp = lax.axis_size("dp")
    n_seq = lax.axis_size("seq")
    devices = n_dp * n_seq
    me = lax.axis_index("seq")
    rows, width = w_query.shape
    heads = w_alpha.shape[1]
    head_width = head_gain.shape[0]
    mine = heads // n_seq
    cols = mine * head_width
    group = head_width // rows
    bands = n_seq // group
    band, place = me // group, me % group
    hidden = w_gate.shape[1]
    ff_rows = w_down.shape[0]
    ff = n_dp * ff_rows
    taps = conv_weight.shape[0]
    tokens_shape = inputs.shape
    span = inputs.shape[2]
    count = inputs.shape[0] * inputs.shape[1]
    total = n_seq * count * span

    def by_device(weight):
        split = weight.reshape(weight.shape[0], group, mine, bands, -1)
        return jnp.transpose(split, (3, 1, 0, 2, 4)).reshape(n_seq, weight.shape[0], -1)

    def by_columns(blocks):
        pieces = []
        for head in range(heads):
            spot, from_band = divmod(head, bands)
            from_place, which = divmod(spot, mine)
            block = blocks[from_band * group + from_place]
            pieces.append(block[:, which * head_width : (which + 1) * head_width])
        return jnp.concatenate(pieces, axis=1).astype(f32)

    def swap_all(blocks):
        return lax.all_to_all(blocks, ALL, split_axis=0, concat_axis=0, tiled=True)

    packed = jnp.concatenate([by_device(w) for w in (w_query, w_key, w_value, w_outgate)], axis=2)

    def exchange(blocks):
        return lax.all_to_all(blocks, "seq", split_axis=0, concat_axis=0, tiled=True)

    def gather_dp(block):
        return lax.all_gather(block, "dp", axis=0, tiled=True)

    sent = exchange(packed)
    mixer_full = gather_dp(sent.reshape(n_seq * rows, -1))
    shared = jnp.concatenate(
        [
            w_alpha.T.reshape(-1),
            w_beta.T.reshape(-1),
            norm_attn,
            norm_mlp,
            conv_weight.reshape(-1),
        ]
    )
    shared, w_gate, w_up, sent = lax.optimization_barrier((shared, w_gate, w_up, sent))
    shared = swap_all(jnp.broadcast_to(shared[None], (devices, shared.shape[0])))

    groups = [list(range(first, first + group)) for first in range(0, n_seq, group)]

    def exchange_group(blocks):
        if group == 2:
            away = swap(lax.dynamic_index_in_dim(blocks, 1 - place, 0, keepdims=False), 1)
            stay = lax.dynamic_index_in_dim(blocks, place, 0, keepdims=False)
            low = place == 0
            return jnp.stack([jnp.where(low, stay, away), jnp.where(low, away, stay)], axis=0)
        return lax.all_to_all(
            blocks, "seq", split_axis=0, concat_axis=0, tiled=True, axis_index_groups=groups
        )

    def to_heads(pieces):
        split = exchange_group(pieces.reshape(group, mine * rows, width))
        split = split.reshape(group, mine, rows, width)
        return jnp.transpose(split, (1, 0, 2, 3)).reshape(cols, width)

    def from_heads(full):
        split = jnp.transpose(full.reshape(mine, group, rows, width), (1, 0, 2, 3))
        return exchange_group(split.reshape(group, mine * rows, width))

    output_full = to_heads(gather_dp(w_output))

    gate_up_sent = exchange(ff_pack(w_gate, w_up, n_seq, ff_rows)).reshape(n_seq * rows, -1)
    gate_up_full = gather_dp(gate_up_sent)
    down_full = gather_dp(w_down).reshape(ff, width)
    mixer_full, shared, output_full = lax.optimization_barrier((mixer_full, shared, output_full))

    x_own = inputs.reshape(count * span, width)
    x_all = gather_seq(x_own).reshape(total, width)
    seed_own = cotangent.reshape(count * span, width)
    seed_all = gather_seq(seed_own).reshape(total, width)

    gates = shared[:, : 2 * heads * rows].reshape(devices, 2 * heads, rows)
    gates = jnp.transpose(gates, (1, 0, 2)).reshape(2, group, mine, bands, width)
    gates = lax.dynamic_index_in_dim(gates, band, 3, keepdims=False)
    gates = lax.dynamic_index_in_dim(gates, place, 1, keepdims=False).reshape(2 * mine, width)
    gates = jnp.pad(gates, ((0, 128 - 2 * mine), (0, 0)))
    first = 2 * heads * rows
    gain_attn = shared[:, first : first + rows].reshape(-1).astype(f32)
    gain_mlp = shared[:, first + rows : first + 2 * rows].reshape(-1).astype(f32)
    conv_all = shared[:, first + 2 * rows :].reshape(devices, taps, -1)
    conv_all = jnp.transpose(conv_all, (1, 0, 2)).reshape(taps, 3, group, mine, bands, head_width)
    conv_mine = lax.dynamic_index_in_dim(conv_all, band, 4, keepdims=False)
    conv_mine = lax.dynamic_index_in_dim(conv_mine, place, 2, keepdims=False)
    conv_mine = conv_mine.reshape(taps, 3 * cols).astype(f32)

    def my_heads(vector):
        split = lax.dynamic_index_in_dim(vector.reshape(group, mine, bands), band, 2, False)
        return lax.dynamic_index_in_dim(split, place, 0, keepdims=False)

    rate_mine = my_heads(decay_rate)
    bias_mine = my_heads(decay_bias)

    hidden_in = rms_scale(x_all.astype(f32), gain_attn).astype(bf16)
    projected = product(hidden_in, mixer_full)
    extra = times_transposed(hidden_in, gates).reshape(2, n_seq // 2, count, span, -1)

    projected = projected.reshape(2, n_seq // 2, count, span, -1)
    me_row = me.astype(jnp.int32).reshape(1)
    gate_rows = jnp.zeros((2, gates.shape[0]), f32)
    gate_rows = gate_rows.at[0, :mine].set(rate_mine).at[1, :mine].set(bias_mine)
    gain_row = head_gain.reshape(1, head_width)
    mixed, *kept_values = mixer_forward(
        me_row, projected, extra, conv_mine, gate_rows, gain_row, mine
    )
    mixed = mixed.reshape(total, cols)

    def shares(value):
        return value.astype(bf16).reshape(n_seq, count * span, -1)

    residual = x_own.astype(f32) + scatter_seq(shares(product(mixed, output_full)))
    normed_mid, pull_mid = jax.vjp(rms_scale, residual, gain_mlp)
    hidden_mid = gather_seq(normed_mid.astype(bf16)).reshape(total, width)
    gate_up = product(hidden_mid, gate_up_full)
    gate_pre, up_proj = gate_up[:, :ff], gate_up[:, ff:]
    sigmoid_gate = jax.nn.sigmoid(gate_pre)
    silu_gate = gate_pre * sigmoid_gate
    activ = (silu_gate * up_proj).astype(bf16)
    down_grads = contract_rows(activ, seed_all).astype(bf16)
    down_full = after(down_full, down_grads)
    from_down = times_transposed(seed_all, down_full)
    grad_gate = from_down * up_proj * sigmoid_gate * (1.0 + gate_pre * (1.0 - sigmoid_gate))
    grad_gate_up = jnp.concatenate([grad_gate, from_down * silu_gate], axis=1).astype(bf16)
    back_mid = scatter_seq(shares(times_transposed(grad_gate_up, gate_up_full)))
    grad_res_norm, grad_gain_mlp = pull_mid(back_mid)
    grad_res = seed_own.astype(f32) + grad_res_norm

    def scatter_dp(value):
        return lax.psum_scatter(value.astype(bf16), "dp", scatter_dimension=0, tiled=True)

    grad_down = scatter_dp(down_grads)
    grad_gate_up_own = scatter_dp(contract_rows(hidden_mid, grad_gate_up))

    grad_mixer_out = gather_seq(grad_res.astype(bf16)).reshape(total, width)
    grad_mixed = times_transposed(grad_mixer_out, output_full).astype(bf16)
    grad_projected, grad_extra, grad_conv, grad_small = mixer_backward(
        me_row,
        projected,
        extra,
        grad_mixed.reshape(2, n_seq // 2, count, span, cols),
        kept_values,
        conv_mine,
        gate_rows,
        gain_row,
        mine,
    )
    grad_projected = grad_projected.reshape(total, -1)
    grad_extra = grad_extra.reshape(total, -1)
    grad_head_gain = grad_small[0]
    grad_rate, grad_bias = grad_small[1, :mine], grad_small[2, :mine]
    grad_output = from_heads(contract_rows(mixed, grad_mixer_out).astype(bf16))
    weight_grads = contract_rows(hidden_in, grad_projected).astype(bf16)
    weight_grads, grad_projected, grad_extra, activ = lax.optimization_barrier(
        (weight_grads, grad_projected, grad_extra, activ)
    )
    mixer_own = scatter_dp(weight_grads)
    back_in = times_transposed(grad_projected, mixer_full) + product(grad_extra, gates)
    grad_output, back_in = lax.optimization_barrier((grad_output, back_in))
    grad_output = scatter_dp(grad_output.reshape(n_dp * rows, width))
    back_in = scatter_seq(shares(back_in))
    grad_gate_up_own = exchange(grad_gate_up_own.reshape(n_seq, rows, -1))
    output_own = residual + scatter_seq(shares(product(activ, down_full)))
    grad_w_gate, grad_w_up = ff_unpack(grad_gate_up_own, ff_rows)
    back_in, grad_w_gate, grad_w_up = lax.optimization_barrier((back_in, grad_w_gate, grad_w_up))
    tokens = x_own.astype(f32)
    _, pull_in = jax.vjp(rms_scale, tokens, gain_attn)
    grad_tok_norm, grad_gain_attn = pull_in(back_in)
    input_grad = grad_res + grad_tok_norm

    conv_grad = jnp.zeros((taps, 3, group, mine, bands, head_width), f32)
    conv_grad = lax.dynamic_update_slice(
        conv_grad,
        grad_conv.reshape(taps, 3, 1, mine, 1, head_width),
        (0, 0, place, 0, band, 0),
    )
    conv_grad = jnp.transpose(conv_grad.reshape(taps, devices, -1), (1, 0, 2))
    gate_grad = contract_rows(grad_extra, hidden_in)[: 2 * mine]
    def place_heads(vector):
        slots = jnp.zeros((group, mine, bands), f32)
        return lax.dynamic_update_slice(
            slots, vector.reshape(1, mine, 1), (place, 0, band)
        ).reshape(heads)

    def by_owner(values):
        split = values.reshape(-1, devices, rows)
        return jnp.transpose(split, (1, 0, 2)).reshape(devices, -1)

    common = jnp.concatenate([grad_head_gain, place_heads(grad_rate), place_heads(grad_bias)])
    parts = [
        by_owner(gate_grad),
        by_owner(jnp.stack([grad_gain_attn, grad_gain_mlp])),
        conv_grad.reshape(devices, -1),
        jnp.broadcast_to(common[None], (devices, common.shape[0])),
    ]
    edges = [0]
    for part in parts:
        edges.append(edges[-1] + part.shape[1])
    parts.append(jnp.zeros((devices, -edges[-1] % 128), f32))
    swapped = swap_all(jnp.concatenate(parts, axis=1))
    done = lax.optimization_barrier(
        (swapped, grad_w_gate, grad_w_up, grad_down.astype(f32), output_own, input_grad)
    )
    mixer_own, *done = lax.optimization_barrier((mixer_own, *done))
    swapped, grad_w_gate, grad_w_up, grad_down, output_own, input_grad = done
    mixer_own = exchange(mixer_own.reshape(n_seq, rows, -1))
    grad_output, mixer_own = lax.optimization_barrier((grad_output, mixer_own))
    grad_output = grad_output.astype(f32)
    sums = jnp.sum(swapped, axis=0)
    gate_sums = jnp.sum(swapped[:, : edges[1]].reshape(n_dp, n_seq, -1), axis=0)
    gate_sums = gate_sums.reshape(bands, group, 2, mine, rows)
    gate_sums = jnp.transpose(gate_sums, (2, 4, 1, 3, 0)).reshape(2, rows, heads)
    gain_sums = sums[edges[1] : edges[2]].reshape(2, rows)
    common = sums[edges[3] : edges[4]]
    return (
        output_own.astype(bf16).reshape(tokens_shape),
        input_grad.reshape(tokens_shape),
        gain_sums[0],
        by_columns(mixer_own[:, :, :cols]),
        by_columns(mixer_own[:, :, cols : 2 * cols]),
        by_columns(mixer_own[:, :, 2 * cols : 3 * cols]),
        sums[edges[2] : edges[3]].reshape(conv_weight.shape),
        gate_sums[0],
        gate_sums[1],
        common[head_width : head_width + heads],
        common[head_width + heads :],
        by_columns(mixer_own[:, :, 3 * cols :]),
        common[:head_width],
        grad_output,
        gain_sums[1],
        grad_w_gate,
        grad_w_up,
        grad_down,
    )


def solution(mesh):
    in_specs = (
        P(None, "dp", "seq", None),
        P(("dp", "seq")),
        P(("dp", "seq"), None),
        P(("dp", "seq"), None),
        P(("dp", "seq"), None),
        P(None, ("dp", "seq")),
        P(("dp", "seq"), None),
        P(("dp", "seq"), None),
        P(),
        P(),
        P(("dp", "seq"), None),
        P(),
        P(("dp", "seq"), None),
        P(("dp", "seq")),
        P(("dp", "seq"), None),
        P(("dp", "seq"), None),
        P(("dp", "seq"), None),
        P(None, "dp", "seq", None),
    )
    out_specs = (
        P(None, "dp", "seq", None),
        P(None, "dp", "seq", None),
        P(("dp", "seq")),
        P(("dp", "seq"), None),
        P(("dp", "seq"), None),
        P(("dp", "seq"), None),
        P(None, ("dp", "seq")),
        P(("dp", "seq"), None),
        P(("dp", "seq"), None),
        P(),
        P(),
        P(("dp", "seq"), None),
        P(),
        P(("dp", "seq"), None),
        P(("dp", "seq")),
        P(("dp", "seq"), None),
        P(("dp", "seq"), None),
        P(("dp", "seq"), None),
    )
    return jax.shard_map(
        on_device, mesh=mesh, in_specs=in_specs, out_specs=out_specs, check_vma=False
    )
```

```python
import functools

import jax
import jax.numpy as jnp
from jax import lax
from jax.experimental import pallas as pl
from jax.experimental.pallas import tpu as pltpu
from jax.sharding import PartitionSpec as P

BLOCK = 64
CONV = 4
MB = 2


eps_norm = 1e-06
highest = lax.Precision.HIGHEST


def rms_scale(values, gain_vec):
    return (
        values * lax.rsqrt(jnp.mean(values * values, axis=-1, keepdims=True) + eps_norm) * gain_vec
    )


def product(left_side, right_side):
    return jnp.dot(left_side, right_side, preferred_element_type=jnp.float32)


def contract_rows(left_side, right_side):
    return lax.dot_general(
        left_side, right_side, (((0,), (0,)), ((), ())), preferred_element_type=jnp.float32
    )


def times_transposed(left_side, right_side):
    return lax.dot_general(
        left_side, right_side, (((1,), (1,)), ((), ())), preferred_element_type=jnp.float32
    )


ALL = ("dp", "seq")


def swap(value, bit):
    count = lax.axis_size("seq")
    return lax.ppermute(value, "seq", [(place, place ^ bit) for place in range(count)])


def seq_offsets():
    count = lax.axis_size("seq")
    half = count // 2
    return [2 * place for place in range(half)] + [2 * place + 1 for place in range(half)]


def gather_seq(value):
    count = lax.axis_size("seq")
    held = {0: value}
    if count == 8:
        half = value.shape[0] // 2
        held[2] = swap(value, 2)
        held[4] = swap(value, 4)
        held[6] = jnp.concatenate(
            [swap(held[2][:half], 4), swap(held[4][half:], 2)], axis=0
        )
    else:
        bit = 2
        while bit < count:
            for offset in list(held):
                held[offset | bit] = swap(held[offset], bit)
            bit *= 2
    for offset in list(held):
        held[offset | 1] = swap(held[offset], 1)
    return jnp.stack([held[offset] for offset in seq_offsets()], axis=0)


def add_low(left_side, right_side):
    return (left_side.astype(jnp.float32) + right_side.astype(jnp.float32)).astype(jnp.bfloat16)


def scatter_seq(parts):
    f32 = jnp.float32
    count = lax.axis_size("seq")
    half = count // 2
    own = add_low(parts[:half], swap(parts[half:], 1))
    if count == 8:
        rows = own.shape[1] // 2
        first, second = own[:, :rows], own[:, rows:]
        first = add_low(first[:2], swap(first[2:], 4))
        second_y = second[0::2]
        second = add_low(second_y, swap(second[1::2], 2))
        first = first[0].astype(f32) + swap(first[1], 2).astype(f32)
        second = second[0].astype(f32) + swap(second[1], 4).astype(f32)
        return jnp.concatenate([first, second], axis=0)
    while half > 1:
        half //= 2
        own = add_low(own[:half], swap(own[half:], 2 * half))
    return own[0].astype(f32)


NN = ((1,), (0,))
NT = ((1,), (1,))
TN = ((0,), (0,))
PAIR = 2


def low_dot(left_side, right_side, dims):
    bf16 = jnp.bfloat16
    return lax.dot_general(
        left_side.astype(bf16),
        right_side.astype(bf16),
        (dims, ((), ())),
        preferred_element_type=jnp.float32,
    )


def two_terms(value):
    bf16 = jnp.bfloat16
    if value.dtype == bf16:
        return [value]
    high = value.astype(bf16)
    return [high, (value - high.astype(jnp.float32)).astype(bf16)]


def wide_dot(left_side, right_side, dims):
    left_terms, right_terms = two_terms(left_side), two_terms(right_side)
    result = low_dot(left_terms[0], right_terms[0], dims)
    for term in right_terms[1:]:
        result = result + low_dot(left_terms[0], term, dims)
    for term in left_terms[1:]:
        result = result + low_dot(term, right_terms[0], dims)
    return result


def rounded(value):
    return value.astype(jnp.bfloat16).astype(jnp.float32)


def softplus(value):
    return jnp.maximum(value, 0.0) + jnp.log1p(jnp.exp(-jnp.abs(value)))


def rows_sum(value):
    return jnp.sum(value, axis=1, keepdims=True)


def stack(pieces):
    return jnp.concatenate(pieces, axis=0)


def half(value, which):
    return value[which * BLOCK : (which + 1) * BLOCK]


def fill_masks(mask_ref, level_ref):
    size = PAIR * BLOCK
    down = lax.broadcasted_iota(jnp.int32, (size, size), 0)
    across = lax.broadcasted_iota(jnp.int32, (size, size), 1)
    apart = down ^ across
    mask_ref[0] = jnp.where((apart < BLOCK) & (down >= across), 1.0, 0.0)
    mask_ref[1] = jnp.where(apart == 0, 1.0, 0.0)
    for level in range(level_ref.shape[0]):
        inside = (apart >= 1 << level) & (apart < 2 << level) & (down > across)
        level_ref[level] = jnp.where(inside, 1.0, 0.0)


def head_pieces(convolved, extras, gate_ref, mine, width):
    chains = []
    for conv_out, extra in zip(convolved, extras):
        active = conv_out * jax.nn.sigmoid(conv_out)
        beta = rounded(jax.nn.sigmoid(extra))
        decay = rounded(-gate_ref[0:1] * softplus(extra + gate_ref[1:2]))
        for head in range(mine):
            part = [
                active[:, (kind * mine + head) * width : (kind * mine + head + 1) * width]
                for kind in range(3)
            ]
            chains.append(
                part + [beta[:, mine + head : mine + head + 1], decay[:, head : head + 1]]
            )
    return chains


def block_values(chains, mask_ref, width):
    raw_query, raw_key, value, beta, decay = [stack(list(pieces)) for pieces in zip(*chains)]
    scale_query = lax.rsqrt(rows_sum(raw_query * raw_query) + eps_norm)
    scale_key = lax.rsqrt(rows_sum(raw_key * raw_key) + eps_norm)
    unit_query, unit_key = raw_query * scale_query, raw_key * scale_key
    query = rounded(unit_query * width ** (-0.5))
    key = rounded(unit_key)
    value = rounded(value)
    within = mask_ref[0]
    cumulative = low_dot(within, jnp.broadcast_to(decay, query.shape), NN)
    along = jnp.transpose(cumulative)[0:1, :]
    fall = within * jnp.exp(within * (cumulative[:, 0:1] - along))
    key_key = low_dot(key, key, NT)
    query_key = low_dot(query, key, NT)
    last = stack(
        [
            jnp.broadcast_to(half(cumulative, which)[BLOCK - 1 :], (BLOCK, width))
            for which in range(PAIR)
        ]
    )
    growth = jnp.exp(cumulative)
    key_fall = jnp.exp(last - cumulative)
    return dict(
        scale_query=scale_query,
        scale_key=scale_key,
        unit_query=unit_query,
        unit_key=unit_key,
        query=query,
        key=key,
        value=value,
        beta=beta,
        fall=fall,
        key_key=key_key,
        query_key=query_key,
        scores=query_key * fall,
        growth=growth,
        key_fall=key_fall,
        key_grown=growth * key,
        query_grown=growth * query,
        key_fallen=key_fall * key,
        totals=jnp.exp(last),
    )


def mixer_forward_body(
    me_ref,
    proj_ref,
    extra_ref,
    conv_ref,
    gate_ref,
    gain_ref,
    mixed_ref,
    conv_out_ref,
    core_ref,
    inverse_ref,
    made_ref,
    written_ref,
    memory_ref,
    rows_ref,
    state_ref,
    mask_ref,
    level_ref,
):
    bf16 = jnp.bfloat16
    sequences = proj_ref.shape[2]
    width = gain_ref.shape[1]
    cols = mixed_ref.shape[4]
    mine = cols // width
    pairs = sequences * mine // PAIR
    taps = conv_ref.shape[0]
    core_bit = jnp.bitwise_and(me_ref[0], 1)

    @pl.when(pl.program_id(0) == 0)
    def _():
        rows_ref[...] = jnp.zeros_like(rows_ref)
        state_ref[...] = jnp.zeros_like(state_ref)
        fill_masks(mask_ref, level_ref)

    blocks = []
    for block in range(2):
        spot = jnp.bitwise_xor(core_bit, block)
        convolved, extras = [], []
        for seq in range(sequences):
            rows_ref[seq, 8:] = rounded(proj_ref[spot, 0, seq, :, : 3 * cols])
            conv_out = conv_ref[0:1] * rows_ref[seq, 9 - taps : 9 - taps + BLOCK]
            for tap in range(1, taps):
                first = 9 - taps + tap
                conv_out = conv_out + conv_ref[tap : tap + 1] * rows_ref[seq, first : first + BLOCK]
            rows_ref[seq, 0:8] = rows_ref[seq, BLOCK : BLOCK + 8]
            conv_out_ref[0, block, seq] = conv_out
            convolved.append(conv_out)
            extras.append(extra_ref[spot, 0, seq])
        chains = head_pieces(convolved, extras, gate_ref, mine, width)
        for pair in range(pairs):
            made = block_values(chains[PAIR * pair : PAIR * (pair + 1)], mask_ref, width)
            made["lower"] = made["beta"] * made["key_key"] * made["fall"]
            made["inverse"] = mask_ref[1] - level_ref[0] * made["lower"]
            blocks.append((block, pair, made))
    for level in range(1, level_ref.shape[0]):
        inner = [
            wide_dot(level_ref[level] * made["lower"], made["inverse"], NN) for _, _, made in blocks
        ]
        for (_, _, made), right_side in zip(blocks, inner):
            made["inverse"] = made["inverse"] - wide_dot(made["inverse"], right_side, NN)
    for block, pair, made in blocks:
        inverse = made["inverse"]
        inverse_ref[0, block, pair] = inverse
        weighted = jnp.concatenate(
            [made["beta"] * made["value"], made["beta"] * made["key_grown"]], axis=1
        )
        made["fresh_carried"] = wide_dot(inverse, weighted, NN)
        made_ref[0, block, pair] = made["fresh_carried"]
    for block, pair, made in blocks:
        fresh, carried = made["fresh_carried"][:, :width], made["fresh_carried"][:, width:]
        written, results = [], []
        for which in range(PAIR):
            chain = PAIR * pair + which
            state = state_ref[chain]
            memory_ref[0, block, chain] = state
            seen = wide_dot(
                stack([half(carried, which), half(made["query_grown"], which)]), state, NN
            )
            new = half(fresh, which) - seen[:BLOCK]
            written.append(new)
            results.append(seen[BLOCK:])
            state_ref[chain] = half(made["totals"], which)[0:1] * state + wide_dot(
                half(made["key_fallen"], which), new, TN
            )
        written = stack(written)
        written_ref[0, block, pair] = written
        core = (stack(results) + wide_dot(made["scores"], written, NN)).astype(bf16)
        core_ref[0, block, pair] = core
        core = core.astype(jnp.float32)
        normed = core * lax.rsqrt(rows_sum(core * core) / width + eps_norm) * gain_ref[0:1]
        spot = jnp.bitwise_xor(core_bit, block)
        for which in range(PAIR):
            seq, head = divmod(PAIR * pair + which, mine)
            span = slice(head * width, (head + 1) * width)
            out_gate = proj_ref[
                spot, 0, seq, :, 3 * cols + head * width : 3 * cols + (head + 1) * width
            ]
            mixed = half(normed, which) * out_gate * jax.nn.sigmoid(out_gate)
            mixed_ref[spot, 0, seq, :, span] = mixed.astype(bf16)


def mixer_backward_body(
    me_ref,
    proj_ref,
    extra_ref,
    grad_mixed_ref,
    conv_out_ref,
    core_ref,
    inverse_ref,
    made_ref,
    written_ref,
    memory_ref,
    conv_ref,
    gate_ref,
    gain_ref,
    grad_proj_ref,
    grad_extra_ref,
    grad_conv_ref,
    grad_small_ref,
    rows_ref,
    state_ref,
    mask_ref,
    level_ref,
):
    f32 = jnp.float32
    bf16 = jnp.bfloat16
    sequences = proj_ref.shape[2]
    width = gain_ref.shape[1]
    cols = grad_mixed_ref.shape[4]
    mine = cols // width
    pairs = sequences * mine // PAIR
    taps = conv_ref.shape[0]
    core_bit = jnp.bitwise_and(me_ref[0], 1)

    @pl.when(pl.program_id(0) == 0)
    def _():
        rows_ref[...] = jnp.zeros_like(rows_ref)
        state_ref[...] = jnp.zeros_like(state_ref)
        grad_conv_ref[...] = jnp.zeros_like(grad_conv_ref)
        grad_small_ref[...] = jnp.zeros_like(grad_small_ref)
        fill_masks(mask_ref, level_ref)

    within = mask_ref[0]
    gain = gain_ref[0:1]
    grad_gain = jnp.zeros((1, width), f32)
    blocks = []
    for block in (1, 0):
        spot = jnp.bitwise_xor(core_bit, block)
        convolved = [conv_out_ref[0, block, seq] for seq in range(sequences)]
        extras = [extra_ref[spot, 0, seq] for seq in range(sequences)]
        chains = head_pieces(convolved, extras, gate_ref, mine, width)
        for pair in range(pairs):
            made = block_values(chains[PAIR * pair : PAIR * (pair + 1)], mask_ref, width)
            core = core_ref[0, block, pair].astype(f32)
            core_scale = lax.rsqrt(rows_sum(core * core) / width + eps_norm)
            normed = core * core_scale
            grad_unit = []
            for which in range(PAIR):
                seq, head = divmod(PAIR * pair + which, mine)
                span = slice(3 * cols + head * width, 3 * cols + (head + 1) * width)
                out_gate = proj_ref[spot, 0, seq, :, span]
                grad_mixed = grad_mixed_ref[
                    spot, 0, seq, :, head * width : (head + 1) * width
                ].astype(f32)
                sigmoid = jax.nn.sigmoid(out_gate)
                silu = out_gate * sigmoid
                scaled = grad_mixed * half(normed, which)
                grad_gate = scaled * gain * (sigmoid + silu * (1.0 - sigmoid))
                grad_proj_ref[spot, 0, seq, :, span] = grad_gate.astype(bf16)
                grad_gain = grad_gain + jnp.sum(scaled * silu, axis=0, keepdims=True)
                grad_unit.append(grad_mixed * gain * silu)
            grad_unit = stack(grad_unit)
            inner = rows_sum(grad_unit * normed) / width
            made["grad_core"] = (core_scale * (grad_unit - normed * inner)).astype(bf16)
            made["from_scores"] = wide_dot(made["scores"], made["grad_core"], TN)
            made["grad_scores"] = (
                wide_dot(made["grad_core"], written_ref[0, block, pair], NT) * made["fall"]
            )
            blocks.append((block, pair, made))
    grad_small_ref[0:1] += grad_gain

    for block, pair, made in blocks:
        carried = made_ref[0, block, pair, :, width:]
        parts = []
        for which in range(PAIR):
            chain = PAIR * pair + which
            state, grad_state = memory_ref[0, block, chain], state_ref[chain]
            grad_out = half(made["grad_core"], which)
            grad_new = half(made["from_scores"], which) + wide_dot(
                half(made["key_fallen"], which), grad_state, NN
            )
            totals = half(made["totals"], which)[0:1]
            state_ref[chain] = (
                totals * grad_state
                + wide_dot(half(made["query_grown"], which), grad_out, TN)
                - wide_dot(half(carried, which), grad_new, TN)
            )
            parts.append(
                (
                    grad_new,
                    wide_dot(grad_out, state, NT),
                    -wide_dot(grad_new, state, NT),
                    wide_dot(half(written_ref[0, block, pair], which), grad_state, NT),
                    rows_sum(jnp.sum(state * grad_state, axis=0, keepdims=True) * totals),
                )
            )
        made["grad_new"], made["grad_query_grown"], made["grad_carried"] = [
            stack([part[index] for part in parts]) for index in range(3)
        ]
        made["grad_key_fallen"] = stack([part[3] for part in parts])
        made["grad_totals"] = [part[4] for part in parts]

    lane = lax.broadcasted_iota(jnp.int32, (BLOCK, extra_ref.shape[4]), 1)
    at_end = lax.broadcasted_iota(jnp.int32, (BLOCK, 1), 0) == BLOCK - 1
    ones = jnp.ones((PAIR * BLOCK, width), bf16)
    results = {}
    for block, pair, made in blocks:
        beta, growth, fall = made["beta"], made["growth"], made["fall"]
        query, key, value = made["query"], made["key"], made["value"]
        fall_strict = fall - mask_ref[1]
        grad_weighted = wide_dot(
            inverse_ref[0, block, pair],
            jnp.concatenate([made["grad_new"], made["grad_carried"]], axis=1),
            TN,
        )
        grad_lower = -wide_dot(grad_weighted, made_ref[0, block, pair], NT) * fall_strict
        grad_key_key = grad_lower * beta
        from_lower = grad_lower * made["key_key"]
        grad_value_part, grad_key_part = grad_weighted[:, :width], grad_weighted[:, width:]
        grad_scores = made["grad_scores"]
        carried_part = grad_key_part * made["key_grown"]
        grad_beta = rows_sum(from_lower) + rows_sum(carried_part + grad_value_part * value)
        shifts = beta * from_lower + grad_scores * made["query_key"]
        fallen_part = made["grad_key_fallen"] * made["key_fallen"]
        fallen = rows_sum(fallen_part)
        grad_cumulative = rows_sum(shifts) + rows_sum(
            made["grad_query_grown"] * made["query_grown"] + beta * carried_part - fallen_part
        )
        ends = stack(
            [
                jnp.where(
                    at_end,
                    jnp.sum(half(fallen, which), axis=0, keepdims=True) + made["grad_totals"][which],
                    0.0,
                )
                for which in range(PAIR)
            ]
        )
        grad_cumulative = grad_cumulative + ends - wide_dot(shifts, ones, TN)
        grad_decay = rounded(wide_dot(within.astype(bf16), grad_cumulative, TN))
        both = stack([grad_scores, grad_key_key])
        down = wide_dot(both, key.astype(bf16), NN)
        grad_query = growth * made["grad_query_grown"] + down[: PAIR * BLOCK]
        grad_key = (
            made["key_fall"] * made["grad_key_fallen"]
            + beta * growth * grad_key_part
            + down[PAIR * BLOCK :]
            + wide_dot(both, stack([query, key]).astype(bf16), TN)
        )
        grad_query = rounded(grad_query) * width ** (-0.5)
        grad_key = rounded(grad_key)
        grad_value = rounded(beta * grad_value_part)
        grad_beta = rounded(grad_beta)
        unit_query, unit_key = made["unit_query"], made["unit_key"]
        grad_query = made["scale_query"] * (
            grad_query - unit_query * rows_sum(grad_query * unit_query)
        )
        grad_key = made["scale_key"] * (grad_key - unit_key * rows_sum(grad_key * unit_key))
        for which in range(PAIR):
            results[block, PAIR * pair + which] = [
                half(part, which)
                for part in (grad_query, grad_key, grad_value, grad_decay, grad_beta)
            ]

    for block in (1, 0):
        spot = jnp.bitwise_xor(core_bit, block)
        for seq in range(sequences):
            conv_out = conv_out_ref[0, block, seq]
            sigmoid = jax.nn.sigmoid(conv_out)
            chains = [results[block, seq * mine + head] for head in range(mine)]
            grad_active = jnp.concatenate(
                [chain[kind] for kind in range(3) for chain in chains], axis=1
            )
            rows_ref[seq, :BLOCK] = grad_active * sigmoid * (1.0 + conv_out * (1.0 - sigmoid))
            pre = rounded(proj_ref[spot, 0, seq, :, : 3 * cols])
            grad_pre = jnp.zeros_like(conv_out)
            for tap in range(taps):
                shifted = rows_ref[seq, taps - 1 - tap : taps - 1 - tap + BLOCK]
                grad_pre = grad_pre + conv_ref[tap : tap + 1] * shifted
                grad_conv_ref[tap : tap + 1] += jnp.sum(pre * shifted, axis=0, keepdims=True)
            grad_proj_ref[spot, 0, seq, :, : 3 * cols] = grad_pre.astype(bf16)
            rows_ref[seq, BLOCK:] = rows_ref[seq, 0:8]
            extra = extra_ref[spot, 0, seq]
            moved = extra + gate_ref[1:2]
            spread_decay = jnp.zeros_like(extra)
            spread_beta = jnp.zeros_like(extra)
            for head, chain in enumerate(chains):
                spread_decay = jnp.where(lane == head, chain[3][:, 0:1], spread_decay)
                spread_beta = jnp.where(lane == mine + head, chain[4], spread_beta)
            grad_alpha = -gate_ref[0:1] * spread_decay * jax.nn.sigmoid(moved)
            squash = jax.nn.sigmoid(extra)
            grad_extra = grad_alpha + spread_beta * squash * (1.0 - squash)
            grad_extra_ref[spot, 0, seq] = grad_extra.astype(bf16)
            grad_small_ref[1:2] -= jnp.sum(spread_decay * softplus(moved), axis=0, keepdims=True)
            grad_small_ref[2:3] += jnp.sum(grad_alpha, axis=0, keepdims=True)


def ff_pack_body(width, gate_ref, up_ref, out_ref):
    count = out_ref.shape[0]
    blocks = gate_ref.shape[1] // (count * width)
    for spot in range(count):
        pieces = [
            ref[:, (block * count + spot) * width : (block * count + spot + 1) * width]
            for ref in (gate_ref, up_ref)
            for block in range(blocks)
        ]
        out_ref[spot] = jnp.concatenate(pieces, axis=1)


def ff_pack(gate, up, count, width):
    rows, hidden = gate.shape
    return pl.pallas_call(
        functools.partial(ff_pack_body, width),
        out_shape=jax.ShapeDtypeStruct((count, rows, 2 * hidden // count), gate.dtype),
    )(gate, up)


def ff_unpack_body(width, in_ref, gate_ref, up_ref):
    count = in_ref.shape[0]
    blocks = gate_ref.shape[1] // (count * width)
    for which, ref in enumerate((gate_ref, up_ref)):
        pieces = []
        for block in range(blocks):
            first = (which * blocks + block) * width
            pieces += [in_ref[spot, :, first : first + width] for spot in range(count)]
        ref[...] = jnp.concatenate([piece.astype(jnp.float32) for piece in pieces], axis=1)


def ff_unpack(packed, width):
    count, rows, columns = packed.shape
    shape = jax.ShapeDtypeStruct((rows, count * columns // 2), jnp.float32)
    return pl.pallas_call(functools.partial(ff_unpack_body, width), out_shape=[shape, shape])(packed)


def mixer_unpack_body(order, in_ref, *out_refs):
    width = out_refs[0].shape[1] // len(order)
    columns = in_ref.shape[2] // len(out_refs)
    for which, ref in enumerate(out_refs):
        for head, (spot, place) in enumerate(order):
            first = which * columns + place * width
            piece = in_ref[spot, :, first : first + width].astype(jnp.float32)
            ref[:, head * width : (head + 1) * width] = piece


def mixer_unpack(packed, order, head_width):
    shape = jax.ShapeDtypeStruct((packed.shape[1], len(order) * head_width), jnp.float32)
    return pl.pallas_call(functools.partial(mixer_unpack_body, order), out_shape=[shape] * 4)(packed)


def whole_spec(shape):
    return pl.BlockSpec(shape, lambda step, me: (0,) * len(shape))


def mixer_specs(projected, head_width, mine, forward):
    _, steps, sequences, span, _ = projected.shape
    chains = sequences * mine
    pairs = chains // PAIR
    cols = mine * head_width

    def step_of(step):
        return step if forward else steps - 1 - step

    def gathered(channels):
        return pl.BlockSpec(
            (2, 1, sequences, span, channels),
            lambda step, me: (
                0,
                jnp.bitwise_xor(jnp.right_shift(me[0], 1), step_of(step)),
                0,
                0,
                0,
            ),
        )

    def ordered(*shape):
        return pl.BlockSpec((1,) + shape, lambda step, me: (step_of(step),) + (0,) * len(shape))

    size = PAIR * span
    kept = [
        (jax.ShapeDtypeStruct((steps,) + shape, kind), ordered(*shape))
        for shape, kind in [
            ((2, sequences, span, 3 * cols), jnp.float32),
            ((2, pairs, size, head_width), jnp.bfloat16),
            ((2, pairs, size, size), jnp.float32),
            ((2, pairs, size, 2 * head_width), jnp.float32),
            ((2, pairs, size, head_width), jnp.float32),
            ((2, chains, head_width, head_width), jnp.float32),
        ]
    ]
    scratch = [
        pltpu.VMEM((sequences, span + 8, 3 * cols), jnp.float32),
        pltpu.VMEM((chains, head_width, head_width), jnp.float32),
        pltpu.VMEM((2, size, size), jnp.float32),
        pltpu.VMEM((int(BLOCK).bit_length() - 1, size, size), jnp.float32),
    ]
    cost = pl.CostEstimate(
        flops=4 * steps * pairs * size**3 * 18,
        bytes_accessed=12 << 20,
        transcendentals=2 * steps << 18,
    )
    return gathered, kept, scratch, cost


def mixer_forward(me, projected, extra, conv_mine, gate_rows, gain_row, mine):
    channels = projected.shape[-1]
    head_width = gain_row.shape[1]
    gathered, kept, scratch, cost = mixer_specs(projected, head_width, mine, True)
    cols = mine * head_width
    return pl.pallas_call(
        mixer_forward_body,
        grid_spec=pltpu.PrefetchScalarGridSpec(
            num_scalar_prefetch=1,
            grid=(projected.shape[1],),
            in_specs=[
                gathered(channels),
                gathered(extra.shape[-1]),
                whole_spec(conv_mine.shape),
                whole_spec(gate_rows.shape),
                whole_spec(gain_row.shape),
            ],
            out_specs=[gathered(cols)] + [spec for _, spec in kept],
            scratch_shapes=scratch,
        ),
        out_shape=[jax.ShapeDtypeStruct(projected.shape[:-1] + (cols,), jnp.bfloat16)]
        + [shape for shape, _ in kept],
        compiler_params=pltpu.CompilerParams(vmem_limit_bytes=40 << 20),
        cost_estimate=cost,
    )(me, projected, extra, conv_mine, gate_rows, gain_row)


def mixer_backward(
    me, projected, extra, grad_mixed, kept_values, conv_mine, gate_rows, gain_row, mine
):
    channels = projected.shape[-1]
    head_width = gain_row.shape[1]
    gathered, kept, scratch, cost = mixer_specs(projected, head_width, mine, False)
    cols = mine * head_width
    return pl.pallas_call(
        mixer_backward_body,
        grid_spec=pltpu.PrefetchScalarGridSpec(
            num_scalar_prefetch=1,
            grid=(projected.shape[1],),
            in_specs=[gathered(channels), gathered(extra.shape[-1]), gathered(cols)]
            + [spec for _, spec in kept]
            + [
                whole_spec(conv_mine.shape),
                whole_spec(gate_rows.shape),
                whole_spec(gain_row.shape),
            ],
            out_specs=[
                gathered(channels),
                gathered(extra.shape[-1]),
                whole_spec(conv_mine.shape),
                whole_spec((8, head_width)),
            ],
            scratch_shapes=scratch,
        ),
        out_shape=[
            jax.ShapeDtypeStruct(projected.shape, jnp.bfloat16),
            jax.ShapeDtypeStruct(extra.shape, jnp.bfloat16),
            jax.ShapeDtypeStruct(conv_mine.shape, jnp.float32),
            jax.ShapeDtypeStruct((8, head_width), jnp.float32),
        ],
        compiler_params=pltpu.CompilerParams(vmem_limit_bytes=40 << 20),
        cost_estimate=cost,
    )(me, projected, extra, grad_mixed, *kept_values, conv_mine, gate_rows, gain_row)


def after(value, *others):
    return lax.optimization_barrier((value,) + others)[0]


def on_device(
    inputs,
    norm_attn,
    w_query,
    w_key,
    w_value,
    conv_weight,
    w_alpha,
    w_beta,
    decay_rate,
    decay_bias,
    w_outgate,
    head_gain,
    w_output,
    norm_mlp,
    w_gate,
    w_up,
    w_down,
    cotangent,
):
    f32 = jnp.float32
    bf16 = jnp.bfloat16
    n_dp = lax.axis_size("dp")
    n_seq = lax.axis_size("seq")
    devices = n_dp * n_seq
    me = lax.axis_index("seq")
    rows, width = w_query.shape
    heads = w_alpha.shape[1]
    head_width = head_gain.shape[0]
    mine = heads // n_seq
    cols = mine * head_width
    group = head_width // rows
    bands = n_seq // group
    band, place = me // group, me % group
    hidden = w_gate.shape[1]
    ff_rows = w_down.shape[0]
    ff = n_dp * ff_rows
    taps = conv_weight.shape[0]
    tokens_shape = inputs.shape
    span = inputs.shape[2]
    count = inputs.shape[0] * inputs.shape[1]
    total = n_seq * count * span

    def by_device(weight):
        split = weight.reshape(weight.shape[0], group, mine, bands, -1)
        return jnp.transpose(split, (3, 1, 0, 2, 4)).reshape(n_seq, weight.shape[0], -1)

    def by_columns(blocks):
        pieces = []
        for head in range(heads):
            spot, from_band = divmod(head, bands)
            from_place, which = divmod(spot, mine)
            block = blocks[from_band * group + from_place]
            pieces.append(block[:, which * head_width : (which + 1) * head_width])
        return jnp.concatenate(pieces, axis=1).astype(f32)

    def swap_all(blocks):
        return lax.all_to_all(blocks, ALL, split_axis=0, concat_axis=0, tiled=True)

    packed = jnp.concatenate([by_device(w) for w in (w_query, w_key, w_value, w_outgate)], axis=2)

    def exchange(blocks):
        return lax.all_to_all(blocks, "seq", split_axis=0, concat_axis=0, tiled=True)

    def gather_dp(block):
        return lax.all_gather(block, "dp", axis=0, tiled=True)

    sent = exchange(packed)
    mixer_full = gather_dp(sent.reshape(n_seq * rows, -1))
    shared = jnp.concatenate(
        [
            w_alpha.T.reshape(-1),
            w_beta.T.reshape(-1),
            norm_attn,
            norm_mlp,
            conv_weight.reshape(-1),
        ]
    )
    shared, w_gate, w_up, sent = lax.optimization_barrier((shared, w_gate, w_up, sent))
    shared = swap_all(jnp.broadcast_to(shared[None], (devices, shared.shape[0])))

    groups = [list(range(first, first + group)) for first in range(0, n_seq, group)]

    def exchange_group(blocks):
        if group == 2:
            away = swap(lax.dynamic_index_in_dim(blocks, 1 - place, 0, keepdims=False), 1)
            stay = lax.dynamic_index_in_dim(blocks, place, 0, keepdims=False)
            low = place == 0
            return jnp.stack([jnp.where(low, stay, away), jnp.where(low, away, stay)], axis=0)
        return lax.all_to_all(
            blocks, "seq", split_axis=0, concat_axis=0, tiled=True, axis_index_groups=groups
        )

    def to_heads(pieces):
        split = exchange_group(pieces.reshape(group, mine * rows, width))
        split = split.reshape(group, mine, rows, width)
        return jnp.transpose(split, (1, 0, 2, 3)).reshape(cols, width)

    def from_heads(full):
        split = jnp.transpose(full.reshape(mine, group, rows, width), (1, 0, 2, 3))
        return exchange_group(split.reshape(group, mine * rows, width))

    output_full = to_heads(gather_dp(w_output))

    gate_up_sent = exchange(ff_pack(w_gate, w_up, n_seq, ff_rows)).reshape(n_seq * rows, -1)
    gate_up_full = gather_dp(gate_up_sent)
    down_full = gather_dp(w_down).reshape(ff, width)
    mixer_full, shared, output_full = lax.optimization_barrier((mixer_full, shared, output_full))

    x_own = inputs.reshape(count * span, width)
    x_all = gather_seq(x_own).reshape(total, width)
    seed_own = cotangent.reshape(count * span, width)
    seed_all = gather_seq(seed_own).reshape(total, width)

    gates = shared[:, : 2 * heads * rows].reshape(devices, 2 * heads, rows)
    gates = jnp.transpose(gates, (1, 0, 2)).reshape(2, group, mine, bands, width)
    gates = lax.dynamic_index_in_dim(gates, band, 3, keepdims=False)
    gates = lax.dynamic_index_in_dim(gates, place, 1, keepdims=False).reshape(2 * mine, width)
    gates = jnp.pad(gates, ((0, 128 - 2 * mine), (0, 0)))
    first = 2 * heads * rows
    gain_attn = shared[:, first : first + rows].reshape(-1).astype(f32)
    gain_mlp = shared[:, first + rows : first + 2 * rows].reshape(-1).astype(f32)
    conv_all = shared[:, first + 2 * rows :].reshape(devices, taps, -1)
    conv_all = jnp.transpose(conv_all, (1, 0, 2)).reshape(taps, 3, group, mine, bands, head_width)
    conv_mine = lax.dynamic_index_in_dim(conv_all, band, 4, keepdims=False)
    conv_mine = lax.dynamic_index_in_dim(conv_mine, place, 2, keepdims=False)
    conv_mine = conv_mine.reshape(taps, 3 * cols).astype(f32)

    def my_heads(vector):
        split = lax.dynamic_index_in_dim(vector.reshape(group, mine, bands), band, 2, False)
        return lax.dynamic_index_in_dim(split, place, 0, keepdims=False)

    rate_mine = my_heads(decay_rate)
    bias_mine = my_heads(decay_bias)

    hidden_in = rms_scale(x_all.astype(f32), gain_attn).astype(bf16)
    projected = product(hidden_in, mixer_full)
    extra = times_transposed(hidden_in, gates).reshape(2, n_seq // 2, count, span, -1)

    projected = projected.reshape(2, n_seq // 2, count, span, -1)
    me_row = me.astype(jnp.int32).reshape(1)
    gate_rows = jnp.zeros((2, gates.shape[0]), f32)
    gate_rows = gate_rows.at[0, :mine].set(rate_mine).at[1, :mine].set(bias_mine)
    gain_row = head_gain.reshape(1, head_width)
    mixed, *kept_values = mixer_forward(
        me_row, projected, extra, conv_mine, gate_rows, gain_row, mine
    )
    mixed = mixed.reshape(total, cols)

    def shares(value):
        return value.astype(bf16).reshape(n_seq, count * span, -1)

    residual = x_own.astype(f32) + scatter_seq(shares(product(mixed, output_full)))
    normed_mid, pull_mid = jax.vjp(rms_scale, residual, gain_mlp)
    hidden_mid = gather_seq(normed_mid.astype(bf16)).reshape(total, width)
    gate_up = product(hidden_mid, gate_up_full)
    gate_pre, up_proj = gate_up[:, :ff], gate_up[:, ff:]
    sigmoid_gate = jax.nn.sigmoid(gate_pre)
    silu_gate = gate_pre * sigmoid_gate
    activ = (silu_gate * up_proj).astype(bf16)
    down_grads = contract_rows(activ, seed_all).astype(bf16)
    down_full = after(down_full, down_grads)
    from_down = times_transposed(seed_all, down_full)
    grad_gate = from_down * up_proj * sigmoid_gate * (1.0 + gate_pre * (1.0 - sigmoid_gate))
    grad_gate_up = jnp.concatenate([grad_gate, from_down * silu_gate], axis=1).astype(bf16)
    back_mid = scatter_seq(shares(times_transposed(grad_gate_up, gate_up_full)))
    grad_res_norm, grad_gain_mlp = pull_mid(back_mid)
    grad_res = seed_own.astype(f32) + grad_res_norm

    def scatter_dp(value):
        return lax.psum_scatter(value.astype(bf16), "dp", scatter_dimension=0, tiled=True)

    grad_down = scatter_dp(down_grads)
    grad_gate_up_own = scatter_dp(contract_rows(hidden_mid, grad_gate_up))

    grad_mixer_out = gather_seq(grad_res.astype(bf16)).reshape(total, width)
    grad_mixed = times_transposed(grad_mixer_out, output_full).astype(bf16)
    grad_projected, grad_extra, grad_conv, grad_small = mixer_backward(
        me_row,
        projected,
        extra,
        grad_mixed.reshape(2, n_seq // 2, count, span, cols),
        kept_values,
        conv_mine,
        gate_rows,
        gain_row,
        mine,
    )
    grad_projected = grad_projected.reshape(total, -1)
    grad_extra = grad_extra.reshape(total, -1)
    grad_head_gain = grad_small[0]
    grad_rate, grad_bias = grad_small[1, :mine], grad_small[2, :mine]
    grad_output = from_heads(contract_rows(mixed, grad_mixer_out).astype(bf16))
    weight_grads = contract_rows(hidden_in, grad_projected).astype(bf16)
    weight_grads, grad_projected, grad_extra, activ = lax.optimization_barrier(
        (weight_grads, grad_projected, grad_extra, activ)
    )
    mixer_own = scatter_dp(weight_grads)
    back_in = times_transposed(grad_projected, mixer_full) + product(grad_extra, gates)
    grad_output, back_in = lax.optimization_barrier((grad_output, back_in))
    grad_output = scatter_dp(grad_output.reshape(n_dp * rows, width))
    back_in = scatter_seq(shares(back_in))
    grad_gate_up_own = exchange(grad_gate_up_own.reshape(n_seq, rows, -1))
    output_own = residual + scatter_seq(shares(product(activ, down_full)))
    grad_w_gate, grad_w_up = ff_unpack(grad_gate_up_own, ff_rows)
    back_in, grad_w_gate, grad_w_up = lax.optimization_barrier((back_in, grad_w_gate, grad_w_up))
    tokens = x_own.astype(f32)
    _, pull_in = jax.vjp(rms_scale, tokens, gain_attn)
    grad_tok_norm, grad_gain_attn = pull_in(back_in)
    input_grad = grad_res + grad_tok_norm

    conv_grad = jnp.zeros((taps, 3, group, mine, bands, head_width), f32)
    conv_grad = lax.dynamic_update_slice(
        conv_grad,
        grad_conv.reshape(taps, 3, 1, mine, 1, head_width),
        (0, 0, place, 0, band, 0),
    )
    conv_grad = jnp.transpose(conv_grad.reshape(taps, devices, -1), (1, 0, 2))
    gate_grad = contract_rows(grad_extra, hidden_in)[: 2 * mine]
    def place_heads(vector):
        slots = jnp.zeros((group, mine, bands), f32)
        return lax.dynamic_update_slice(
            slots, vector.reshape(1, mine, 1), (place, 0, band)
        ).reshape(heads)

    def by_owner(values):
        split = values.reshape(-1, devices, rows)
        return jnp.transpose(split, (1, 0, 2)).reshape(devices, -1)

    common = jnp.concatenate([grad_head_gain, place_heads(grad_rate), place_heads(grad_bias)])
    parts = [
        by_owner(gate_grad),
        by_owner(jnp.stack([grad_gain_attn, grad_gain_mlp])),
        conv_grad.reshape(devices, -1),
        jnp.broadcast_to(common[None], (devices, common.shape[0])),
    ]
    edges = [0]
    for part in parts:
        edges.append(edges[-1] + part.shape[1])
    parts.append(jnp.zeros((devices, -edges[-1] % 128), f32))
    swapped = swap_all(jnp.concatenate(parts, axis=1))
    done = lax.optimization_barrier(
        (swapped, grad_w_gate, grad_w_up, grad_down.astype(f32), output_own, input_grad)
    )
    mixer_own, *done = lax.optimization_barrier((mixer_own, *done))
    swapped, grad_w_gate, grad_w_up, grad_down, output_own, input_grad = done
    mixer_own = exchange(mixer_own.reshape(n_seq, rows, -1))
    order = []
    for head in range(heads):
        spot, from_band = divmod(head, bands)
        from_place, which = divmod(spot, mine)
        order.append((from_band * group + from_place, which))
    mixer_grads = mixer_unpack(mixer_own, tuple(order), head_width)
    grad_output, *mixer_grads = lax.optimization_barrier((grad_output, *mixer_grads))
    grad_output = grad_output.astype(f32)
    sums = jnp.sum(swapped, axis=0)
    gate_sums = jnp.sum(swapped[:, : edges[1]].reshape(n_dp, n_seq, -1), axis=0)
    gate_sums = gate_sums.reshape(bands, group, 2, mine, rows)
    gate_sums = jnp.transpose(gate_sums, (2, 4, 1, 3, 0)).reshape(2, rows, heads)
    gain_sums = sums[edges[1] : edges[2]].reshape(2, rows)
    common = sums[edges[3] : edges[4]]
    return (
        output_own.astype(bf16).reshape(tokens_shape),
        input_grad.reshape(tokens_shape),
        gain_sums[0],
        *mixer_grads[:3],
        sums[edges[2] : edges[3]].reshape(conv_weight.shape),
        gate_sums[0],
        gate_sums[1],
        common[head_width : head_width + heads],
        common[head_width + heads :],
        mixer_grads[3],
        common[:head_width],
        grad_output,
        gain_sums[1],
        grad_w_gate,
        grad_w_up,
        grad_down,
    )


def solution(mesh):
    in_specs = (
        P(None, "dp", "seq", None),
        P(("dp", "seq")),
        P(("dp", "seq"), None),
        P(("dp", "seq"), None),
        P(("dp", "seq"), None),
        P(None, ("dp", "seq")),
        P(("dp", "seq"), None),
        P(("dp", "seq"), None),
        P(),
        P(),
        P(("dp", "seq"), None),
        P(),
        P(("dp", "seq"), None),
        P(("dp", "seq")),
        P(("dp", "seq"), None),
        P(("dp", "seq"), None),
        P(("dp", "seq"), None),
        P(None, "dp", "seq", None),
    )
    out_specs = (
        P(None, "dp", "seq", None),
        P(None, "dp", "seq", None),
        P(("dp", "seq")),
        P(("dp", "seq"), None),
        P(("dp", "seq"), None),
        P(("dp", "seq"), None),
        P(None, ("dp", "seq")),
        P(("dp", "seq"), None),
        P(("dp", "seq"), None),
        P(),
        P(),
        P(("dp", "seq"), None),
        P(),
        P(("dp", "seq"), None),
        P(("dp", "seq")),
        P(("dp", "seq"), None),
        P(("dp", "seq"), None),
        P(("dp", "seq"), None),
    )
    return jax.shard_map(
        on_device, mesh=mesh, in_specs=in_specs, out_specs=out_specs, check_vma=False
    )
```

```python
import functools

import jax
import jax.numpy as jnp
from jax import lax
from jax.experimental import pallas as pl
from jax.experimental.pallas import tpu as pltpu
from jax.sharding import PartitionSpec as P

BLOCK = 64
CONV = 4
MB = 2


eps_norm = 1e-06
highest = lax.Precision.HIGHEST


def rms_scale(values, gain_vec):
    return (
        values * lax.rsqrt(jnp.mean(values * values, axis=-1, keepdims=True) + eps_norm) * gain_vec
    )


def product(left_side, right_side):
    return jnp.dot(left_side, right_side, preferred_element_type=jnp.float32)


def contract_rows(left_side, right_side):
    return lax.dot_general(
        left_side, right_side, (((0,), (0,)), ((), ())), preferred_element_type=jnp.float32
    )


def times_transposed(left_side, right_side):
    return lax.dot_general(
        left_side, right_side, (((1,), (1,)), ((), ())), preferred_element_type=jnp.float32
    )


ALL = ("dp", "seq")


def swap(value, bit):
    count = lax.axis_size("seq")
    return lax.ppermute(value, "seq", [(place, place ^ bit) for place in range(count)])


def seq_offsets():
    count = lax.axis_size("seq")
    half = count // 2
    return [2 * place for place in range(half)] + [2 * place + 1 for place in range(half)]


def gather_seq(value):
    count = lax.axis_size("seq")
    held = {0: value}
    if count == 8:
        half = value.shape[0] // 2
        held[2] = swap(value, 2)
        held[4] = swap(value, 4)
        held[6] = jnp.concatenate(
            [swap(held[2][:half], 4), swap(held[4][half:], 2)], axis=0
        )
    else:
        bit = 2
        while bit < count:
            for offset in list(held):
                held[offset | bit] = swap(held[offset], bit)
            bit *= 2
    for offset in list(held):
        held[offset | 1] = swap(held[offset], 1)
    return jnp.stack([held[offset] for offset in seq_offsets()], axis=0)


def add_low(left_side, right_side):
    return (left_side.astype(jnp.float32) + right_side.astype(jnp.float32)).astype(jnp.bfloat16)


def scatter_seq(parts):
    f32 = jnp.float32
    count = lax.axis_size("seq")
    half = count // 2
    own = add_low(parts[:half], swap(parts[half:], 1))
    if count == 8:
        rows = own.shape[1] // 2
        first, second = own[:, :rows], own[:, rows:]
        first = add_low(first[:2], swap(first[2:], 4))
        second_y = second[0::2]
        second = add_low(second_y, swap(second[1::2], 2))
        first = first[0].astype(f32) + swap(first[1], 2).astype(f32)
        second = second[0].astype(f32) + swap(second[1], 4).astype(f32)
        return jnp.concatenate([first, second], axis=0)
    while half > 1:
        half //= 2
        own = add_low(own[:half], swap(own[half:], 2 * half))
    return own[0].astype(f32)


NN = ((1,), (0,))
NT = ((1,), (1,))
TN = ((0,), (0,))
PAIR = 2


def low_dot(left_side, right_side, dims):
    bf16 = jnp.bfloat16
    return lax.dot_general(
        left_side.astype(bf16),
        right_side.astype(bf16),
        (dims, ((), ())),
        preferred_element_type=jnp.float32,
    )


def two_terms(value):
    bf16 = jnp.bfloat16
    if value.dtype == bf16:
        return [value]
    high = value.astype(bf16)
    return [high, (value - high.astype(jnp.float32)).astype(bf16)]


def wide_dot(left_side, right_side, dims):
    left_terms, right_terms = two_terms(left_side), two_terms(right_side)
    result = low_dot(left_terms[0], right_terms[0], dims)
    for term in right_terms[1:]:
        result = result + low_dot(left_terms[0], term, dims)
    for term in left_terms[1:]:
        result = result + low_dot(term, right_terms[0], dims)
    return result


def rounded(value):
    return value.astype(jnp.bfloat16).astype(jnp.float32)


def softplus(value):
    return jnp.maximum(value, 0.0) + jnp.log1p(jnp.exp(-jnp.abs(value)))


def rows_sum(value):
    return jnp.sum(value, axis=1, keepdims=True)


def stack(pieces):
    return jnp.concatenate(pieces, axis=0)


def half(value, which):
    return value[which * BLOCK : (which + 1) * BLOCK]


def fill_masks(mask_ref, level_ref):
    size = PAIR * BLOCK
    down = lax.broadcasted_iota(jnp.int32, (size, size), 0)
    across = lax.broadcasted_iota(jnp.int32, (size, size), 1)
    apart = down ^ across
    mask_ref[0] = jnp.where((apart < BLOCK) & (down >= across), 1.0, 0.0)
    mask_ref[1] = jnp.where(apart == 0, 1.0, 0.0)
    for level in range(level_ref.shape[0]):
        inside = (apart >= 1 << level) & (apart < 2 << level) & (down > across)
        level_ref[level] = jnp.where(inside, 1.0, 0.0)


def head_pieces(convolved, extras, gate_ref, mine, width):
    chains = []
    for conv_out, extra in zip(convolved, extras):
        active = conv_out * jax.nn.sigmoid(conv_out)
        beta = rounded(jax.nn.sigmoid(extra))
        decay = rounded(-gate_ref[0:1] * softplus(extra + gate_ref[1:2]))
        for head in range(mine):
            part = [
                active[:, (kind * mine + head) * width : (kind * mine + head + 1) * width]
                for kind in range(3)
            ]
            chains.append(
                part + [beta[:, mine + head : mine + head + 1], decay[:, head : head + 1]]
            )
    return chains


def block_values(chains, mask_ref, width):
    raw_query, raw_key, value, beta, decay = [stack(list(pieces)) for pieces in zip(*chains)]
    scale_query = lax.rsqrt(rows_sum(raw_query * raw_query) + eps_norm)
    scale_key = lax.rsqrt(rows_sum(raw_key * raw_key) + eps_norm)
    unit_query, unit_key = raw_query * scale_query, raw_key * scale_key
    query = rounded(unit_query * width ** (-0.5))
    key = rounded(unit_key)
    value = rounded(value)
    within = mask_ref[0]
    cumulative = low_dot(within, jnp.broadcast_to(decay, query.shape), NN)
    along = jnp.transpose(cumulative)[0:1, :]
    fall = within * jnp.exp(within * (cumulative[:, 0:1] - along))
    key_key = low_dot(key, key, NT)
    query_key = low_dot(query, key, NT)
    last = stack(
        [
            jnp.broadcast_to(half(cumulative, which)[BLOCK - 1 :], (BLOCK, width))
            for which in range(PAIR)
        ]
    )
    growth = jnp.exp(cumulative)
    key_fall = jnp.exp(last - cumulative)
    return dict(
        scale_query=scale_query,
        scale_key=scale_key,
        unit_query=unit_query,
        unit_key=unit_key,
        query=query,
        key=key,
        value=value,
        beta=beta,
        fall=fall,
        key_key=key_key,
        query_key=query_key,
        scores=query_key * fall,
        growth=growth,
        key_fall=key_fall,
        key_grown=growth * key,
        query_grown=growth * query,
        key_fallen=key_fall * key,
        totals=jnp.exp(last),
    )


def mixer_forward_body(
    me_ref,
    proj_ref,
    extra_ref,
    conv_ref,
    gate_ref,
    gain_ref,
    mixed_ref,
    conv_out_ref,
    core_ref,
    inverse_ref,
    made_ref,
    written_ref,
    memory_ref,
    rows_ref,
    state_ref,
    mask_ref,
    level_ref,
):
    bf16 = jnp.bfloat16
    sequences = proj_ref.shape[2]
    width = gain_ref.shape[1]
    cols = mixed_ref.shape[4]
    mine = cols // width
    pairs = sequences * mine // PAIR
    taps = conv_ref.shape[0]
    core_bit = jnp.bitwise_and(me_ref[0], 1)

    @pl.when(pl.program_id(0) == 0)
    def _():
        rows_ref[...] = jnp.zeros_like(rows_ref)
        state_ref[...] = jnp.zeros_like(state_ref)
        fill_masks(mask_ref, level_ref)

    blocks = []
    for block in range(2):
        spot = jnp.bitwise_xor(core_bit, block)
        convolved, extras = [], []
        for seq in range(sequences):
            rows_ref[seq, 8:] = rounded(proj_ref[spot, 0, seq, :, : 3 * cols])
            conv_out = conv_ref[0:1] * rows_ref[seq, 9 - taps : 9 - taps + BLOCK]
            for tap in range(1, taps):
                first = 9 - taps + tap
                conv_out = conv_out + conv_ref[tap : tap + 1] * rows_ref[seq, first : first + BLOCK]
            rows_ref[seq, 0:8] = rows_ref[seq, BLOCK : BLOCK + 8]
            conv_out_ref[0, block, seq] = conv_out
            convolved.append(conv_out)
            extras.append(extra_ref[spot, 0, seq])
        chains = head_pieces(convolved, extras, gate_ref, mine, width)
        for pair in range(pairs):
            made = block_values(chains[PAIR * pair : PAIR * (pair + 1)], mask_ref, width)
            made["lower"] = made["beta"] * made["key_key"] * made["fall"]
            made["inverse"] = mask_ref[1] - level_ref[0] * made["lower"]
            blocks.append((block, pair, made))
    for level in range(1, level_ref.shape[0]):
        inner = [
            wide_dot(level_ref[level] * made["lower"], made["inverse"], NN) for _, _, made in blocks
        ]
        for (_, _, made), right_side in zip(blocks, inner):
            made["inverse"] = made["inverse"] - wide_dot(made["inverse"], right_side, NN)
    for block, pair, made in blocks:
        inverse = made["inverse"]
        inverse_ref[0, block, pair] = inverse
        weighted = jnp.concatenate(
            [made["beta"] * made["value"], made["beta"] * made["key_grown"]], axis=1
        )
        made["fresh_carried"] = wide_dot(inverse, weighted, NN)
        made_ref[0, block, pair] = made["fresh_carried"]
    for block, pair, made in blocks:
        fresh, carried = made["fresh_carried"][:, :width], made["fresh_carried"][:, width:]
        written, results = [], []
        for which in range(PAIR):
            chain = PAIR * pair + which
            state = state_ref[chain]
            memory_ref[0, block, chain] = state
            seen = wide_dot(
                stack([half(carried, which), half(made["query_grown"], which)]), state, NN
            )
            new = half(fresh, which) - seen[:BLOCK]
            written.append(new)
            results.append(seen[BLOCK:])
            state_ref[chain] = half(made["totals"], which)[0:1] * state + wide_dot(
                half(made["key_fallen"], which), new, TN
            )
        written = stack(written)
        written_ref[0, block, pair] = written
        core = (stack(results) + wide_dot(made["scores"], written, NN)).astype(bf16)
        core_ref[0, block, pair] = core
        core = core.astype(jnp.float32)
        normed = core * lax.rsqrt(rows_sum(core * core) / width + eps_norm) * gain_ref[0:1]
        spot = jnp.bitwise_xor(core_bit, block)
        for which in range(PAIR):
            seq, head = divmod(PAIR * pair + which, mine)
            span = slice(head * width, (head + 1) * width)
            out_gate = proj_ref[
                spot, 0, seq, :, 3 * cols + head * width : 3 * cols + (head + 1) * width
            ]
            mixed = half(normed, which) * out_gate * jax.nn.sigmoid(out_gate)
            mixed_ref[spot, 0, seq, :, span] = mixed.astype(bf16)


def mixer_backward_body(
    me_ref,
    proj_ref,
    extra_ref,
    grad_mixed_ref,
    conv_out_ref,
    core_ref,
    inverse_ref,
    made_ref,
    written_ref,
    memory_ref,
    conv_ref,
    gate_ref,
    gain_ref,
    grad_proj_ref,
    grad_extra_ref,
    grad_conv_ref,
    grad_small_ref,
    rows_ref,
    state_ref,
    mask_ref,
    level_ref,
):
    f32 = jnp.float32
    bf16 = jnp.bfloat16
    sequences = proj_ref.shape[2]
    width = gain_ref.shape[1]
    cols = grad_mixed_ref.shape[4]
    mine = cols // width
    pairs = sequences * mine // PAIR
    taps = conv_ref.shape[0]
    core_bit = jnp.bitwise_and(me_ref[0], 1)

    @pl.when(pl.program_id(0) == 0)
    def _():
        rows_ref[...] = jnp.zeros_like(rows_ref)
        state_ref[...] = jnp.zeros_like(state_ref)
        grad_conv_ref[...] = jnp.zeros_like(grad_conv_ref)
        grad_small_ref[...] = jnp.zeros_like(grad_small_ref)
        fill_masks(mask_ref, level_ref)

    within = mask_ref[0]
    gain = gain_ref[0:1]
    grad_gain = jnp.zeros((1, width), f32)
    blocks = []
    for block in (1, 0):
        spot = jnp.bitwise_xor(core_bit, block)
        convolved = [conv_out_ref[0, block, seq] for seq in range(sequences)]
        extras = [extra_ref[spot, 0, seq] for seq in range(sequences)]
        chains = head_pieces(convolved, extras, gate_ref, mine, width)
        for pair in range(pairs):
            made = block_values(chains[PAIR * pair : PAIR * (pair + 1)], mask_ref, width)
            core = core_ref[0, block, pair].astype(f32)
            core_scale = lax.rsqrt(rows_sum(core * core) / width + eps_norm)
            normed = core * core_scale
            grad_unit = []
            for which in range(PAIR):
                seq, head = divmod(PAIR * pair + which, mine)
                span = slice(3 * cols + head * width, 3 * cols + (head + 1) * width)
                out_gate = proj_ref[spot, 0, seq, :, span]
                grad_mixed = grad_mixed_ref[
                    spot, 0, seq, :, head * width : (head + 1) * width
                ].astype(f32)
                sigmoid = jax.nn.sigmoid(out_gate)
                silu = out_gate * sigmoid
                scaled = grad_mixed * half(normed, which)
                grad_gate = scaled * gain * (sigmoid + silu * (1.0 - sigmoid))
                grad_proj_ref[spot, 0, seq, :, span] = grad_gate.astype(bf16)
                grad_gain = grad_gain + jnp.sum(scaled * silu, axis=0, keepdims=True)
                grad_unit.append(grad_mixed * gain * silu)
            grad_unit = stack(grad_unit)
            inner = rows_sum(grad_unit * normed) / width
            made["grad_core"] = (core_scale * (grad_unit - normed * inner)).astype(bf16)
            made["from_scores"] = wide_dot(made["scores"], made["grad_core"], TN)
            made["grad_scores"] = (
                wide_dot(made["grad_core"], written_ref[0, block, pair], NT) * made["fall"]
            )
            blocks.append((block, pair, made))
    grad_small_ref[0:1] += grad_gain

    for block, pair, made in blocks:
        carried = made_ref[0, block, pair, :, width:]
        parts = []
        for which in range(PAIR):
            chain = PAIR * pair + which
            state, grad_state = memory_ref[0, block, chain], state_ref[chain]
            grad_out = half(made["grad_core"], which)
            grad_new = half(made["from_scores"], which) + wide_dot(
                half(made["key_fallen"], which), grad_state, NN
            )
            totals = half(made["totals"], which)[0:1]
            state_ref[chain] = (
                totals * grad_state
                + wide_dot(half(made["query_grown"], which), grad_out, TN)
                - wide_dot(half(carried, which), grad_new, TN)
            )
            parts.append(
                (
                    grad_new,
                    wide_dot(grad_out, state, NT),
                    -wide_dot(grad_new, state, NT),
                    wide_dot(half(written_ref[0, block, pair], which), grad_state, NT),
                    rows_sum(jnp.sum(state * grad_state, axis=0, keepdims=True) * totals),
                )
            )
        made["grad_new"], made["grad_query_grown"], made["grad_carried"] = [
            stack([part[index] for part in parts]) for index in range(3)
        ]
        made["grad_key_fallen"] = stack([part[3] for part in parts])
        made["grad_totals"] = [part[4] for part in parts]

    lane = lax.broadcasted_iota(jnp.int32, (BLOCK, extra_ref.shape[4]), 1)
    at_end = lax.broadcasted_iota(jnp.int32, (BLOCK, 1), 0) == BLOCK - 1
    ones = jnp.ones((PAIR * BLOCK, width), bf16)
    results = {}
    for block, pair, made in blocks:
        beta, growth, fall = made["beta"], made["growth"], made["fall"]
        query, key, value = made["query"], made["key"], made["value"]
        fall_strict = fall - mask_ref[1]
        grad_weighted = wide_dot(
            inverse_ref[0, block, pair],
            jnp.concatenate([made["grad_new"], made["grad_carried"]], axis=1),
            TN,
        )
        grad_lower = -wide_dot(grad_weighted, made_ref[0, block, pair], NT) * fall_strict
        grad_key_key = grad_lower * beta
        from_lower = grad_lower * made["key_key"]
        grad_value_part, grad_key_part = grad_weighted[:, :width], grad_weighted[:, width:]
        grad_scores = made["grad_scores"]
        carried_part = grad_key_part * made["key_grown"]
        grad_beta = rows_sum(from_lower) + rows_sum(carried_part + grad_value_part * value)
        shifts = beta * from_lower + grad_scores * made["query_key"]
        fallen_part = made["grad_key_fallen"] * made["key_fallen"]
        fallen = rows_sum(fallen_part)
        grad_cumulative = rows_sum(shifts) + rows_sum(
            made["grad_query_grown"] * made["query_grown"] + beta * carried_part - fallen_part
        )
        ends = stack(
            [
                jnp.where(
                    at_end,
                    jnp.sum(half(fallen, which), axis=0, keepdims=True) + made["grad_totals"][which],
                    0.0,
                )
                for which in range(PAIR)
            ]
        )
        grad_cumulative = grad_cumulative + ends - wide_dot(shifts, ones, TN)
        grad_decay = rounded(wide_dot(within.astype(bf16), grad_cumulative, TN))
        both = stack([grad_scores, grad_key_key])
        down = wide_dot(both, key.astype(bf16), NN)
        grad_query = growth * made["grad_query_grown"] + down[: PAIR * BLOCK]
        grad_key = (
            made["key_fall"] * made["grad_key_fallen"]
            + beta * growth * grad_key_part
            + down[PAIR * BLOCK :]
            + wide_dot(both, stack([query, key]).astype(bf16), TN)
        )
        grad_query = rounded(grad_query) * width ** (-0.5)
        grad_key = rounded(grad_key)
        grad_value = rounded(beta * grad_value_part)
        grad_beta = rounded(grad_beta)
        unit_query, unit_key = made["unit_query"], made["unit_key"]
        grad_query = made["scale_query"] * (
            grad_query - unit_query * rows_sum(grad_query * unit_query)
        )
        grad_key = made["scale_key"] * (grad_key - unit_key * rows_sum(grad_key * unit_key))
        for which in range(PAIR):
            results[block, PAIR * pair + which] = [
                half(part, which)
                for part in (grad_query, grad_key, grad_value, grad_decay, grad_beta)
            ]

    for block in (1, 0):
        spot = jnp.bitwise_xor(core_bit, block)
        for seq in range(sequences):
            conv_out = conv_out_ref[0, block, seq]
            sigmoid = jax.nn.sigmoid(conv_out)
            chains = [results[block, seq * mine + head] for head in range(mine)]
            grad_active = jnp.concatenate(
                [chain[kind] for kind in range(3) for chain in chains], axis=1
            )
            rows_ref[seq, :BLOCK] = grad_active * sigmoid * (1.0 + conv_out * (1.0 - sigmoid))
            pre = rounded(proj_ref[spot, 0, seq, :, : 3 * cols])
            grad_pre = jnp.zeros_like(conv_out)
            for tap in range(taps):
                shifted = rows_ref[seq, taps - 1 - tap : taps - 1 - tap + BLOCK]
                grad_pre = grad_pre + conv_ref[tap : tap + 1] * shifted
                grad_conv_ref[tap : tap + 1] += jnp.sum(pre * shifted, axis=0, keepdims=True)
            grad_proj_ref[spot, 0, seq, :, : 3 * cols] = grad_pre.astype(bf16)
            rows_ref[seq, BLOCK:] = rows_ref[seq, 0:8]
            extra = extra_ref[spot, 0, seq]
            moved = extra + gate_ref[1:2]
            spread_decay = jnp.zeros_like(extra)
            spread_beta = jnp.zeros_like(extra)
            for head, chain in enumerate(chains):
                spread_decay = jnp.where(lane == head, chain[3][:, 0:1], spread_decay)
                spread_beta = jnp.where(lane == mine + head, chain[4], spread_beta)
            grad_alpha = -gate_ref[0:1] * spread_decay * jax.nn.sigmoid(moved)
            squash = jax.nn.sigmoid(extra)
            grad_extra = grad_alpha + spread_beta * squash * (1.0 - squash)
            grad_extra_ref[spot, 0, seq] = grad_extra.astype(bf16)
            grad_small_ref[1:2] -= jnp.sum(spread_decay * softplus(moved), axis=0, keepdims=True)
            grad_small_ref[2:3] += jnp.sum(grad_alpha, axis=0, keepdims=True)


def ff_pack_body(width, gate_ref, up_ref, out_ref):
    count = out_ref.shape[0]
    blocks = gate_ref.shape[1] // (count * width)
    for spot in range(count):
        pieces = [
            ref[:, (block * count + spot) * width : (block * count + spot + 1) * width]
            for ref in (gate_ref, up_ref)
            for block in range(blocks)
        ]
        out_ref[spot] = jnp.concatenate(pieces, axis=1)


def ff_pack(gate, up, count, width):
    rows, hidden = gate.shape
    return pl.pallas_call(
        functools.partial(ff_pack_body, width),
        out_shape=jax.ShapeDtypeStruct((count, rows, 2 * hidden // count), gate.dtype),
    )(gate, up)


def ff_unpack_body(width, in_ref, gate_ref, up_ref):
    count = in_ref.shape[0]
    blocks = gate_ref.shape[1] // (count * width)
    for which, ref in enumerate((gate_ref, up_ref)):
        pieces = []
        for block in range(blocks):
            first = (which * blocks + block) * width
            pieces += [in_ref[spot, :, first : first + width] for spot in range(count)]
        ref[...] = jnp.concatenate([piece.astype(jnp.float32) for piece in pieces], axis=1)


def ff_unpack(packed, width):
    count, rows, columns = packed.shape
    shape = jax.ShapeDtypeStruct((rows, count * columns // 2), jnp.float32)
    return pl.pallas_call(functools.partial(ff_unpack_body, width), out_shape=[shape, shape])(packed)


def mixer_unpack_body(order, in_ref, *out_refs):
    width = out_refs[0].shape[1] // len(order)
    columns = in_ref.shape[2] // len(out_refs)
    for which, ref in enumerate(out_refs):
        for head, (spot, place) in enumerate(order):
            first = which * columns + place * width
            piece = in_ref[spot, :, first : first + width].astype(jnp.float32)
            ref[:, head * width : (head + 1) * width] = piece


def mixer_unpack(packed, order, head_width):
    shape = jax.ShapeDtypeStruct((packed.shape[1], len(order) * head_width), jnp.float32)
    return pl.pallas_call(functools.partial(mixer_unpack_body, order), out_shape=[shape] * 4)(packed)


def whole_spec(shape):
    return pl.BlockSpec(shape, lambda step, me: (0,) * len(shape))


def mixer_specs(projected, head_width, mine, forward):
    _, steps, sequences, span, _ = projected.shape
    chains = sequences * mine
    pairs = chains // PAIR
    cols = mine * head_width

    def step_of(step):
        return step if forward else steps - 1 - step

    def gathered(channels):
        return pl.BlockSpec(
            (2, 1, sequences, span, channels),
            lambda step, me: (
                0,
                jnp.bitwise_xor(jnp.right_shift(me[0], 1), step_of(step)),
                0,
                0,
                0,
            ),
        )

    def ordered(*shape):
        return pl.BlockSpec((1,) + shape, lambda step, me: (step_of(step),) + (0,) * len(shape))

    size = PAIR * span
    kept = [
        (jax.ShapeDtypeStruct((steps,) + shape, kind), ordered(*shape))
        for shape, kind in [
            ((2, sequences, span, 3 * cols), jnp.float32),
            ((2, pairs, size, head_width), jnp.bfloat16),
            ((2, pairs, size, size), jnp.float32),
            ((2, pairs, size, 2 * head_width), jnp.float32),
            ((2, pairs, size, head_width), jnp.float32),
            ((2, chains, head_width, head_width), jnp.float32),
        ]
    ]
    scratch = [
        pltpu.VMEM((sequences, span + 8, 3 * cols), jnp.float32),
        pltpu.VMEM((chains, head_width, head_width), jnp.float32),
        pltpu.VMEM((2, size, size), jnp.float32),
        pltpu.VMEM((int(BLOCK).bit_length() - 1, size, size), jnp.float32),
    ]
    cost = pl.CostEstimate(
        flops=4 * steps * pairs * size**3 * 18,
        bytes_accessed=12 << 20,
        transcendentals=2 * steps << 18,
    )
    return gathered, kept, scratch, cost


def mixer_forward(me, projected, extra, conv_mine, gate_rows, gain_row, mine):
    channels = projected.shape[-1]
    head_width = gain_row.shape[1]
    gathered, kept, scratch, cost = mixer_specs(projected, head_width, mine, True)
    cols = mine * head_width
    return pl.pallas_call(
        mixer_forward_body,
        grid_spec=pltpu.PrefetchScalarGridSpec(
            num_scalar_prefetch=1,
            grid=(projected.shape[1],),
            in_specs=[
                gathered(channels),
                gathered(extra.shape[-1]),
                whole_spec(conv_mine.shape),
                whole_spec(gate_rows.shape),
                whole_spec(gain_row.shape),
            ],
            out_specs=[gathered(cols)] + [spec for _, spec in kept],
            scratch_shapes=scratch,
        ),
        out_shape=[jax.ShapeDtypeStruct(projected.shape[:-1] + (cols,), jnp.bfloat16)]
        + [shape for shape, _ in kept],
        compiler_params=pltpu.CompilerParams(vmem_limit_bytes=40 << 20),
        cost_estimate=cost,
    )(me, projected, extra, conv_mine, gate_rows, gain_row)


def mixer_backward(
    me, projected, extra, grad_mixed, kept_values, conv_mine, gate_rows, gain_row, mine
):
    channels = projected.shape[-1]
    head_width = gain_row.shape[1]
    gathered, kept, scratch, cost = mixer_specs(projected, head_width, mine, False)
    cols = mine * head_width
    return pl.pallas_call(
        mixer_backward_body,
        grid_spec=pltpu.PrefetchScalarGridSpec(
            num_scalar_prefetch=1,
            grid=(projected.shape[1],),
            in_specs=[gathered(channels), gathered(extra.shape[-1]), gathered(cols)]
            + [spec for _, spec in kept]
            + [
                whole_spec(conv_mine.shape),
                whole_spec(gate_rows.shape),
                whole_spec(gain_row.shape),
            ],
            out_specs=[
                gathered(channels),
                gathered(extra.shape[-1]),
                whole_spec(conv_mine.shape),
                whole_spec((8, head_width)),
            ],
            scratch_shapes=scratch,
        ),
        out_shape=[
            jax.ShapeDtypeStruct(projected.shape, jnp.bfloat16),
            jax.ShapeDtypeStruct(extra.shape, jnp.bfloat16),
            jax.ShapeDtypeStruct(conv_mine.shape, jnp.float32),
            jax.ShapeDtypeStruct((8, head_width), jnp.float32),
        ],
        compiler_params=pltpu.CompilerParams(vmem_limit_bytes=40 << 20),
        cost_estimate=cost,
    )(me, projected, extra, grad_mixed, *kept_values, conv_mine, gate_rows, gain_row)


def after(value, *others):
    return lax.optimization_barrier((value,) + others)[0]


def shift_dp(value, step, sources):
    return lax.ppermute(value, "dp", [(place, place + step) for place in sources])


def line_gather(block, ties):
    count = lax.axis_size("dp")
    me = lax.axis_index("dp")
    ups, downs = [block], [block]
    for step in range(1, count):
        if step <= len(ties):
            ups[-1], downs[-1] = lax.optimization_barrier((ups[-1], downs[-1], ties[step - 1]))[:2]
        ups.append(shift_dp(ups[-1], 1, range(step - 1, count - 1)))
        downs.append(shift_dp(downs[-1], -1, range(1, count - step + 1)))
    result = jnp.zeros((count,) + block.shape, block.dtype)
    for step in range(count):
        piece = block if step == 0 else ups[step] + downs[count - step]
        result = lax.dynamic_update_index_in_dim(result, piece, (me - step) % count, 0)
    return result


def on_device(
    inputs,
    norm_attn,
    w_query,
    w_key,
    w_value,
    conv_weight,
    w_alpha,
    w_beta,
    decay_rate,
    decay_bias,
    w_outgate,
    head_gain,
    w_output,
    norm_mlp,
    w_gate,
    w_up,
    w_down,
    cotangent,
):
    f32 = jnp.float32
    bf16 = jnp.bfloat16
    n_dp = lax.axis_size("dp")
    n_seq = lax.axis_size("seq")
    devices = n_dp * n_seq
    me = lax.axis_index("seq")
    rows, width = w_query.shape
    heads = w_alpha.shape[1]
    head_width = head_gain.shape[0]
    mine = heads // n_seq
    cols = mine * head_width
    group = head_width // rows
    bands = n_seq // group
    band, place = me // group, me % group
    hidden = w_gate.shape[1]
    ff_rows = w_down.shape[0]
    ff = n_dp * ff_rows
    taps = conv_weight.shape[0]
    tokens_shape = inputs.shape
    span = inputs.shape[2]
    count = inputs.shape[0] * inputs.shape[1]
    total = n_seq * count * span

    def by_device(weight):
        split = weight.reshape(weight.shape[0], group, mine, bands, -1)
        return jnp.transpose(split, (3, 1, 0, 2, 4)).reshape(n_seq, weight.shape[0], -1)

    def by_columns(blocks):
        pieces = []
        for head in range(heads):
            spot, from_band = divmod(head, bands)
            from_place, which = divmod(spot, mine)
            block = blocks[from_band * group + from_place]
            pieces.append(block[:, which * head_width : (which + 1) * head_width])
        return jnp.concatenate(pieces, axis=1).astype(f32)

    def swap_all(blocks):
        return lax.all_to_all(blocks, ALL, split_axis=0, concat_axis=0, tiled=True)

    packed = jnp.concatenate([by_device(w) for w in (w_query, w_key, w_value, w_outgate)], axis=2)

    def exchange(blocks):
        return lax.all_to_all(blocks, "seq", split_axis=0, concat_axis=0, tiled=True)

    def gather_dp(block):
        return lax.all_gather(block, "dp", axis=0, tiled=True)

    sent = exchange(packed)
    mixer_full = gather_dp(sent.reshape(n_seq * rows, -1))
    shared = jnp.concatenate(
        [
            w_alpha.T.reshape(-1),
            w_beta.T.reshape(-1),
            norm_attn,
            norm_mlp,
            conv_weight.reshape(-1),
        ]
    )
    shared, w_gate, w_up, sent = lax.optimization_barrier((shared, w_gate, w_up, sent))
    shared = swap_all(jnp.broadcast_to(shared[None], (devices, shared.shape[0])))

    groups = [list(range(first, first + group)) for first in range(0, n_seq, group)]

    def exchange_group(blocks):
        if group == 2:
            away = swap(lax.dynamic_index_in_dim(blocks, 1 - place, 0, keepdims=False), 1)
            stay = lax.dynamic_index_in_dim(blocks, place, 0, keepdims=False)
            low = place == 0
            return jnp.stack([jnp.where(low, stay, away), jnp.where(low, away, stay)], axis=0)
        return lax.all_to_all(
            blocks, "seq", split_axis=0, concat_axis=0, tiled=True, axis_index_groups=groups
        )

    def to_heads(pieces):
        split = exchange_group(pieces.reshape(group, mine * rows, width))
        split = split.reshape(group, mine, rows, width)
        return jnp.transpose(split, (1, 0, 2, 3)).reshape(cols, width)

    def from_heads(full):
        split = jnp.transpose(full.reshape(mine, group, rows, width), (1, 0, 2, 3))
        return exchange_group(split.reshape(group, mine * rows, width))

    output_full = to_heads(gather_dp(w_output))

    gate_up_sent = exchange(ff_pack(w_gate, w_up, n_seq, ff_rows)).reshape(n_seq * rows, -1)
    gate_up_full = gather_dp(gate_up_sent)
    most = ff_rows - min(64, ff_rows // 2)
    down_rest = gather_dp(w_down[most:]).reshape(n_dp, ff_rows - most, width)
    mixer_full, shared, output_full = lax.optimization_barrier((mixer_full, shared, output_full))

    x_own = inputs.reshape(count * span, width)
    x_all = gather_seq(x_own).reshape(total, width)
    seed_own = cotangent.reshape(count * span, width)
    seed_all = gather_seq(seed_own).reshape(total, width)

    gates = shared[:, : 2 * heads * rows].reshape(devices, 2 * heads, rows)
    gates = jnp.transpose(gates, (1, 0, 2)).reshape(2, group, mine, bands, width)
    gates = lax.dynamic_index_in_dim(gates, band, 3, keepdims=False)
    gates = lax.dynamic_index_in_dim(gates, place, 1, keepdims=False).reshape(2 * mine, width)
    gates = jnp.pad(gates, ((0, 128 - 2 * mine), (0, 0)))
    first = 2 * heads * rows
    gain_attn = shared[:, first : first + rows].reshape(-1).astype(f32)
    gain_mlp = shared[:, first + rows : first + 2 * rows].reshape(-1).astype(f32)
    conv_all = shared[:, first + 2 * rows :].reshape(devices, taps, -1)
    conv_all = jnp.transpose(conv_all, (1, 0, 2)).reshape(taps, 3, group, mine, bands, head_width)
    conv_mine = lax.dynamic_index_in_dim(conv_all, band, 4, keepdims=False)
    conv_mine = lax.dynamic_index_in_dim(conv_mine, place, 2, keepdims=False)
    conv_mine = conv_mine.reshape(taps, 3 * cols).astype(f32)

    def my_heads(vector):
        split = lax.dynamic_index_in_dim(vector.reshape(group, mine, bands), band, 2, False)
        return lax.dynamic_index_in_dim(split, place, 0, keepdims=False)

    rate_mine = my_heads(decay_rate)
    bias_mine = my_heads(decay_bias)

    hidden_in = rms_scale(x_all.astype(f32), gain_attn).astype(bf16)
    projected = product(hidden_in, mixer_full)
    extra = times_transposed(hidden_in, gates).reshape(2, n_seq // 2, count, span, -1)

    projected = projected.reshape(2, n_seq // 2, count, span, -1)
    me_row = me.astype(jnp.int32).reshape(1)
    gate_rows = jnp.zeros((2, gates.shape[0]), f32)
    gate_rows = gate_rows.at[0, :mine].set(rate_mine).at[1, :mine].set(bias_mine)
    gain_row = head_gain.reshape(1, head_width)
    mixed, *kept_values = mixer_forward(
        me_row, projected, extra, conv_mine, gate_rows, gain_row, mine
    )
    mixed = mixed.reshape(total, cols)

    def shares(value):
        return value.astype(bf16).reshape(n_seq, count * span, -1)

    residual = x_own.astype(f32) + scatter_seq(shares(product(mixed, output_full)))
    normed_mid, pull_mid = jax.vjp(rms_scale, residual, gain_mlp)
    hidden_mid = gather_seq(normed_mid.astype(bf16)).reshape(total, width)
    down_most = line_gather(w_down[:most], (mixer_full, residual, hidden_mid))
    gate_up = product(hidden_mid, gate_up_full)
    gate_pre, up_proj = gate_up[:, :ff], gate_up[:, ff:]
    sigmoid_gate = jax.nn.sigmoid(gate_pre)
    silu_gate = gate_pre * sigmoid_gate
    activ = (silu_gate * up_proj).astype(bf16)
    down_grads = contract_rows(activ, seed_all).astype(bf16)
    down_rest = after(down_rest, down_grads)
    down_full = jnp.concatenate([down_most, down_rest], axis=1).reshape(ff, width)
    from_down = times_transposed(seed_all, down_full)
    grad_gate = from_down * up_proj * sigmoid_gate * (1.0 + gate_pre * (1.0 - sigmoid_gate))
    grad_gate_up = jnp.concatenate([grad_gate, from_down * silu_gate], axis=1).astype(bf16)
    back_mid = scatter_seq(shares(times_transposed(grad_gate_up, gate_up_full)))
    grad_res_norm, grad_gain_mlp = pull_mid(back_mid)
    grad_res = seed_own.astype(f32) + grad_res_norm

    def scatter_dp(value):
        return lax.psum_scatter(value.astype(bf16), "dp", scatter_dimension=0, tiled=True)

    grad_down = scatter_dp(down_grads)
    grad_gate_up_own = scatter_dp(contract_rows(hidden_mid, grad_gate_up))

    grad_mixer_out = gather_seq(grad_res.astype(bf16)).reshape(total, width)
    grad_mixed = times_transposed(grad_mixer_out, output_full).astype(bf16)
    grad_projected, grad_extra, grad_conv, grad_small = mixer_backward(
        me_row,
        projected,
        extra,
        grad_mixed.reshape(2, n_seq // 2, count, span, cols),
        kept_values,
        conv_mine,
        gate_rows,
        gain_row,
        mine,
    )
    grad_projected = grad_projected.reshape(total, -1)
    grad_extra = grad_extra.reshape(total, -1)
    grad_head_gain = grad_small[0]
    grad_rate, grad_bias = grad_small[1, :mine], grad_small[2, :mine]
    grad_output = from_heads(contract_rows(mixed, grad_mixer_out).astype(bf16))
    weight_grads = contract_rows(hidden_in, grad_projected).astype(bf16)
    weight_grads, grad_projected, grad_extra, activ = lax.optimization_barrier(
        (weight_grads, grad_projected, grad_extra, activ)
    )
    mixer_own = scatter_dp(weight_grads)
    back_in = times_transposed(grad_projected, mixer_full) + product(grad_extra, gates)
    grad_output, back_in = lax.optimization_barrier((grad_output, back_in))
    grad_output = scatter_dp(grad_output.reshape(n_dp * rows, width))
    back_in = scatter_seq(shares(back_in))
    grad_gate_up_own = exchange(grad_gate_up_own.reshape(n_seq, rows, -1))
    output_own = residual + scatter_seq(shares(product(activ, down_full)))
    grad_w_gate, grad_w_up = ff_unpack(grad_gate_up_own, ff_rows)
    back_in, grad_w_gate, grad_w_up = lax.optimization_barrier((back_in, grad_w_gate, grad_w_up))
    tokens = x_own.astype(f32)
    _, pull_in = jax.vjp(rms_scale, tokens, gain_attn)
    grad_tok_norm, grad_gain_attn = pull_in(back_in)
    input_grad = grad_res + grad_tok_norm

    conv_grad = jnp.zeros((taps, 3, group, mine, bands, head_width), f32)
    conv_grad = lax.dynamic_update_slice(
        conv_grad,
        grad_conv.reshape(taps, 3, 1, mine, 1, head_width),
        (0, 0, place, 0, band, 0),
    )
    conv_grad = jnp.transpose(conv_grad.reshape(taps, devices, -1), (1, 0, 2))
    gate_grad = contract_rows(grad_extra, hidden_in)[: 2 * mine]
    def place_heads(vector):
        slots = jnp.zeros((group, mine, bands), f32)
        return lax.dynamic_update_slice(
            slots, vector.reshape(1, mine, 1), (place, 0, band)
        ).reshape(heads)

    def by_owner(values):
        split = values.reshape(-1, devices, rows)
        return jnp.transpose(split, (1, 0, 2)).reshape(devices, -1)

    common = jnp.concatenate([grad_head_gain, place_heads(grad_rate), place_heads(grad_bias)])
    parts = [
        by_owner(gate_grad),
        by_owner(jnp.stack([grad_gain_attn, grad_gain_mlp])),
        conv_grad.reshape(devices, -1),
        jnp.broadcast_to(common[None], (devices, common.shape[0])),
    ]
    edges = [0]
    for part in parts:
        edges.append(edges[-1] + part.shape[1])
    parts.append(jnp.zeros((devices, -edges[-1] % 128), f32))
    swapped = swap_all(jnp.concatenate(parts, axis=1))
    done = lax.optimization_barrier(
        (swapped, grad_w_gate, grad_w_up, grad_down.astype(f32), output_own, input_grad)
    )
    mixer_own, *done = lax.optimization_barrier((mixer_own, *done))
    swapped, grad_w_gate, grad_w_up, grad_down, output_own, input_grad = done
    mixer_own = exchange(mixer_own.reshape(n_seq, rows, -1))
    order = []
    for head in range(heads):
        spot, from_band = divmod(head, bands)
        from_place, which = divmod(spot, mine)
        order.append((from_band * group + from_place, which))
    mixer_grads = mixer_unpack(mixer_own, tuple(order), head_width)
    grad_output, *mixer_grads = lax.optimization_barrier((grad_output, *mixer_grads))
    grad_output = grad_output.astype(f32)
    sums = jnp.sum(swapped, axis=0)
    gate_sums = jnp.sum(swapped[:, : edges[1]].reshape(n_dp, n_seq, -1), axis=0)
    gate_sums = gate_sums.reshape(bands, group, 2, mine, rows)
    gate_sums = jnp.transpose(gate_sums, (2, 4, 1, 3, 0)).reshape(2, rows, heads)
    gain_sums = sums[edges[1] : edges[2]].reshape(2, rows)
    common = sums[edges[3] : edges[4]]
    return (
        output_own.astype(bf16).reshape(tokens_shape),
        input_grad.reshape(tokens_shape),
        gain_sums[0],
        *mixer_grads[:3],
        sums[edges[2] : edges[3]].reshape(conv_weight.shape),
        gate_sums[0],
        gate_sums[1],
        common[head_width : head_width + heads],
        common[head_width + heads :],
        mixer_grads[3],
        common[:head_width],
        grad_output,
        gain_sums[1],
        grad_w_gate,
        grad_w_up,
        grad_down,
    )


def solution(mesh):
    in_specs = (
        P(None, "dp", "seq", None),
        P(("dp", "seq")),
        P(("dp", "seq"), None),
        P(("dp", "seq"), None),
        P(("dp", "seq"), None),
        P(None, ("dp", "seq")),
        P(("dp", "seq"), None),
        P(("dp", "seq"), None),
        P(),
        P(),
        P(("dp", "seq"), None),
        P(),
        P(("dp", "seq"), None),
        P(("dp", "seq")),
        P(("dp", "seq"), None),
        P(("dp", "seq"), None),
        P(("dp", "seq"), None),
        P(None, "dp", "seq", None),
    )
    out_specs = (
        P(None, "dp", "seq", None),
        P(None, "dp", "seq", None),
        P(("dp", "seq")),
        P(("dp", "seq"), None),
        P(("dp", "seq"), None),
        P(("dp", "seq"), None),
        P(None, ("dp", "seq")),
        P(("dp", "seq"), None),
        P(("dp", "seq"), None),
        P(),
        P(),
        P(("dp", "seq"), None),
        P(),
        P(("dp", "seq"), None),
        P(("dp", "seq")),
        P(("dp", "seq"), None),
        P(("dp", "seq"), None),
        P(("dp", "seq"), None),
    )
    return jax.shard_map(
        on_device, mesh=mesh, in_specs=in_specs, out_specs=out_specs, check_vma=False
    )
```

```python
import functools

import jax
import jax.numpy as jnp
from jax import lax
from jax.experimental import pallas as pl
from jax.experimental.pallas import tpu as pltpu
from jax.sharding import PartitionSpec as P

BLOCK = 64
CONV = 4
MB = 2


eps_norm = 1e-06
highest = lax.Precision.HIGHEST


def rms_scale(values, gain_vec):
    return (
        values * lax.rsqrt(jnp.mean(values * values, axis=-1, keepdims=True) + eps_norm) * gain_vec
    )


def product(left_side, right_side):
    return jnp.dot(left_side, right_side, preferred_element_type=jnp.float32)


def contract_rows(left_side, right_side):
    return lax.dot_general(
        left_side, right_side, (((0,), (0,)), ((), ())), preferred_element_type=jnp.float32
    )


def times_transposed(left_side, right_side):
    return lax.dot_general(
        left_side, right_side, (((1,), (1,)), ((), ())), preferred_element_type=jnp.float32
    )


ALL = ("dp", "seq")


def swap(value, bit):
    count = lax.axis_size("seq")
    return lax.ppermute(value, "seq", [(place, place ^ bit) for place in range(count)])


def seq_offsets():
    count = lax.axis_size("seq")
    half = count // 2
    return [2 * place for place in range(half)] + [2 * place + 1 for place in range(half)]


def gather_seq(value):
    count = lax.axis_size("seq")
    held = {0: value}
    if count == 8:
        half = value.shape[0] // 2
        held[2] = swap(value, 2)
        held[4] = swap(value, 4)
        held[6] = jnp.concatenate(
            [swap(held[2][:half], 4), swap(held[4][half:], 2)], axis=0
        )
    else:
        bit = 2
        while bit < count:
            for offset in list(held):
                held[offset | bit] = swap(held[offset], bit)
            bit *= 2
    for offset in list(held):
        held[offset | 1] = swap(held[offset], 1)
    return jnp.stack([held[offset] for offset in seq_offsets()], axis=0)


def add_low(left_side, right_side):
    return (left_side.astype(jnp.float32) + right_side.astype(jnp.float32)).astype(jnp.bfloat16)


def scatter_seq(parts):
    f32 = jnp.float32
    count = lax.axis_size("seq")
    half = count // 2
    own = add_low(parts[:half], swap(parts[half:], 1))
    if count == 8:
        rows = own.shape[1] // 2
        first, second = own[:, :rows], own[:, rows:]
        first = add_low(first[:2], swap(first[2:], 4))
        second_y = second[0::2]
        second = add_low(second_y, swap(second[1::2], 2))
        first = first[0].astype(f32) + swap(first[1], 2).astype(f32)
        second = second[0].astype(f32) + swap(second[1], 4).astype(f32)
        return jnp.concatenate([first, second], axis=0)
    while half > 1:
        half //= 2
        own = add_low(own[:half], swap(own[half:], 2 * half))
    return own[0].astype(f32)


NN = ((1,), (0,))
NT = ((1,), (1,))
TN = ((0,), (0,))
PAIR = 2


def low_dot(left_side, right_side, dims):
    bf16 = jnp.bfloat16
    return lax.dot_general(
        left_side.astype(bf16),
        right_side.astype(bf16),
        (dims, ((), ())),
        preferred_element_type=jnp.float32,
    )


def two_terms(value):
    bf16 = jnp.bfloat16
    if value.dtype == bf16:
        return [value]
    high = value.astype(bf16)
    return [high, (value - high.astype(jnp.float32)).astype(bf16)]


def wide_dot(left_side, right_side, dims):
    left_terms, right_terms = two_terms(left_side), two_terms(right_side)
    result = low_dot(left_terms[0], right_terms[0], dims)
    for term in right_terms[1:]:
        result = result + low_dot(left_terms[0], term, dims)
    for term in left_terms[1:]:
        result = result + low_dot(term, right_terms[0], dims)
    return result


def rounded(value):
    return value.astype(jnp.bfloat16).astype(jnp.float32)


def softplus(value):
    return jnp.maximum(value, 0.0) + jnp.log1p(jnp.exp(-jnp.abs(value)))


def rows_sum(value):
    return jnp.sum(value, axis=1, keepdims=True)


def stack(pieces):
    return jnp.concatenate(pieces, axis=0)


def half(value, which):
    return value[which * BLOCK : (which + 1) * BLOCK]


def fill_masks(mask_ref, level_ref):
    size = PAIR * BLOCK
    down = lax.broadcasted_iota(jnp.int32, (size, size), 0)
    across = lax.broadcasted_iota(jnp.int32, (size, size), 1)
    apart = down ^ across
    mask_ref[0] = jnp.where((apart < BLOCK) & (down >= across), 1.0, 0.0)
    mask_ref[1] = jnp.where(apart == 0, 1.0, 0.0)
    for level in range(level_ref.shape[0]):
        inside = (apart >= 1 << level) & (apart < 2 << level) & (down > across)
        level_ref[level] = jnp.where(inside, 1.0, 0.0)


def head_pieces(convolved, extras, gate_ref, mine, width):
    chains = []
    for conv_out, extra in zip(convolved, extras):
        active = conv_out * jax.nn.sigmoid(conv_out)
        beta = rounded(jax.nn.sigmoid(extra))
        decay = rounded(-gate_ref[0:1] * softplus(extra + gate_ref[1:2]))
        for head in range(mine):
            part = [
                active[:, (kind * mine + head) * width : (kind * mine + head + 1) * width]
                for kind in range(3)
            ]
            chains.append(
                part + [beta[:, mine + head : mine + head + 1], decay[:, head : head + 1]]
            )
    return chains


def block_values(chains, mask_ref, width):
    raw_query, raw_key, value, beta, decay = [stack(list(pieces)) for pieces in zip(*chains)]
    scale_query = lax.rsqrt(rows_sum(raw_query * raw_query) + eps_norm)
    scale_key = lax.rsqrt(rows_sum(raw_key * raw_key) + eps_norm)
    unit_query, unit_key = raw_query * scale_query, raw_key * scale_key
    query = rounded(unit_query * width ** (-0.5))
    key = rounded(unit_key)
    value = rounded(value)
    within = mask_ref[0]
    cumulative = low_dot(within, jnp.broadcast_to(decay, query.shape), NN)
    along = jnp.transpose(cumulative)[0:1, :]
    fall = within * jnp.exp(within * (cumulative[:, 0:1] - along))
    key_key = low_dot(key, key, NT)
    query_key = low_dot(query, key, NT)
    last = stack(
        [
            jnp.broadcast_to(half(cumulative, which)[BLOCK - 1 :], (BLOCK, width))
            for which in range(PAIR)
        ]
    )
    growth = jnp.exp(cumulative)
    key_fall = jnp.exp(last - cumulative)
    return dict(
        scale_query=scale_query,
        scale_key=scale_key,
        unit_query=unit_query,
        unit_key=unit_key,
        query=query,
        key=key,
        value=value,
        beta=beta,
        fall=fall,
        key_key=key_key,
        query_key=query_key,
        scores=query_key * fall,
        growth=growth,
        key_fall=key_fall,
        key_grown=growth * key,
        query_grown=growth * query,
        key_fallen=key_fall * key,
        totals=jnp.exp(last),
    )


def mixer_forward_body(
    me_ref,
    proj_ref,
    extra_ref,
    conv_ref,
    gate_ref,
    gain_ref,
    mixed_ref,
    conv_out_ref,
    core_ref,
    inverse_ref,
    made_ref,
    written_ref,
    memory_ref,
    rows_ref,
    state_ref,
    mask_ref,
    level_ref,
):
    bf16 = jnp.bfloat16
    sequences = proj_ref.shape[2]
    width = gain_ref.shape[1]
    cols = mixed_ref.shape[4]
    mine = cols // width
    pairs = sequences * mine // PAIR
    taps = conv_ref.shape[0]
    core_bit = jnp.bitwise_and(me_ref[0], 1)

    @pl.when(pl.program_id(0) == 0)
    def _():
        rows_ref[...] = jnp.zeros_like(rows_ref)
        state_ref[...] = jnp.zeros_like(state_ref)
        fill_masks(mask_ref, level_ref)

    blocks = []
    for block in range(2):
        spot = jnp.bitwise_xor(core_bit, block)
        convolved, extras = [], []
        for seq in range(sequences):
            rows_ref[seq, 8:] = rounded(proj_ref[spot, 0, seq, :, : 3 * cols])
            conv_out = conv_ref[0:1] * rows_ref[seq, 9 - taps : 9 - taps + BLOCK]
            for tap in range(1, taps):
                first = 9 - taps + tap
                conv_out = conv_out + conv_ref[tap : tap + 1] * rows_ref[seq, first : first + BLOCK]
            rows_ref[seq, 0:8] = rows_ref[seq, BLOCK : BLOCK + 8]
            conv_out_ref[0, block, seq] = conv_out
            convolved.append(conv_out)
            extras.append(extra_ref[spot, 0, seq])
        chains = head_pieces(convolved, extras, gate_ref, mine, width)
        for pair in range(pairs):
            made = block_values(chains[PAIR * pair : PAIR * (pair + 1)], mask_ref, width)
            made["lower"] = made["beta"] * made["key_key"] * made["fall"]
            made["inverse"] = mask_ref[1] - level_ref[0] * made["lower"]
            blocks.append((block, pair, made))
    for level in range(1, level_ref.shape[0]):
        inner = [
            wide_dot(level_ref[level] * made["lower"], made["inverse"], NN) for _, _, made in blocks
        ]
        for (_, _, made), right_side in zip(blocks, inner):
            made["inverse"] = made["inverse"] - wide_dot(made["inverse"], right_side, NN)
    for block, pair, made in blocks:
        inverse = made["inverse"]
        inverse_ref[0, block, pair] = inverse
        weighted = jnp.concatenate(
            [made["beta"] * made["value"], made["beta"] * made["key_grown"]], axis=1
        )
        made["fresh_carried"] = wide_dot(inverse, weighted, NN)
        made_ref[0, block, pair] = made["fresh_carried"]
    for block, pair, made in blocks:
        fresh, carried = made["fresh_carried"][:, :width], made["fresh_carried"][:, width:]
        written, results = [], []
        for which in range(PAIR):
            chain = PAIR * pair + which
            state = state_ref[chain]
            memory_ref[0, block, chain] = state
            seen = wide_dot(
                stack([half(carried, which), half(made["query_grown"], which)]), state, NN
            )
            new = half(fresh, which) - seen[:BLOCK]
            written.append(new)
            results.append(seen[BLOCK:])
            state_ref[chain] = half(made["totals"], which)[0:1] * state + wide_dot(
                half(made["key_fallen"], which), new, TN
            )
        written = stack(written)
        written_ref[0, block, pair] = written
        core = (stack(results) + wide_dot(made["scores"], written, NN)).astype(bf16)
        core_ref[0, block, pair] = core
        core = core.astype(jnp.float32)
        normed = core * lax.rsqrt(rows_sum(core * core) / width + eps_norm) * gain_ref[0:1]
        spot = jnp.bitwise_xor(core_bit, block)
        for which in range(PAIR):
            seq, head = divmod(PAIR * pair + which, mine)
            span = slice(head * width, (head + 1) * width)
            out_gate = proj_ref[
                spot, 0, seq, :, 3 * cols + head * width : 3 * cols + (head + 1) * width
            ]
            mixed = half(normed, which) * out_gate * jax.nn.sigmoid(out_gate)
            mixed_ref[spot, 0, seq, :, span] = mixed.astype(bf16)


def mixer_backward_body(
    me_ref,
    proj_ref,
    extra_ref,
    grad_mixed_ref,
    conv_out_ref,
    core_ref,
    inverse_ref,
    made_ref,
    written_ref,
    memory_ref,
    conv_ref,
    gate_ref,
    gain_ref,
    grad_proj_ref,
    grad_extra_ref,
    grad_conv_ref,
    grad_small_ref,
    rows_ref,
    state_ref,
    mask_ref,
    level_ref,
):
    f32 = jnp.float32
    bf16 = jnp.bfloat16
    sequences = proj_ref.shape[2]
    width = gain_ref.shape[1]
    cols = grad_mixed_ref.shape[4]
    mine = cols // width
    pairs = sequences * mine // PAIR
    taps = conv_ref.shape[0]
    core_bit = jnp.bitwise_and(me_ref[0], 1)

    @pl.when(pl.program_id(0) == 0)
    def _():
        rows_ref[...] = jnp.zeros_like(rows_ref)
        state_ref[...] = jnp.zeros_like(state_ref)
        grad_conv_ref[...] = jnp.zeros_like(grad_conv_ref)
        grad_small_ref[...] = jnp.zeros_like(grad_small_ref)
        fill_masks(mask_ref, level_ref)

    within = mask_ref[0]
    gain = gain_ref[0:1]
    grad_gain = jnp.zeros((1, width), f32)
    blocks = []
    for block in (1, 0):
        spot = jnp.bitwise_xor(core_bit, block)
        convolved = [conv_out_ref[0, block, seq] for seq in range(sequences)]
        extras = [extra_ref[spot, 0, seq] for seq in range(sequences)]
        chains = head_pieces(convolved, extras, gate_ref, mine, width)
        for pair in range(pairs):
            made = block_values(chains[PAIR * pair : PAIR * (pair + 1)], mask_ref, width)
            core = core_ref[0, block, pair].astype(f32)
            core_scale = lax.rsqrt(rows_sum(core * core) / width + eps_norm)
            normed = core * core_scale
            grad_unit = []
            for which in range(PAIR):
                seq, head = divmod(PAIR * pair + which, mine)
                span = slice(3 * cols + head * width, 3 * cols + (head + 1) * width)
                out_gate = proj_ref[spot, 0, seq, :, span]
                grad_mixed = grad_mixed_ref[
                    spot, 0, seq, :, head * width : (head + 1) * width
                ].astype(f32)
                sigmoid = jax.nn.sigmoid(out_gate)
                silu = out_gate * sigmoid
                scaled = grad_mixed * half(normed, which)
                grad_gate = scaled * gain * (sigmoid + silu * (1.0 - sigmoid))
                grad_proj_ref[spot, 0, seq, :, span] = grad_gate.astype(bf16)
                grad_gain = grad_gain + jnp.sum(scaled * silu, axis=0, keepdims=True)
                grad_unit.append(grad_mixed * gain * silu)
            grad_unit = stack(grad_unit)
            inner = rows_sum(grad_unit * normed) / width
            made["grad_core"] = (core_scale * (grad_unit - normed * inner)).astype(bf16)
            made["from_scores"] = wide_dot(made["scores"], made["grad_core"], TN)
            made["grad_scores"] = (
                wide_dot(made["grad_core"], written_ref[0, block, pair], NT) * made["fall"]
            )
            blocks.append((block, pair, made))
    grad_small_ref[0:1] += grad_gain

    for block, pair, made in blocks:
        carried = made_ref[0, block, pair, :, width:]
        parts = []
        for which in range(PAIR):
            chain = PAIR * pair + which
            state, grad_state = memory_ref[0, block, chain], state_ref[chain]
            grad_out = half(made["grad_core"], which)
            grad_new = half(made["from_scores"], which) + wide_dot(
                half(made["key_fallen"], which), grad_state, NN
            )
            totals = half(made["totals"], which)[0:1]
            state_ref[chain] = (
                totals * grad_state
                + wide_dot(half(made["query_grown"], which), grad_out, TN)
                - wide_dot(half(carried, which), grad_new, TN)
            )
            parts.append(
                (
                    grad_new,
                    wide_dot(grad_out, state, NT),
                    -wide_dot(grad_new, state, NT),
                    wide_dot(half(written_ref[0, block, pair], which), grad_state, NT),
                    rows_sum(jnp.sum(state * grad_state, axis=0, keepdims=True) * totals),
                )
            )
        made["grad_new"], made["grad_query_grown"], made["grad_carried"] = [
            stack([part[index] for part in parts]) for index in range(3)
        ]
        made["grad_key_fallen"] = stack([part[3] for part in parts])
        made["grad_totals"] = [part[4] for part in parts]

    lane = lax.broadcasted_iota(jnp.int32, (BLOCK, extra_ref.shape[4]), 1)
    at_end = lax.broadcasted_iota(jnp.int32, (BLOCK, 1), 0) == BLOCK - 1
    ones = jnp.ones((PAIR * BLOCK, width), bf16)
    results = {}
    for block, pair, made in blocks:
        beta, growth, fall = made["beta"], made["growth"], made["fall"]
        query, key, value = made["query"], made["key"], made["value"]
        fall_strict = fall - mask_ref[1]
        grad_weighted = wide_dot(
            inverse_ref[0, block, pair],
            jnp.concatenate([made["grad_new"], made["grad_carried"]], axis=1),
            TN,
        )
        grad_lower = -wide_dot(grad_weighted, made_ref[0, block, pair], NT) * fall_strict
        grad_key_key = grad_lower * beta
        from_lower = grad_lower * made["key_key"]
        grad_value_part, grad_key_part = grad_weighted[:, :width], grad_weighted[:, width:]
        grad_scores = made["grad_scores"]
        carried_part = grad_key_part * made["key_grown"]
        grad_beta = rows_sum(from_lower) + rows_sum(carried_part + grad_value_part * value)
        shifts = beta * from_lower + grad_scores * made["query_key"]
        fallen_part = made["grad_key_fallen"] * made["key_fallen"]
        fallen = rows_sum(fallen_part)
        grad_cumulative = rows_sum(shifts) + rows_sum(
            made["grad_query_grown"] * made["query_grown"] + beta * carried_part - fallen_part
        )
        ends = stack(
            [
                jnp.where(
                    at_end,
                    jnp.sum(half(fallen, which), axis=0, keepdims=True) + made["grad_totals"][which],
                    0.0,
                )
                for which in range(PAIR)
            ]
        )
        grad_cumulative = grad_cumulative + ends - wide_dot(shifts, ones, TN)
        grad_decay = rounded(wide_dot(within.astype(bf16), grad_cumulative, TN))
        both = stack([grad_scores, grad_key_key])
        down = wide_dot(both, key.astype(bf16), NN)
        grad_query = growth * made["grad_query_grown"] + down[: PAIR * BLOCK]
        grad_key = (
            made["key_fall"] * made["grad_key_fallen"]
            + beta * growth * grad_key_part
            + down[PAIR * BLOCK :]
            + wide_dot(both, stack([query, key]).astype(bf16), TN)
        )
        grad_query = rounded(grad_query) * width ** (-0.5)
        grad_key = rounded(grad_key)
        grad_value = rounded(beta * grad_value_part)
        grad_beta = rounded(grad_beta)
        unit_query, unit_key = made["unit_query"], made["unit_key"]
        grad_query = made["scale_query"] * (
            grad_query - unit_query * rows_sum(grad_query * unit_query)
        )
        grad_key = made["scale_key"] * (grad_key - unit_key * rows_sum(grad_key * unit_key))
        for which in range(PAIR):
            results[block, PAIR * pair + which] = [
                half(part, which)
                for part in (grad_query, grad_key, grad_value, grad_decay, grad_beta)
            ]

    for block in (1, 0):
        spot = jnp.bitwise_xor(core_bit, block)
        for seq in range(sequences):
            conv_out = conv_out_ref[0, block, seq]
            sigmoid = jax.nn.sigmoid(conv_out)
            chains = [results[block, seq * mine + head] for head in range(mine)]
            grad_active = jnp.concatenate(
                [chain[kind] for kind in range(3) for chain in chains], axis=1
            )
            rows_ref[seq, :BLOCK] = grad_active * sigmoid * (1.0 + conv_out * (1.0 - sigmoid))
            pre = rounded(proj_ref[spot, 0, seq, :, : 3 * cols])
            grad_pre = jnp.zeros_like(conv_out)
            for tap in range(taps):
                shifted = rows_ref[seq, taps - 1 - tap : taps - 1 - tap + BLOCK]
                grad_pre = grad_pre + conv_ref[tap : tap + 1] * shifted
                grad_conv_ref[tap : tap + 1] += jnp.sum(pre * shifted, axis=0, keepdims=True)
            grad_proj_ref[spot, 0, seq, :, : 3 * cols] = grad_pre.astype(bf16)
            rows_ref[seq, BLOCK:] = rows_ref[seq, 0:8]
            extra = extra_ref[spot, 0, seq]
            moved = extra + gate_ref[1:2]
            spread_decay = jnp.zeros_like(extra)
            spread_beta = jnp.zeros_like(extra)
            for head, chain in enumerate(chains):
                spread_decay = jnp.where(lane == head, chain[3][:, 0:1], spread_decay)
                spread_beta = jnp.where(lane == mine + head, chain[4], spread_beta)
            grad_alpha = -gate_ref[0:1] * spread_decay * jax.nn.sigmoid(moved)
            squash = jax.nn.sigmoid(extra)
            grad_extra = grad_alpha + spread_beta * squash * (1.0 - squash)
            grad_extra_ref[spot, 0, seq] = grad_extra.astype(bf16)
            grad_small_ref[1:2] -= jnp.sum(spread_decay * softplus(moved), axis=0, keepdims=True)
            grad_small_ref[2:3] += jnp.sum(grad_alpha, axis=0, keepdims=True)


def ff_pack_body(width, gate_ref, up_ref, out_ref):
    count = out_ref.shape[0]
    blocks = gate_ref.shape[1] // (count * width)
    for spot in range(count):
        pieces = [
            ref[:, (block * count + spot) * width : (block * count + spot + 1) * width]
            for ref in (gate_ref, up_ref)
            for block in range(blocks)
        ]
        out_ref[spot] = jnp.concatenate(pieces, axis=1)


def ff_pack(gate, up, count, width):
    rows, hidden = gate.shape
    return pl.pallas_call(
        functools.partial(ff_pack_body, width),
        out_shape=jax.ShapeDtypeStruct((count, rows, 2 * hidden // count), gate.dtype),
    )(gate, up)


def ff_unpack_body(width, in_ref, gate_ref, up_ref):
    count = in_ref.shape[0]
    blocks = gate_ref.shape[1] // (count * width)
    for which, ref in enumerate((gate_ref, up_ref)):
        pieces = []
        for block in range(blocks):
            first = (which * blocks + block) * width
            pieces += [in_ref[spot, :, first : first + width] for spot in range(count)]
        ref[...] = jnp.concatenate([piece.astype(jnp.float32) for piece in pieces], axis=1)


def ff_unpack(packed, width):
    count, rows, columns = packed.shape
    shape = jax.ShapeDtypeStruct((rows, count * columns // 2), jnp.float32)
    return pl.pallas_call(functools.partial(ff_unpack_body, width), out_shape=[shape, shape])(packed)


def mixer_unpack_body(order, in_ref, *out_refs):
    width = out_refs[0].shape[1] // len(order)
    columns = in_ref.shape[2] // len(out_refs)
    for which, ref in enumerate(out_refs):
        for head, (spot, place) in enumerate(order):
            first = which * columns + place * width
            piece = in_ref[spot, :, first : first + width].astype(jnp.float32)
            ref[:, head * width : (head + 1) * width] = piece


def mixer_unpack(packed, order, head_width):
    shape = jax.ShapeDtypeStruct((packed.shape[1], len(order) * head_width), jnp.float32)
    return pl.pallas_call(functools.partial(mixer_unpack_body, order), out_shape=[shape] * 4)(packed)


def whole_spec(shape):
    return pl.BlockSpec(shape, lambda step, me: (0,) * len(shape))


def mixer_specs(projected, head_width, mine, forward):
    _, steps, sequences, span, _ = projected.shape
    chains = sequences * mine
    pairs = chains // PAIR
    cols = mine * head_width

    def step_of(step):
        return step if forward else steps - 1 - step

    def gathered(channels):
        return pl.BlockSpec(
            (2, 1, sequences, span, channels),
            lambda step, me: (
                0,
                jnp.bitwise_xor(jnp.right_shift(me[0], 1), step_of(step)),
                0,
                0,
                0,
            ),
        )

    def ordered(*shape):
        return pl.BlockSpec((1,) + shape, lambda step, me: (step_of(step),) + (0,) * len(shape))

    size = PAIR * span
    kept = [
        (jax.ShapeDtypeStruct((steps,) + shape, kind), ordered(*shape))
        for shape, kind in [
            ((2, sequences, span, 3 * cols), jnp.float32),
            ((2, pairs, size, head_width), jnp.bfloat16),
            ((2, pairs, size, size), jnp.float32),
            ((2, pairs, size, 2 * head_width), jnp.float32),
            ((2, pairs, size, head_width), jnp.float32),
            ((2, chains, head_width, head_width), jnp.float32),
        ]
    ]
    scratch = [
        pltpu.VMEM((sequences, span + 8, 3 * cols), jnp.float32),
        pltpu.VMEM((chains, head_width, head_width), jnp.float32),
        pltpu.VMEM((2, size, size), jnp.float32),
        pltpu.VMEM((int(BLOCK).bit_length() - 1, size, size), jnp.float32),
    ]
    cost = pl.CostEstimate(
        flops=4 * steps * pairs * size**3 * 18,
        bytes_accessed=12 << 20,
        transcendentals=2 * steps << 18,
    )
    return gathered, kept, scratch, cost


def mixer_forward(me, projected, extra, conv_mine, gate_rows, gain_row, mine):
    channels = projected.shape[-1]
    head_width = gain_row.shape[1]
    gathered, kept, scratch, cost = mixer_specs(projected, head_width, mine, True)
    cols = mine * head_width
    return pl.pallas_call(
        mixer_forward_body,
        grid_spec=pltpu.PrefetchScalarGridSpec(
            num_scalar_prefetch=1,
            grid=(projected.shape[1],),
            in_specs=[
                gathered(channels),
                gathered(extra.shape[-1]),
                whole_spec(conv_mine.shape),
                whole_spec(gate_rows.shape),
                whole_spec(gain_row.shape),
            ],
            out_specs=[gathered(cols)] + [spec for _, spec in kept],
            scratch_shapes=scratch,
        ),
        out_shape=[jax.ShapeDtypeStruct(projected.shape[:-1] + (cols,), jnp.bfloat16)]
        + [shape for shape, _ in kept],
        compiler_params=pltpu.CompilerParams(vmem_limit_bytes=40 << 20),
        cost_estimate=cost,
    )(me, projected, extra, conv_mine, gate_rows, gain_row)


def mixer_backward(
    me, projected, extra, grad_mixed, kept_values, conv_mine, gate_rows, gain_row, mine
):
    channels = projected.shape[-1]
    head_width = gain_row.shape[1]
    gathered, kept, scratch, cost = mixer_specs(projected, head_width, mine, False)
    cols = mine * head_width
    return pl.pallas_call(
        mixer_backward_body,
        grid_spec=pltpu.PrefetchScalarGridSpec(
            num_scalar_prefetch=1,
            grid=(projected.shape[1],),
            in_specs=[gathered(channels), gathered(extra.shape[-1]), gathered(cols)]
            + [spec for _, spec in kept]
            + [
                whole_spec(conv_mine.shape),
                whole_spec(gate_rows.shape),
                whole_spec(gain_row.shape),
            ],
            out_specs=[
                gathered(channels),
                gathered(extra.shape[-1]),
                whole_spec(conv_mine.shape),
                whole_spec((8, head_width)),
            ],
            scratch_shapes=scratch,
        ),
        out_shape=[
            jax.ShapeDtypeStruct(projected.shape, jnp.bfloat16),
            jax.ShapeDtypeStruct(extra.shape, jnp.bfloat16),
            jax.ShapeDtypeStruct(conv_mine.shape, jnp.float32),
            jax.ShapeDtypeStruct((8, head_width), jnp.float32),
        ],
        compiler_params=pltpu.CompilerParams(vmem_limit_bytes=40 << 20),
        cost_estimate=cost,
    )(me, projected, extra, grad_mixed, *kept_values, conv_mine, gate_rows, gain_row)


def after(value, *others):
    return lax.optimization_barrier((value,) + others)[0]


def shift_dp(value, step, sources):
    return lax.ppermute(value, "dp", [(place, place + step) for place in sources])


def line_gather(block, ties):
    count = lax.axis_size("dp")
    me = lax.axis_index("dp")
    ups, downs = [block], [block]
    for step in range(1, count):
        if step <= len(ties):
            ups[-1], downs[-1] = lax.optimization_barrier((ups[-1], downs[-1], ties[step - 1]))[:2]
        ups.append(shift_dp(ups[-1], 1, range(step - 1, count - 1)))
        downs.append(shift_dp(downs[-1], -1, range(1, count - step + 1)))
    result = jnp.zeros((count,) + block.shape, block.dtype)
    for step in range(count):
        piece = block if step == 0 else ups[step] + downs[count - step]
        result = lax.dynamic_update_index_in_dim(result, piece, (me - step) % count, 0)
    return result


def on_device(
    inputs,
    norm_attn,
    w_query,
    w_key,
    w_value,
    conv_weight,
    w_alpha,
    w_beta,
    decay_rate,
    decay_bias,
    w_outgate,
    head_gain,
    w_output,
    norm_mlp,
    w_gate,
    w_up,
    w_down,
    cotangent,
):
    f32 = jnp.float32
    bf16 = jnp.bfloat16
    n_dp = lax.axis_size("dp")
    n_seq = lax.axis_size("seq")
    devices = n_dp * n_seq
    me = lax.axis_index("seq")
    rows, width = w_query.shape
    heads = w_alpha.shape[1]
    head_width = head_gain.shape[0]
    mine = heads // n_seq
    cols = mine * head_width
    group = head_width // rows
    bands = n_seq // group
    band, place = me // group, me % group
    hidden = w_gate.shape[1]
    ff_rows = w_down.shape[0]
    ff = n_dp * ff_rows
    taps = conv_weight.shape[0]
    tokens_shape = inputs.shape
    span = inputs.shape[2]
    count = inputs.shape[0] * inputs.shape[1]
    total = n_seq * count * span

    def by_device(weight):
        split = weight.reshape(weight.shape[0], group, mine, bands, -1)
        return jnp.transpose(split, (3, 1, 0, 2, 4)).reshape(n_seq, weight.shape[0], -1)

    def by_columns(blocks):
        pieces = []
        for head in range(heads):
            spot, from_band = divmod(head, bands)
            from_place, which = divmod(spot, mine)
            block = blocks[from_band * group + from_place]
            pieces.append(block[:, which * head_width : (which + 1) * head_width])
        return jnp.concatenate(pieces, axis=1).astype(f32)

    def swap_all(blocks):
        return lax.all_to_all(blocks, ALL, split_axis=0, concat_axis=0, tiled=True)

    packed = jnp.concatenate([by_device(w) for w in (w_query, w_key, w_value, w_outgate)], axis=2)

    def exchange(blocks):
        return lax.all_to_all(blocks, "seq", split_axis=0, concat_axis=0, tiled=True)

    def gather_dp(block):
        return lax.all_gather(block, "dp", axis=0, tiled=True)

    sent = exchange(packed)
    mixer_full = gather_dp(sent.reshape(n_seq * rows, -1))
    shared = jnp.concatenate(
        [
            w_alpha.T.reshape(-1),
            w_beta.T.reshape(-1),
            norm_attn,
            norm_mlp,
            conv_weight.reshape(-1),
        ]
    )
    shared, w_gate, w_up, sent = lax.optimization_barrier((shared, w_gate, w_up, sent))
    shared = swap_all(jnp.broadcast_to(shared[None], (devices, shared.shape[0])))

    groups = [list(range(first, first + group)) for first in range(0, n_seq, group)]

    def exchange_group(blocks):
        if group == 2:
            away = swap(lax.dynamic_index_in_dim(blocks, 1 - place, 0, keepdims=False), 1)
            stay = lax.dynamic_index_in_dim(blocks, place, 0, keepdims=False)
            low = place == 0
            return jnp.stack([jnp.where(low, stay, away), jnp.where(low, away, stay)], axis=0)
        return lax.all_to_all(
            blocks, "seq", split_axis=0, concat_axis=0, tiled=True, axis_index_groups=groups
        )

    def to_heads(pieces):
        split = exchange_group(pieces.reshape(group, mine * rows, width))
        split = split.reshape(group, mine, rows, width)
        return jnp.transpose(split, (1, 0, 2, 3)).reshape(cols, width)

    def from_heads(full):
        split = jnp.transpose(full.reshape(mine, group, rows, width), (1, 0, 2, 3))
        return exchange_group(split.reshape(group, mine * rows, width))

    output_full = to_heads(gather_dp(w_output))

    gate_up_sent = exchange(ff_pack(w_gate, w_up, n_seq, ff_rows)).reshape(n_seq * rows, -1)
    gate_up_full = gather_dp(gate_up_sent)
    most = ff_rows - min(64, ff_rows // 2)
    down_rest = gather_dp(w_down[most:]).reshape(n_dp, ff_rows - most, width)
    mixer_full, shared, output_full = lax.optimization_barrier((mixer_full, shared, output_full))

    x_own = inputs.reshape(count * span, width)
    x_all = gather_seq(x_own).reshape(total, width)
    seed_own = cotangent.reshape(count * span, width)
    seed_all = gather_seq(seed_own).reshape(total, width)

    gates = shared[:, : 2 * heads * rows].reshape(devices, 2 * heads, rows)
    gates = jnp.transpose(gates, (1, 0, 2)).reshape(2, group, mine, bands, width)
    gates = lax.dynamic_index_in_dim(gates, band, 3, keepdims=False)
    gates = lax.dynamic_index_in_dim(gates, place, 1, keepdims=False).reshape(2 * mine, width)
    gates = jnp.pad(gates, ((0, 128 - 2 * mine), (0, 0)))
    first = 2 * heads * rows
    gain_attn = shared[:, first : first + rows].reshape(-1).astype(f32)
    gain_mlp = shared[:, first + rows : first + 2 * rows].reshape(-1).astype(f32)
    conv_all = shared[:, first + 2 * rows :].reshape(devices, taps, -1)
    conv_all = jnp.transpose(conv_all, (1, 0, 2)).reshape(taps, 3, group, mine, bands, head_width)
    conv_mine = lax.dynamic_index_in_dim(conv_all, band, 4, keepdims=False)
    conv_mine = lax.dynamic_index_in_dim(conv_mine, place, 2, keepdims=False)
    conv_mine = conv_mine.reshape(taps, 3 * cols).astype(f32)

    def my_heads(vector):
        split = lax.dynamic_index_in_dim(vector.reshape(group, mine, bands), band, 2, False)
        return lax.dynamic_index_in_dim(split, place, 0, keepdims=False)

    rate_mine = my_heads(decay_rate)
    bias_mine = my_heads(decay_bias)

    hidden_in = rms_scale(x_all.astype(f32), gain_attn).astype(bf16)
    projected = product(hidden_in, mixer_full)
    extra = times_transposed(hidden_in, gates).reshape(2, n_seq // 2, count, span, -1)

    projected = projected.reshape(2, n_seq // 2, count, span, -1)
    me_row = me.astype(jnp.int32).reshape(1)
    gate_rows = jnp.zeros((2, gates.shape[0]), f32)
    gate_rows = gate_rows.at[0, :mine].set(rate_mine).at[1, :mine].set(bias_mine)
    gain_row = head_gain.reshape(1, head_width)
    mixed, *kept_values = mixer_forward(
        me_row, projected, extra, conv_mine, gate_rows, gain_row, mine
    )
    mixed = mixed.reshape(total, cols)

    def shares(value):
        return value.astype(bf16).reshape(n_seq, count * span, -1)

    residual = x_own.astype(f32) + scatter_seq(shares(product(mixed, output_full)))
    normed_mid, pull_mid = jax.vjp(rms_scale, residual, gain_mlp)
    hidden_mid = gather_seq(normed_mid.astype(bf16)).reshape(total, width)
    down_most = line_gather(w_down[:most], (mixer_full, mixed, hidden_mid))
    gate_up = product(hidden_mid, gate_up_full)
    gate_pre, up_proj = gate_up[:, :ff], gate_up[:, ff:]
    sigmoid_gate = jax.nn.sigmoid(gate_pre)
    silu_gate = gate_pre * sigmoid_gate
    activ = (silu_gate * up_proj).astype(bf16)
    down_grads = contract_rows(activ, seed_all).astype(bf16)
    down_rest = after(down_rest, down_grads)
    down_full = jnp.concatenate([down_most, down_rest], axis=1).reshape(ff, width)
    from_down = times_transposed(seed_all, down_full)
    grad_gate = from_down * up_proj * sigmoid_gate * (1.0 + gate_pre * (1.0 - sigmoid_gate))
    grad_gate_up = jnp.concatenate([grad_gate, from_down * silu_gate], axis=1).astype(bf16)
    back_mid = scatter_seq(shares(times_transposed(grad_gate_up, gate_up_full)))
    grad_res_norm, grad_gain_mlp = pull_mid(back_mid)
    grad_res = seed_own.astype(f32) + grad_res_norm

    def scatter_dp(value):
        return lax.psum_scatter(value.astype(bf16), "dp", scatter_dimension=0, tiled=True)

    grad_down = scatter_dp(down_grads)
    grad_gate_up_own = scatter_dp(contract_rows(hidden_mid, grad_gate_up))

    grad_mixer_out = gather_seq(grad_res.astype(bf16)).reshape(total, width)
    grad_mixed = times_transposed(grad_mixer_out, output_full).astype(bf16)
    grad_projected, grad_extra, grad_conv, grad_small = mixer_backward(
        me_row,
        projected,
        extra,
        grad_mixed.reshape(2, n_seq // 2, count, span, cols),
        kept_values,
        conv_mine,
        gate_rows,
        gain_row,
        mine,
    )
    grad_projected = grad_projected.reshape(total, -1)
    grad_extra = grad_extra.reshape(total, -1)
    grad_head_gain = grad_small[0]
    grad_rate, grad_bias = grad_small[1, :mine], grad_small[2, :mine]
    grad_output = from_heads(contract_rows(mixed, grad_mixer_out).astype(bf16))
    weight_grads = contract_rows(hidden_in, grad_projected).astype(bf16)
    weight_grads, grad_projected, grad_extra, activ = lax.optimization_barrier(
        (weight_grads, grad_projected, grad_extra, activ)
    )
    mixer_own = scatter_dp(weight_grads)
    back_in = times_transposed(grad_projected, mixer_full) + product(grad_extra, gates)
    grad_output, back_in = lax.optimization_barrier((grad_output, back_in))
    grad_output = scatter_dp(grad_output.reshape(n_dp * rows, width))
    back_in = scatter_seq(shares(back_in))
    grad_gate_up_own = exchange(grad_gate_up_own.reshape(n_seq, rows, -1))
    output_own = residual + scatter_seq(shares(product(activ, down_full)))
    grad_w_gate, grad_w_up = ff_unpack(grad_gate_up_own, ff_rows)
    back_in, grad_w_gate, grad_w_up = lax.optimization_barrier((back_in, grad_w_gate, grad_w_up))
    tokens = x_own.astype(f32)
    _, pull_in = jax.vjp(rms_scale, tokens, gain_attn)
    grad_tok_norm, grad_gain_attn = pull_in(back_in)
    input_grad = grad_res + grad_tok_norm

    conv_grad = jnp.zeros((taps, 3, group, mine, bands, head_width), f32)
    conv_grad = lax.dynamic_update_slice(
        conv_grad,
        grad_conv.reshape(taps, 3, 1, mine, 1, head_width),
        (0, 0, place, 0, band, 0),
    )
    conv_grad = jnp.transpose(conv_grad.reshape(taps, devices, -1), (1, 0, 2))
    gate_grad = contract_rows(grad_extra, hidden_in)[: 2 * mine]
    def place_heads(vector):
        slots = jnp.zeros((group, mine, bands), f32)
        return lax.dynamic_update_slice(
            slots, vector.reshape(1, mine, 1), (place, 0, band)
        ).reshape(heads)

    def by_owner(values):
        split = values.reshape(-1, devices, rows)
        return jnp.transpose(split, (1, 0, 2)).reshape(devices, -1)

    common = jnp.concatenate([grad_head_gain, place_heads(grad_rate), place_heads(grad_bias)])
    parts = [
        by_owner(gate_grad),
        by_owner(jnp.stack([grad_gain_attn, grad_gain_mlp])),
        conv_grad.reshape(devices, -1),
        jnp.broadcast_to(common[None], (devices, common.shape[0])),
    ]
    edges = [0]
    for part in parts:
        edges.append(edges[-1] + part.shape[1])
    parts.append(jnp.zeros((devices, -edges[-1] % 128), f32))
    swapped = swap_all(jnp.concatenate(parts, axis=1))
    done = lax.optimization_barrier(
        (grad_w_gate, grad_w_up, grad_down.astype(f32), output_own, input_grad)
    )
    mixer_own, *done = lax.optimization_barrier((mixer_own, *done))
    grad_w_gate, grad_w_up, grad_down, output_own, input_grad = done
    mixer_own = exchange(mixer_own.reshape(n_seq, rows, -1))
    order = []
    for head in range(heads):
        spot, from_band = divmod(head, bands)
        from_place, which = divmod(spot, mine)
        order.append((from_band * group + from_place, which))
    mixer_grads = mixer_unpack(mixer_own, tuple(order), head_width)
    grad_output, *mixer_grads = lax.optimization_barrier((grad_output, *mixer_grads))
    grad_output = grad_output.astype(f32)
    sums = jnp.sum(swapped, axis=0)
    gate_sums = jnp.sum(swapped[:, : edges[1]].reshape(n_dp, n_seq, -1), axis=0)
    gate_sums = gate_sums.reshape(bands, group, 2, mine, rows)
    gate_sums = jnp.transpose(gate_sums, (2, 4, 1, 3, 0)).reshape(2, rows, heads)
    gain_sums = sums[edges[1] : edges[2]].reshape(2, rows)
    common = sums[edges[3] : edges[4]]
    return (
        output_own.astype(bf16).reshape(tokens_shape),
        input_grad.reshape(tokens_shape),
        gain_sums[0],
        *mixer_grads[:3],
        sums[edges[2] : edges[3]].reshape(conv_weight.shape),
        gate_sums[0],
        gate_sums[1],
        common[head_width : head_width + heads],
        common[head_width + heads :],
        mixer_grads[3],
        common[:head_width],
        grad_output,
        gain_sums[1],
        grad_w_gate,
        grad_w_up,
        grad_down,
    )


def solution(mesh):
    in_specs = (
        P(None, "dp", "seq", None),
        P(("dp", "seq")),
        P(("dp", "seq"), None),
        P(("dp", "seq"), None),
        P(("dp", "seq"), None),
        P(None, ("dp", "seq")),
        P(("dp", "seq"), None),
        P(("dp", "seq"), None),
        P(),
        P(),
        P(("dp", "seq"), None),
        P(),
        P(("dp", "seq"), None),
        P(("dp", "seq")),
        P(("dp", "seq"), None),
        P(("dp", "seq"), None),
        P(("dp", "seq"), None),
        P(None, "dp", "seq", None),
    )
    out_specs = (
        P(None, "dp", "seq", None),
        P(None, "dp", "seq", None),
        P(("dp", "seq")),
        P(("dp", "seq"), None),
        P(("dp", "seq"), None),
        P(("dp", "seq"), None),
        P(None, ("dp", "seq")),
        P(("dp", "seq"), None),
        P(("dp", "seq"), None),
        P(),
        P(),
        P(("dp", "seq"), None),
        P(),
        P(("dp", "seq"), None),
        P(("dp", "seq")),
        P(("dp", "seq"), None),
        P(("dp", "seq"), None),
        P(("dp", "seq"), None),
    )
    return jax.shard_map(
        on_device, mesh=mesh, in_specs=in_specs, out_specs=out_specs, check_vma=False
    )
```
